256 devices in a mesh: grp: 8 (over x_lo, y), ep: 32 (over z, x_hi, core).
Axes of the slice: x: 4 (x_hi: 2, x_lo: 2; x = x_hi * 2 + x_lo), y: 4, z: 8, core: 2. Of those that a mesh axis runs over, the one named last changes fastest.
Arguments:
- tokens: bfloat16 [32768, 2048], P(('grp', 'ep')), may hold values from -6 to 6
- routes: int32 [32768, 6], P(('grp', 'ep')), may hold values from 0 to 31, all different within a row; in each aligned block of 128 rows (0 to 127, 128 to 255, ...) at most 32 rows name the same one
- route_gain: float32 [32768, 6], P(('grp', 'ep')), may hold values from 0.05 to 0.6
- gate_weight: bfloat16 [32, 2048, 768], P('ep', 'grp'), may hold values from -0.125 to 0.125
- up_weight: bfloat16 [32, 2048, 768], P('ep', 'grp'), may hold values from -0.125 to 0.125
- down_weight: bfloat16 [32, 768, 2048], P('ep', None, 'grp'), may hold values from -0.21875 to 0.21875
- norm_gain: float32 [2048], replicated, may hold values from 0.25 to 1.75
- query_weight: bfloat16 [2048, 1536], P(None, 'grp'), may hold values from -0.125 to 0.125
Outputs:
- mixed: bfloat16 [32768, 2048], P(('grp', 'ep'))
- query: bfloat16 [32768, 1536], P(('grp', 'ep'))
The draws below stay inside these ranges and needn't reach their ends.
Inputs may be any that keep to these rules, and one draw needn't show every extreme that they name: `routes`: each row names 6 different experts. Among the 128 rows of one device no expert is named by more than 32 rows, a bound that some of them reach.
All inputs are finite; a program needn't handle non-finite values.
Results may differ from the reference program's by a relative error of at most 0.0053.
Values may be sent and summed in bfloat16 or wider, within the bound.
No kernel may reach another device: no remote copies, remote signals or barrier semaphores. Data moves between devices by JAX's collectives and lax.ppermute only.
A program may use at most 128 MiB of HBM per device.

```python
import math
import jax
import jax.numpy as jnp
import numpy as np
from jax import lax

D = 2048
FF_E = 768
QW = 1536
TOP = 6
TOK_DEV = 128
EXPERTS = 32
CAP = 32
TOKENS = 32768
N_GRP = 8
N_EP = 32


def block_levels(rng, shape, shards, smallest, largest):
    factor_of, own = 1.0, jax.random.fold_in(rng, 6)
    for axis_at, shards_of in shards:
        draws = jnp.exp(jax.random.uniform(jax.random.fold_in(own, axis_at), (shards_of,), jnp.float32, smallest / len(shards), largest / len(shards)))
        factor_of = factor_of * jnp.repeat(draws, shape[axis_at] // shards_of).reshape([-1 if axis == axis_at else 1 for axis in range(len(shape))])
    return factor_of


def routed_block(rng, own, number, rows, amount, top, limit, lean):
    ranking = jax.random.permutation(rng, amount)
    packed, ordinary = load_shares(amount, rows * top, limit, lean, True), load_shares(amount, rows * top, limit, lean, False)
    places = jnp.arange(amount)

    def named(tallies, offset_by):
        used = int((tallies > 0).sum())
        fixed = max(1, used // 4)
        passed = fixed + (places - fixed + offset_by * (used - fixed)) % max(1, amount - fixed)
        return jnp.zeros((amount,), jnp.int32).at[ranking[jnp.where(places < fixed, places, passed)]].set(jnp.asarray(tallies, jnp.int32))

    tallies = jnp.where(number % 4 == 0, named(packed, number // 4), named(ordinary, number - number // 4 - 1))
    mixed = jax.random.permutation(jax.random.fold_in(own, 3), amount)
    source_of, sink = mixed[0:amount // 2 * 2:2], mixed[1:amount // 2 * 2:2]
    margin = jnp.minimum(tallies[source_of] - 1, limit - tallies[sink]) // 2
    margin = jnp.where((source_of == ranking[0]) | (sink == ranking[0]) | (tallies[sink] == 0), 0, jnp.maximum(margin, 0))
    passed = jax.random.randint(jax.random.fold_in(own, 4), (amount // 2,), 0, 1 << 20) % (margin + 1)
    tallies = tallies.at[source_of].add(-passed).at[sink].add(passed)
    items = jnp.searchsorted(jnp.cumsum(tallies), jnp.arange(rows * top), side="right").astype(jnp.int32)
    listing = items.reshape(top, rows).T
    listing = listing[jax.random.permutation(jax.random.fold_in(own, 1), rows)]
    offset_by = jax.random.randint(jax.random.fold_in(own, 2), (rows, 1), 0, top)
    return jnp.take_along_axis(listing, (jnp.arange(top)[None, :] + offset_by) % top, axis=1)


def load_shares(number_of, total, most, slope, full):
    loads = [(1 << 20) // math.isqrt(grade ** slope) + 1 for grade in range(1, number_of + 1)]
    largest = most if full else min(most, max(-(-total // number_of), total * loads[0] // sum(loads)))
    least = 1 if total - largest >= number_of - 1 else 0
    counts, spare = [largest] + [least] * (number_of - 1), total - largest - least * (number_of - 1)
    while spare > 0:
        free = [i for i in range(1, number_of) if counts[i] < largest] or [i for i in range(1, number_of) if counts[i] < most]
        mass, budget = sum([loads[i] for i in free]), spare
        for i in free:
            addition = min(most - counts[i], max(1, budget * loads[i] // mass), spare)
            counts[i] = counts[i] + addition
            spare = spare - addition
    return np.array(counts)


def bell_draw(stream_key, dims, scale, reach, split=(), held_as=jnp.bfloat16):
    entries = scale * jax.random.normal(stream_key, dims, jnp.float32)
    if split:
        entries = entries * block_levels(stream_key, dims, split, -0.22, 0.18)
    return jnp.clip(entries, -reach, reach).astype(held_as)


def setup_inputs(seed: int = 0) -> dict:
    key_of = jax.random.split(jax.random.key(seed), 9)
    tokens = bell_draw(key_of[0], (TOKENS, D), 1.0, 6.0, ((0, 256),))
    routes_keys = jax.random.split(jax.random.fold_in(key_of[1], 1), TOKENS // TOK_DEV)
    routes_turns = jax.random.permutation(jax.random.fold_in(key_of[1], 3), TOKENS // TOK_DEV)
    routes = jax.vmap(lambda own, number: routed_block(jax.random.fold_in(key_of[1], 2), own, number, TOK_DEV, EXPERTS, TOP, CAP, 2))(routes_keys, routes_turns).reshape((TOKENS, TOP))
    route_gain = jnp.clip(jnp.exp(math.log(0.6) - 2.4849067 * jax.random.uniform(key_of[2], (TOKENS, TOP), jnp.float32) ** block_levels(key_of[2], (TOKENS, TOP), ((0, 256),), -0.2, 0.2)), 0.05, 0.6)
    gate_weight = bell_draw(key_of[3], (EXPERTS, D, FF_E), D ** -0.5, 0.125, ((0, 32), (1, 8)))
    up_weight = bell_draw(key_of[4], (EXPERTS, D, FF_E), D ** -0.5, 0.125, ((0, 32), (1, 8)))
    down_weight = bell_draw(key_of[5], (EXPERTS, FF_E, D), FF_E ** -0.5, 0.21875, ((0, 32), (2, 8)))
    norm_gain = jnp.clip(1.0 + 0.15 * jax.random.normal(key_of[6], (D,), jnp.float32), 0.25, 1.75)
    query_weight = bell_draw(key_of[7], (D, QW), D ** -0.5, 0.125, ((1, 8),))
    return dict(tokens=tokens, routes=routes, route_gain=route_gain, gate_weight=gate_weight, up_weight=up_weight, down_weight=down_weight, norm_gain=norm_gain, query_weight=query_weight)


def expert_apply(rows, wg, wu, wd):
    gate = jnp.dot(rows, wg, preferred_element_type=jnp.float32)
    up = jnp.dot(rows, wu, preferred_element_type=jnp.float32)
    hidden = (jax.nn.silu(gate) * up).astype(jnp.bfloat16)
    return jnp.dot(hidden, wd, preferred_element_type=jnp.float32).astype(jnp.bfloat16)

def reference(tokens, routes, route_gain, gate_weight, up_weight, down_weight, norm_gain, query_weight):
    flat = routes.reshape(-1)
    weight_flat = route_gain.reshape(-1)
    bucket = N_GRP * N_EP * CAP

    def one_expert(acc, expert):
        chosen = flat == expert
        index = jnp.nonzero(chosen, size=bucket, fill_value=0)[0]
        live = (jnp.arange(bucket) < jnp.sum(chosen)).astype(jnp.float32)
        source = index // TOP
        rows = tokens[source]
        answer = expert_apply(rows, gate_weight[expert], up_weight[expert], down_weight[expert]).astype(jnp.float32)
        acc = acc.at[source].add(answer * (weight_flat[index] * live)[:, None])
        return (acc, None)
    acc, _ = lax.scan(one_expert, jnp.zeros((TOKENS, D), jnp.float32), jnp.arange(EXPERTS))
    total = tokens.astype(jnp.float32) + acc
    square = lax.optimization_barrier(jnp.mean(total * total, axis=-1, keepdims=True))
    normed = (total * lax.rsqrt(square + 1e-06) * norm_gain).astype(jnp.bfloat16)
    query = jnp.dot(normed, query_weight, preferred_element_type=jnp.float32).astype(jnp.bfloat16)
    return (total.astype(jnp.bfloat16), query)
```

```python
import functools

import jax
import jax.numpy as jnp
from jax import lax
from jax.experimental import pallas as pl
from jax.experimental.pallas import tpu as pltpu
from jax.sharding import Mesh, PartitionSpec as P

BF = jnp.bfloat16
F32 = jnp.float32
SLOTS = 32
ANY = pl.BlockSpec(memory_space=pl.ANY)
SMEM = pl.BlockSpec(memory_space=pltpu.SMEM)
VMEM = pl.BlockSpec(memory_space=pltpu.VMEM)
FIRST = (2, 6, 1, 7, 0)
SECOND = (4, 3, 5)


def params(mib):
    return pltpu.CompilerParams(vmem_limit_bytes=mib << 20)


def cost(flops, size):
    return pl.CostEstimate(flops=flops, bytes_accessed=size, transcendentals=0)


def shift(x, axis, by):
    n = lax.axis_size(axis)
    return lax.ppermute(x, axis, [(i, (i + by) % n) for i in range(n)])


def swap(x, axes, k):
    n = lax.axis_size(axes)
    return lax.ppermute(x, axes, [(i, i ^ k) for i in range(n)])


def table_kernel(place, table, code, gain, match):
    z, me = place[0], place[1]
    for s in range(8):
        block = table[lax.rem(z - s + 8, 8)]
        for k in range(4):
            expert = (4 * z + lax.bitwise_xor(me, k)).astype(F32)
            hit = block[0:6] == expert
            row = slice(4 * s + k, 4 * s + k + 1)
            match[row] = jnp.sum(jnp.where(hit, 1.0, 0.0), axis=0, keepdims=True)
            gain[row] = jnp.sum(jnp.where(hit, block[6:12], 0.0), axis=0, keepdims=True)
    chosen = match[...]
    before = lax.broadcasted_iota(jnp.int32, (128, 128), 0) < lax.broadcasted_iota(jnp.int32, (128, 128), 1)
    rank = jnp.dot(chosen.astype(BF), jnp.where(before, 1.0, 0.0).astype(BF), preferred_element_type=F32)
    code[...] = jnp.where(chosen > 0.5, rank, -1.0)


def make_table(place, table):
    return pl.pallas_call(
        table_kernel,
        out_shape=(jax.ShapeDtypeStruct((32, 128), F32),) * 2,
        in_specs=[SMEM, VMEM],
        out_specs=(VMEM, VMEM),
        scratch_shapes=[pltpu.VMEM((32, 128), F32)],
        cost_estimate=cost(1 << 20, 1 << 17),
    )(place, table)


def chosen_rows(code, s):
    slot = lax.broadcasted_iota(jnp.int32, (SLOTS, 128), 0).astype(F32)
    return [code[4 * s + k : 4 * s + k + 1, :] == slot for k in range(4)]


def select_kernel(blocks, *refs):
    code, refs = refs[0], list(refs[1:])
    outs = refs[-5:-1]
    joined = refs[-1]
    at = 0
    for b, s in enumerate(blocks):
        if s == 4:
            joined[0:64] = refs[at][...]
            joined[64:128] = refs[at + 1][...]
            source, at = joined[...], at + 2
        else:
            source, at = refs[at][...], at + 1
        onehot = jnp.concatenate([jnp.where(hit, 1.0, 0.0).astype(BF) for hit in chosen_rows(code, s)], axis=0)
        rows = jnp.dot(onehot, source, preferred_element_type=F32).astype(BF)
        for k in range(4):
            outs[k][b * SLOTS : (b + 1) * SLOTS] = rows[k * SLOTS : (k + 1) * SLOTS]


def select(blocks, code, sources):
    width, step = sources[0].shape[1], 512
    rows = len(blocks) * SLOTS
    return pl.pallas_call(
        functools.partial(select_kernel, blocks),
        out_shape=(jax.ShapeDtypeStruct((rows, width), BF),) * 4,
        grid=(width // step,),
        in_specs=[pl.BlockSpec((32, 128), lambda j: (0, 0))]
        + [pl.BlockSpec((x.shape[0], step), lambda j: (0, j)) for x in sources],
        out_specs=(pl.BlockSpec((rows, step), lambda j: (0, j)),) * 4,
        scratch_shapes=[pltpu.VMEM((128, step), BF)],
        compiler_params=params(32),
        cost_estimate=cost(len(blocks) << 26, len(blocks) << 20),
    )(code, *sources)


def hidden_kernel(n_rows, offsets, *refs):
    pieces, weights, out = refs[:4], refs[4:14], refs[14]
    x, gate, up, sems = refs[15:]
    half = 256
    copies = []

    def copy(src, dst):
        c = pltpu.make_async_copy(src, dst, sems.at[len(copies)])
        c.start()
        copies.append(c)

    for ring in range(2):
        whole = weights[5 * ring : 5 * ring + 3]
        for i in range(3):
            off = pl.multiple_of(offsets[4 * ring + i], half)
            copy(whole[i].at[0:half], gate.at[pl.ds(off, half)])
            copy(whole[i].at[half : 2 * half], up.at[pl.ds(off, half)])
        off = pl.multiple_of(offsets[4 * ring + 3], half)
        copy(weights[5 * ring + 3], gate.at[pl.ds(off, half)])
        copy(weights[5 * ring + 4], up.at[pl.ds(off, half)])
    for k in range(4):
        copy(pieces[k], x.at[k * n_rows : (k + 1) * n_rows])
    for c in copies:
        c.wait()

    @pl.loop(0, gate.shape[1] // 256)
    def _(j):
        cols = pl.ds(pl.multiple_of(j * 256, 256), 256)
        g = jnp.dot(x[...], gate[:, cols], preferred_element_type=F32)
        u = jnp.dot(x[...], up[:, cols], preferred_element_type=F32)
        out[:, cols] = (g / (1.0 + jnp.exp(-g)) * u).astype(BF)


def hidden_of(offsets, pieces, weights):
    n_rows, width = pieces[0].shape
    units = weights[0].shape[1]
    return pl.pallas_call(
        functools.partial(hidden_kernel, n_rows),
        out_shape=jax.ShapeDtypeStruct((4 * n_rows, units), BF),
        in_specs=[SMEM] + [ANY] * (len(pieces) + len(weights)),
        out_specs=VMEM,
        scratch_shapes=[
            pltpu.VMEM((4 * n_rows, width), BF),
            pltpu.VMEM((width, units), BF),
            pltpu.VMEM((width, units), BF),
            pltpu.SemaphoreType.DMA((20,)),
        ],
        compiler_params=params(40),
        cost_estimate=cost(16 * n_rows * width * units, 8 << 20),
    )(offsets, *pieces, *weights)


def answer_kernel(sizes, offsets, *refs):
    hidden, weights = refs[0], refs[1:11]
    outs, (down, sems) = refs[11:-2], refs[-2:]
    copies = []

    def copy(src, dst):
        c = pltpu.make_async_copy(src, dst, sems.at[len(copies)])
        c.start()
        copies.append(c)

    half = down.shape[0] // 2
    for ring in range(2):
        for i in range(3):
            cols = pl.ds(pl.multiple_of(offsets[4 * ring + i], 256), 256)
            copy(weights[5 * ring + i], down.at[:, cols])
        cols = pl.ds(pl.multiple_of(offsets[4 * ring + 3], 256), 256)
        copy(weights[5 * ring + 3], down.at[0:half, cols])
        copy(weights[5 * ring + 4], down.at[half : 2 * half, cols])
    for c in copies:
        c.wait()
    total = sum(sizes)

    @pl.loop(0, down.shape[1] // 256)
    def _(j):
        cols = pl.ds(pl.multiple_of(j * 256, 256), 256)
        answer = jnp.dot(hidden[...], down[:, cols], preferred_element_type=F32).astype(BF)
        for k in range(4):
            at = k * total
            for i, size in enumerate(sizes):
                outs[4 * i + k][:, cols] = answer[at : at + size]
                at += size


def answers_of(sizes, offsets, hidden, weights):
    width = 8 * weights[0].shape[1]
    units = hidden.shape[1]
    shapes = [jax.ShapeDtypeStruct((size, width), BF) for size in sizes for _ in range(4)]
    out = pl.pallas_call(
        functools.partial(answer_kernel, sizes),
        out_shape=tuple(shapes),
        in_specs=[SMEM, VMEM] + [ANY] * len(weights),
        out_specs=(VMEM,) * len(shapes),
        scratch_shapes=[pltpu.VMEM((units, width), BF), pltpu.SemaphoreType.DMA((10,))],
        compiler_params=params(40),
        cost_estimate=cost(2 * hidden.shape[0] * width * units, 8 << 20),
    )(offsets, hidden, *weights)
    return [out[4 * i : 4 * i + 4] for i in range(len(sizes))]


def combined(code, gain, s, answers):
    weight = jnp.concatenate(
        [jnp.where(hit, gain[4 * s + k : 4 * s + k + 1, :], 0.0) for k, hit in enumerate(chosen_rows(code, s))], axis=0
    )
    high = weight.astype(BF)
    low = (weight - high.astype(F32)).astype(BF)
    rows = jnp.concatenate(answers, axis=0)
    dims = (((0,), (0,)), ((), ()))
    return lax.dot_general(high, rows, dims, preferred_element_type=F32) + lax.dot_general(
        low, rows, dims, preferred_element_type=F32
    )


def combine_kernel(blocks, start, n_in, code, gain, *refs):
    answers, arrived, outs = refs[:4], refs[4 : 4 + n_in], refs[4 + n_in :]
    for i, s in enumerate(blocks):
        rows = slice(start + i * SLOTS, start + (i + 1) * SLOTS)
        total = combined(code, gain, s, [a[rows] for a in answers])
        if s == 4:
            outs[0][...] = total[0:64].astype(BF)
            outs[1][...] = total[64:128].astype(BF)
        elif s == 3:
            outs[i][0:64] = (total[0:64] + arrived[i][...].astype(F32)).astype(BF)
            outs[i][64:128] = total[64:128].astype(BF)
        elif s == 5:
            outs[i][0:64] = total[0:64].astype(BF)
            outs[i][64:128] = (total[64:128] + arrived[i][...].astype(F32)).astype(BF)
        else:
            outs[i][...] = (total + arrived[i][...].astype(F32)).astype(BF)


def combine(blocks, start, code, gain, answers, arrived):
    width, step = answers[0].shape[1], 512
    height = 64 if blocks == (4,) else 128
    whole = pl.BlockSpec((32, 128), lambda j: (0, 0))
    return pl.pallas_call(
        functools.partial(combine_kernel, blocks, start, len(arrived)),
        out_shape=(jax.ShapeDtypeStruct((height, width), BF),) * 2,
        grid=(width // step,),
        in_specs=[whole, whole]
        + [pl.BlockSpec((x.shape[0], step), lambda j: (0, j)) for x in (*answers, *arrived)],
        out_specs=(pl.BlockSpec((height, step), lambda j: (0, j)),) * 2,
        compiler_params=params(32),
        cost_estimate=cost(len(blocks) << 27, 2 << 20),
    )(code, gain, *answers, *arrived)


def final_kernel(start, offsets, code, gain, a0, a1, a2, a3, tokens, left, right, norm, q0, q1, mixed, query, total, normed, held, sems):
    copies = [pltpu.make_async_copy(q, held.at[i], sems.at[i]) for i, q in enumerate((q0, q1))]
    for c in copies:
        c.start()
    width, step = tokens.shape[1], 512
    square = jnp.zeros((128, 1), F32)
    for j in range(width // step):
        cols = slice(j * step, (j + 1) * step)
        part = combined(code, gain, 0, [a[start : start + SLOTS, cols] for a in (a0, a1, a2, a3)])
        part = part + tokens[:, cols].astype(F32)
        part = part + left[:, cols].astype(F32) + right[:, cols].astype(F32)
        mixed[:, cols] = part.astype(BF)
        total[:, cols] = part
        square = square + jnp.sum(part * part, axis=1, keepdims=True)
    scale = lax.rsqrt(square / width + 1e-06)
    for j in range(width // step):
        cols = slice(j * step, (j + 1) * step)
        normed[:, cols] = (total[:, cols] * scale * norm[:, cols]).astype(BF)
    for c in copies:
        c.wait()
    half = width // 2
    sides = [normed[:, pl.ds(pl.multiple_of(offsets[i], half), half)] for i in range(2)]
    dims = (((1,), (1,)), ((), ()))
    tile = 256
    for j in range(query.shape[1] // tile):
        cols = slice(j * tile, (j + 1) * tile)
        out = lax.dot_general(sides[0], held[0, cols], dims, preferred_element_type=F32)
        out = out + lax.dot_general(sides[1], held[1, cols], dims, preferred_element_type=F32)
        query[:, cols] = out.astype(BF)


def final(start, offsets, code, gain, answers, tokens, left, right, norm, q0, q1):
    rows, width = tokens.shape
    features = q0.shape[0]
    return pl.pallas_call(
        functools.partial(final_kernel, start),
        out_shape=(jax.ShapeDtypeStruct((rows, width), BF), jax.ShapeDtypeStruct((rows, features), BF)),
        in_specs=[SMEM] + [VMEM] * 10 + [ANY] * 2,
        out_specs=(VMEM, VMEM),
        scratch_shapes=[
            pltpu.VMEM((rows, width), F32),
            pltpu.VMEM((rows, width), BF),
            pltpu.VMEM((2, features, width // 2), BF),
            pltpu.SemaphoreType.DMA((2,)),
        ],
        compiler_params=params(40),
        cost_estimate=cost(2 * rows * width * features, 8 << 20),
    )(offsets, code, gain, *answers, tokens, left, right, norm, q0, q1)


def ring_of_four(x, half):
    up, down = shift(x, "y", 1), shift(x, "y", -1)
    return [x, up, down, shift(up[:half], "y", 1), shift(down[half:], "y", -1)]


def shards(tokens, routes, route_gain, gate_weight, up_weight, down_weight, norm_gain, query_weight):
    xl, y, z, c = (lax.axis_index(a) for a in ("xl", "y", "z", "c"))
    me = 2 * lax.axis_index("xh") + c
    plane = ("xh", "c")
    around = [xl * 4 + lax.rem(y + d, 4) for d in (0, 3, 1, 2)]
    across = [(1 - xl) * 4 + lax.rem(y + d, 4) for d in (0, 3, 1, 2)]
    offsets = (256 * jnp.stack(around + across)).astype(jnp.int32)
    place = jnp.stack([z, me]).astype(jnp.int32)

    table = lax.all_gather(jnp.concatenate([routes.T.astype(F32), route_gain.T], axis=0), "z")
    code, gain = make_table(place, table)

    up1, down1 = shift(tokens, "z", 1), shift(tokens, "z", -1)
    gate_up = jnp.concatenate([gate_weight[0], up_weight[0]], axis=0)
    other = swap(gate_up, "xl", 1)
    wide = ring_of_four(gate_up, 256) + ring_of_four(other, 256)
    up2, down2 = shift(up1, "z", 1), shift(down1, "z", -1)
    tall = down_weight[0]
    narrow = ring_of_four(tall, 384) + ring_of_four(swap(tall, "xl", 1), 384)

    sent = select(FIRST, code, [up2, down2, up1, down1, tokens])
    rows_a = [sent[0]] + [swap(sent[k], plane, k) for k in (1, 2, 3)]
    up3, down3 = shift(up2, "z", 1), shift(down2, "z", -1)
    up4, down4 = shift(up3[:64], "z", 1), shift(down3[64:], "z", -1)
    sent = select(SECOND, code, [up4, down4, up3, down3])
    rows_b = [sent[0]] + [swap(sent[k], plane, k) for k in (1, 2, 3)]

    hidden_a = hidden_of(offsets, rows_a, wide)
    hidden_b = hidden_of(offsets, rows_b, wide)
    ans4, ans3 = answers_of((32, 64), offsets, hidden_b, narrow)
    ans2, ans1 = answers_of((64, 96), offsets, hidden_a, narrow)

    half = query_weight.shape[0] // 2
    share = lax.dynamic_slice(query_weight.T, (0, c * half), (query_weight.shape[1], half))
    share, _ = lax.optimization_barrier((share, wide[8]))
    q_own = lax.all_gather(share, ("xl", "y"), axis=0, tiled=True)
    q_other = swap(q_own, "c", 1)
    sides = (half * jnp.stack([c, 1 - c])).astype(jnp.int32)

    def back(pieces):
        return [pieces[0]] + [swap(pieces[k], plane, k) for k in (1, 2, 3)]

    ans4, ans3, ans2, ans1 = back(ans4), back(ans3), back(ans2), back(ans1)
    low, high = combine((4,), 0, code, gain, ans4, [])
    low, high = shift(low, "z", -1), shift(high, "z", 1)
    low, high = combine((3, 5), 0, code, gain, ans3, [low, high])
    low, high = shift(low, "z", -1), shift(high, "z", 1)
    low, high = combine((2, 6), 0, code, gain, ans2, [low, high])
    low, high = shift(low, "z", -1), shift(high, "z", 1)
    low, high = combine((1, 7), 0, code, gain, ans1, [low, high])
    low, high = shift(low, "z", -1), shift(high, "z", 1)
    return final(64, sides, code, gain, ans1, tokens, low, high, norm_gain[None, :], q_own, q_other)


def solution(mesh):
    fine = Mesh(mesh.devices.reshape(2, 4, 8, 2, 2), ("xl", "y", "z", "xh", "c"))
    grp, ep = ("xl", "y"), ("z", "xh", "c")
    placed = (
        P(grp + ep, None),
        P(grp + ep, None),
        P(grp + ep, None),
        P(ep, grp, None),
        P(ep, grp, None),
        P(ep, None, grp),
        P(),
        P(None, grp),
    )
    return jax.shard_map(
        shards,
        mesh=fine,
        in_specs=placed,
        out_specs=(P(grp + ep, None), P(grp + ep, None)),
        check_vma=False,
    )
```

```python
import functools

import jax
import jax.numpy as jnp
from jax import lax
from jax.experimental import pallas as pl
from jax.experimental.pallas import tpu as pltpu
from jax.sharding import Mesh, PartitionSpec as P

BF = jnp.bfloat16
F32 = jnp.float32
SLOTS = 32
ANY = pl.BlockSpec(memory_space=pltpu.HBM)
SMEM = pl.BlockSpec(memory_space=pltpu.SMEM)
VMEM = pl.BlockSpec(memory_space=pltpu.VMEM)
FIRST = (2, 6, 1, 7, 0)
SECOND = (4, 3, 5)


def params(mib):
    return pltpu.CompilerParams(vmem_limit_bytes=mib << 20)


def cost(flops, size):
    return pl.CostEstimate(flops=flops, bytes_accessed=size, transcendentals=0)


def shift(x, axis, by):
    n = lax.axis_size(axis)
    return lax.ppermute(x, axis, [(i, (i + by) % n) for i in range(n)])


def swap(x, axes, k):
    n = lax.axis_size(axes)
    return lax.ppermute(x, axes, [(i, i ^ k) for i in range(n)])


def prepare_kernel(tokens, routes, gain, gate, up, down, block, weights, extra, sems):
    copies = []

    def copy(src, dst):
        c = pltpu.make_async_copy(src, dst, sems.at[len(copies)])
        c.start()
        copies.append(c)

    rows = tokens.shape[0]
    copy(tokens, block.at[0:rows])
    for j in range(3):
        copy(gate.at[:, 256 * j : 256 * (j + 1)], weights.at[256 * j : 256 * (j + 1)])
        copy(up.at[:, 256 * j : 256 * (j + 1)], weights.at[768 + 256 * j : 768 + 256 * (j + 1)])
    copy(down, weights.at[1536:2304])
    extra[...] = jnp.zeros_like(extra)
    g = gain[...]
    high = g.astype(BF)
    rest = g - high.astype(F32)
    middle = rest.astype(BF)
    low = (rest - middle.astype(F32)).astype(BF)
    for i, part in enumerate((routes[...].astype(F32).astype(BF), high, middle, low)):
        extra[0:6, 128 * i : 128 * (i + 1)] = part
    copy(extra, block.at[rows : rows + 16])
    for c in copies:
        c.wait()


def prepare(tokens, routes, gain, gate, up, down):
    rows, width = tokens.shape
    return pl.pallas_call(
        prepare_kernel,
        out_shape=(jax.ShapeDtypeStruct((rows + 16, width), BF), jax.ShapeDtypeStruct((2304, 256), BF)),
        in_specs=[ANY, VMEM, VMEM, ANY, ANY, ANY],
        out_specs=(ANY, ANY),
        scratch_shapes=[pltpu.VMEM((16, width), BF), pltpu.SemaphoreType.DMA((9,))],
        compiler_params=params(62),
        cost_estimate=cost(1 << 16, 4 << 20),
    )(tokens, routes, gain, gate, up, down)


def chosen_rows(code, i):
    slot = lax.broadcasted_iota(jnp.int32, (SLOTS, 128), 0).astype(F32)
    return [code[4 * i + k : 4 * i + k + 1, :] == slot for k in range(4)]


def select_kernel(blocks, n_in, place, *refs):
    sources, extras, refs = refs[:n_in], refs[n_in : n_in + len(blocks)], refs[n_in + len(blocks) :]
    outs, (code, gain, match, joined) = refs[:4], refs[4:]

    @pl.when(pl.program_id(0) == 0)
    def _():
        z, me = place[0], place[1]
        for i, extra in enumerate(extras):
            block = extra[...].astype(F32)
            routes = block[0:6, 0:128]
            gains = block[0:6, 128:256] + block[0:6, 256:384] + block[0:6, 384:512]
            for k in range(4):
                expert = (4 * z + lax.bitwise_xor(me, k)).astype(F32)
                hit = routes == expert
                row = slice(4 * i + k, 4 * i + k + 1)
                match[row] = jnp.sum(jnp.where(hit, 1.0, 0.0), axis=0, keepdims=True)
                gain[row] = jnp.sum(jnp.where(hit, gains, 0.0), axis=0, keepdims=True)
        chosen = match[...]
        before = lax.broadcasted_iota(jnp.int32, (128, 128), 0) < lax.broadcasted_iota(jnp.int32, (128, 128), 1)
        rank = jnp.dot(chosen.astype(BF), jnp.where(before, 1.0, 0.0).astype(BF), preferred_element_type=F32)
        code[...] = jnp.where(chosen > 0.5, rank, -1.0)

    at = 0
    for i, s in enumerate(blocks):
        if s == 4:
            joined[0:64] = sources[at][0:64]
            joined[64:128] = sources[at + 1][0:64]
            source, at = joined[...], at + 2
        else:
            source, at = sources[at][0:128], at + 1
        onehot = jnp.concatenate([jnp.where(hit, 1.0, 0.0).astype(BF) for hit in chosen_rows(code, i)], axis=0)
        rows = jnp.dot(onehot, source, preferred_element_type=F32).astype(BF)
        for k in range(4):
            outs[k][i * SLOTS : (i + 1) * SLOTS] = rows[k * SLOTS : (k + 1) * SLOTS]


def select(blocks, place, sources):
    width, step = sources[0].shape[1], 512
    n, rows = len(blocks), len(blocks) * SLOTS
    holders = [x for x in sources if x.shape[0] > 64]
    below = [pl.BlockSpec((16, step), functools.partial(lambda i, j: (i, 0), x.shape[0] // 16 - 1)) for x in holders]
    out = pl.pallas_call(
        functools.partial(select_kernel, blocks, len(sources)),
        out_shape=(jax.ShapeDtypeStruct((rows, width), BF),) * 4 + (jax.ShapeDtypeStruct((4 * n, 128), F32),) * 2,
        grid=(width // step,),
        in_specs=[SMEM] + [pl.BlockSpec((x.shape[0], step), lambda j: (0, j)) for x in sources] + below,
        out_specs=(pl.BlockSpec((rows, step), lambda j: (0, j)),) * 4 + (pl.BlockSpec((4 * n, 128), lambda j: (0, 0)),) * 2,
        scratch_shapes=[pltpu.VMEM((4 * n, 128), F32), pltpu.VMEM((128, step), BF)],
        compiler_params=params(62),
        cost_estimate=cost(n << 26, n << 20),
    )(place, *sources, *holders)
    return out[:4], out[4], out[5]


def hidden_kernel(n_rows, offsets, *refs):
    pieces, weights, out = refs[:4], refs[4:14], refs[14]
    x, gate, up, sems = refs[15:]
    copies = []

    def copy(src, dst):
        c = pltpu.make_async_copy(src, dst, sems.at[len(copies)])
        c.start()
        copies.append(c)

    for ring in range(2):
        whole, far = weights[5 * ring : 5 * ring + 3], weights[5 * ring + 3 : 5 * ring + 5]
        for i in range(4):
            rows = pl.ds(pl.multiple_of(offsets[4 * ring + i], 256), 256)
            for j in range(3):
                cols = slice(256 * j, 256 * (j + 1))
                if i < 3:
                    copy(whole[i].at[cols], gate.at[rows, cols])
                    copy(whole[i].at[768 + 256 * j : 768 + 256 * (j + 1)], up.at[rows, cols])
                else:
                    copy(far[0].at[cols], gate.at[rows, cols])
                    copy(far[1].at[cols], up.at[rows, cols])
    for k in range(4):
        copy(pieces[k], x.at[k * n_rows : (k + 1) * n_rows])
    for c in copies:
        c.wait()

    @pl.loop(0, gate.shape[1] // 256)
    def _(j):
        cols = pl.ds(pl.multiple_of(j * 256, 256), 256)
        g = jnp.dot(x[...], gate[:, cols], preferred_element_type=F32)
        u = jnp.dot(x[...], up[:, cols], preferred_element_type=F32)
        out[:, cols] = (g / (1.0 + jnp.exp(-g)) * u).astype(BF)


def hidden_of(offsets, pieces, weights):
    n_rows, width = pieces[0].shape
    units = 768
    return pl.pallas_call(
        functools.partial(hidden_kernel, n_rows),
        out_shape=jax.ShapeDtypeStruct((4 * n_rows, units), BF),
        in_specs=[SMEM] + [ANY] * (len(pieces) + len(weights)),
        out_specs=VMEM,
        scratch_shapes=[
            pltpu.VMEM((4 * n_rows, width), BF),
            pltpu.VMEM((width, units), BF),
            pltpu.VMEM((width, units), BF),
            pltpu.SemaphoreType.DMA((52,)),
        ],
        compiler_params=params(62),
        cost_estimate=cost(16 * n_rows * width * units, 8 << 20),
    )(offsets, *pieces, *weights)


def answer_kernel(sizes, offsets, *refs):
    hidden, weights = refs[0], refs[1:11]
    outs, (down, sems) = refs[11:-2], refs[-2:]
    copies = []

    def copy(src, dst):
        c = pltpu.make_async_copy(src, dst, sems.at[len(copies)])
        c.start()
        copies.append(c)

    half = down.shape[0] // 2
    for ring in range(2):
        for i in range(3):
            cols = pl.ds(pl.multiple_of(offsets[4 * ring + i], 256), 256)
            copy(weights[5 * ring + i].at[1536:2304], down.at[:, cols])
        cols = pl.ds(pl.multiple_of(offsets[4 * ring + 3], 256), 256)
        copy(weights[5 * ring + 3], down.at[0:half, cols])
        copy(weights[5 * ring + 4], down.at[half : 2 * half, cols])
    for c in copies:
        c.wait()
    total = sum(sizes)

    @pl.loop(0, down.shape[1] // 256)
    def _(j):
        cols = pl.ds(pl.multiple_of(j * 256, 256), 256)
        answer = jnp.dot(hidden[...], down[:, cols], preferred_element_type=F32).astype(BF)
        for k in range(4):
            at = k * total
            for i, size in enumerate(sizes):
                outs[4 * i + k][:, cols] = answer[at : at + size]
                at += size


def answers_of(sizes, offsets, hidden, weights):
    width = 8 * weights[0].shape[1]
    units = hidden.shape[1]
    shapes = [jax.ShapeDtypeStruct((size, width), BF) for size in sizes for _ in range(4)]
    out = pl.pallas_call(
        functools.partial(answer_kernel, sizes),
        out_shape=tuple(shapes),
        in_specs=[SMEM, VMEM] + [ANY] * len(weights),
        out_specs=(VMEM,) * len(shapes),
        scratch_shapes=[pltpu.VMEM((units, width), BF), pltpu.SemaphoreType.DMA((10,))],
        compiler_params=params(62),
        cost_estimate=cost(2 * hidden.shape[0] * width * units, 8 << 20),
    )(offsets, hidden, *weights)
    return [out[4 * i : 4 * i + 4] for i in range(len(sizes))]


def combined(code, gain, i, answers):
    weight = jnp.concatenate(
        [jnp.where(hit, gain[4 * i + k : 4 * i + k + 1, :], 0.0) for k, hit in enumerate(chosen_rows(code, i))], axis=0
    )
    high = weight.astype(BF)
    low = (weight - high.astype(F32)).astype(BF)
    rows = jnp.concatenate(answers, axis=0)
    dims = (((0,), (0,)), ((), ()))
    return lax.dot_general(high, rows, dims, preferred_element_type=F32) + lax.dot_general(
        low, rows, dims, preferred_element_type=F32
    )


def combine_kernel(blocks, first, start, n_in, code, gain, *refs):
    answers, arrived, outs = refs[:4], refs[4 : 4 + n_in], refs[4 + n_in :]
    for i, s in enumerate(blocks):
        rows = slice(start + i * SLOTS, start + (i + 1) * SLOTS)
        total = combined(code, gain, first + i, [a[rows] for a in answers])
        if s == 4:
            outs[0][...] = total[0:64].astype(BF)
            outs[1][...] = total[64:128].astype(BF)
        elif s == 3:
            outs[i][0:64] = (total[0:64] + arrived[i][...].astype(F32)).astype(BF)
            outs[i][64:128] = total[64:128].astype(BF)
        elif s == 5:
            outs[i][0:64] = total[0:64].astype(BF)
            outs[i][64:128] = (total[64:128] + arrived[i][...].astype(F32)).astype(BF)
        else:
            outs[i][...] = (total + arrived[i][...].astype(F32)).astype(BF)


def combine(blocks, first, start, code, gain, answers, arrived):
    width, step = answers[0].shape[1], 512
    height = 64 if blocks == (4,) else 128
    whole = pl.BlockSpec(code.shape, lambda j: (0, 0))
    return pl.pallas_call(
        functools.partial(combine_kernel, blocks, first, start, len(arrived)),
        out_shape=(jax.ShapeDtypeStruct((height, width), BF),) * 2,
        grid=(width // step,),
        in_specs=[whole, whole]
        + [pl.BlockSpec((x.shape[0], step), lambda j: (0, j)) for x in (*answers, *arrived)],
        out_specs=(pl.BlockSpec((height, step), lambda j: (0, j)),) * 2,
        compiler_params=params(62),
        cost_estimate=cost(len(blocks) << 27, 2 << 20),
    )(code, gain, *answers, *arrived)


def final_kernel(start, offsets, code, gain, a0, a1, a2, a3, tokens, left, right, norm, q0, q1, mixed, query, total, normed, held, sems):
    copies = [pltpu.make_async_copy(q, held.at[i], sems.at[i]) for i, q in enumerate((q0, q1))]
    for c in copies:
        c.start()
    width, step = tokens.shape[1], 512
    square = jnp.zeros((128, 1), F32)
    for j in range(width // step):
        cols = slice(j * step, (j + 1) * step)
        part = combined(code, gain, 4, [a[start : start + SLOTS, cols] for a in (a0, a1, a2, a3)])
        part = part + tokens[:, cols].astype(F32)
        part = part + left[:, cols].astype(F32) + right[:, cols].astype(F32)
        mixed[:, cols] = part.astype(BF)
        total[:, cols] = part
        square = square + jnp.sum(part * part, axis=1, keepdims=True)
    scale = lax.rsqrt(square / width + 1e-06)
    for j in range(width // step):
        cols = slice(j * step, (j + 1) * step)
        normed[:, cols] = (total[:, cols] * scale * norm[:, cols]).astype(BF)
    for c in copies:
        c.wait()
    half = width // 2
    sides = [normed[:, pl.ds(pl.multiple_of(offsets[i], half), half)] for i in range(2)]
    dims = (((1,), (1,)), ((), ()))

    @pl.loop(0, query.shape[1] // 256)
    def _(j):
        cols = pl.ds(pl.multiple_of(j * 256, 256), 256)
        out = lax.dot_general(sides[0], held[0, cols], dims, preferred_element_type=F32)
        out = out + lax.dot_general(sides[1], held[1, cols], dims, preferred_element_type=F32)
        query[:, cols] = out.astype(BF)


def final(start, offsets, code, gain, answers, tokens, left, right, norm, q0, q1):
    rows, width = tokens.shape
    features = q0.shape[0]
    return pl.pallas_call(
        functools.partial(final_kernel, start),
        out_shape=(jax.ShapeDtypeStruct((rows, width), BF), jax.ShapeDtypeStruct((rows, features), BF)),
        in_specs=[SMEM] + [VMEM] * 10 + [ANY] * 2,
        out_specs=(VMEM, VMEM),
        scratch_shapes=[
            pltpu.VMEM((rows, width), F32),
            pltpu.VMEM((rows, width), BF),
            pltpu.VMEM((2, features, width // 2), BF),
            pltpu.SemaphoreType.DMA((2,)),
        ],
        compiler_params=params(62),
        cost_estimate=cost(2 * rows * width * features, 8 << 20),
    )(offsets, code, gain, *answers, tokens, left, right, norm, q0, q1)


def shards(tokens, routes, route_gain, gate_weight, up_weight, down_weight, norm_gain, query_weight):
    xl, y, z, c = (lax.axis_index(a) for a in ("xl", "y", "z", "c"))
    me = 2 * lax.axis_index("xh") + c
    plane = ("xh", "c")
    around = [xl * 4 + lax.rem(y + d, 4) for d in (0, 3, 1, 2)]
    across = [(1 - xl) * 4 + lax.rem(y + d, 4) for d in (0, 3, 1, 2)]
    offsets = (256 * jnp.stack(around + across)).astype(jnp.int32)
    place = jnp.stack([z, me]).astype(jnp.int32)
    hold = lax.optimization_barrier

    def exchange(pieces):
        return tuple(swap(pieces[k], plane, k) for k in (1, 2, 3))

    block, own = prepare(tokens, routes.T, route_gain.T, gate_weight[0], up_weight[0], down_weight[0])

    up1, down1 = shift(block, "z", 1), shift(block, "z", -1)
    own_u, own_d, other = shift(own, "y", 1), shift(own, "y", -1), swap(own, "xl", 1)
    up2, down2 = shift(up1, "z", 1), shift(down1, "z", -1)
    up1, down1, up2, down2, own_u, own_d, other = hold((up1, down1, up2, down2, own_u, own_d, other))

    oth_u, oth_d = shift(other, "y", 1), shift(other, "y", -1)
    sent_a, code_a, gain_a = select(FIRST, place, [up2, down2, up1, down1, block])
    got_a = exchange(sent_a)
    up3, down3 = shift(up2, "z", 1), shift(down2, "z", -1)
    up4, down4 = shift(up3[:64], "z", 1), shift(down3[64:], "z", -1)
    near = (own_u[:768], own_d[768:1536], own_u[1536:1920], own_d[1920:])
    oth_u, oth_d, got_a, up3, down3, up4, down4, near = hold((oth_u, oth_d, got_a, up3, down3, up4, down4, near))

    far = (shift(near[0], "y", 1), shift(near[1], "y", -1), shift(oth_u[:768], "y", 1), shift(oth_d[768:1536], "y", -1))
    sent_b, code_b, gain_b = select(SECOND, place, [up4, down4, up3, down3])
    got_b = exchange(sent_b)
    half = query_weight.shape[0] // 2
    share = lax.dynamic_slice(query_weight.T, (0, c * half), (query_weight.shape[1], half))
    near = near[2:] + (oth_u[1536:1920], oth_d[1920:])
    far, got_b, near, share = hold((far, got_b, near, share))

    q_own = lax.all_gather(share, ("xl", "y"), axis=0, tiled=True)
    low = tuple(shift(x, "y", d) for x, d in zip(near, (1, -1, 1, -1)))
    wide = [own, own_u, own_d, far[0], far[1], other, oth_u, oth_d, far[2], far[3]]
    hidden_a = hidden_of(offsets, (sent_a[0],) + got_a, wide)
    hidden_b = hidden_of(offsets, (sent_b[0],) + got_b, wide)
    low, hidden_a, hidden_b = hold((low, hidden_a, hidden_b))
    narrow = [own, own_u, own_d, low[0], low[1], other, oth_u, oth_d, low[2], low[3]]

    ans4, ans3 = answers_of((32, 64), offsets, hidden_b, narrow)
    ans2, ans1 = answers_of((64, 96), offsets, hidden_a, narrow)
    got4 = exchange(ans4)
    got4, ans3, ans2, ans1 = hold((got4, ans3, ans2, ans1))
    low, high = combine((4,), 0, 0, code_b, gain_b, (ans4[0],) + got4, [])
    low, high, got3 = shift(low, "z", -1), shift(high, "z", 1), exchange(ans3)
    low, high, got3, ans2 = hold((low, high, got3, ans2))
    low, high = combine((3, 5), 1, 0, code_b, gain_b, (ans3[0],) + got3, [low, high])
    low, high, got2 = shift(low, "z", -1), shift(high, "z", 1), exchange(ans2)
    low, high, got2, ans1 = hold((low, high, got2, ans1))
    low, high = combine((2, 6), 0, 0, code_a, gain_a, (ans2[0],) + got2, [low, high])
    low, high, got1 = shift(low, "z", -1), shift(high, "z", 1), exchange(ans1)
    low, high, got1, q_own = hold((low, high, got1, q_own))
    got1 = (ans1[0],) + got1
    low, high = combine((1, 7), 2, 0, code_a, gain_a, got1, [low, high])
    low, high, q_other = shift(low, "z", -1), shift(high, "z", 1), swap(q_own, "c", 1)
    sides = (half * jnp.stack([c, 1 - c])).astype(jnp.int32)
    return final(64, sides, code_a, gain_a, got1, tokens, low, high, norm_gain[None, :], q_own, q_other)


def solution(mesh):
    fine = Mesh(mesh.devices.reshape(2, 4, 8, 2, 2), ("xl", "y", "z", "xh", "c"))
    grp, ep = ("xl", "y"), ("z", "xh", "c")
    placed = (
        P(grp + ep, None),
        P(grp + ep, None),
        P(grp + ep, None),
        P(ep, grp, None),
        P(ep, grp, None),
        P(ep, None, grp),
        P(),
        P(None, grp),
    )
    return jax.shard_map(
        shards,
        mesh=fine,
        in_specs=placed,
        out_specs=(P(grp + ep, None), P(grp + ep, None)),
        check_vma=False,
    )
```

```python
import functools

import jax
import jax.numpy as jnp
from jax import lax
from jax.experimental import pallas as pl
from jax.experimental.pallas import tpu as pltpu
from jax.sharding import Mesh, PartitionSpec as P

BF = jnp.bfloat16
F32 = jnp.float32
SLOTS = 32
ANY = pl.BlockSpec(memory_space=pltpu.HBM)
SMEM = pl.BlockSpec(memory_space=pltpu.SMEM)
VMEM = pl.BlockSpec(memory_space=pltpu.VMEM)
GROUPS = ((4,), (3, 5), (2, 6), (1, 7, 0))


def params(mib):
    return pltpu.CompilerParams(vmem_limit_bytes=mib << 20)


def cost(flops, size):
    return pl.CostEstimate(flops=flops, bytes_accessed=size, transcendentals=0)


def shift(x, axis, by):
    n = lax.axis_size(axis)
    return lax.ppermute(x, axis, [(i, (i + by) % n) for i in range(n)])


def swap(x, axes, k):
    n = lax.axis_size(axes)
    return lax.ppermute(x, axes, [(i, i ^ k) for i in range(n)])


def dispatch_kernel(routes, gains, tokens, out, table, onehot):
    experts, rows = 32, tokens.shape[0]

    @pl.when(pl.program_id(0) == 0)
    def _():
        expert = lax.broadcasted_iota(jnp.int32, (experts, rows), 0)
        match = jnp.zeros((experts, rows), F32)
        gain = jnp.zeros((experts, rows), F32)
        for j in range(6):
            hit = routes[j : j + 1, :] == expert
            match = match + jnp.where(hit, 1.0, 0.0)
            gain = gain + jnp.where(hit, gains[j : j + 1, :], 0.0)
        before = lax.broadcasted_iota(jnp.int32, (rows, rows), 0) < lax.broadcasted_iota(jnp.int32, (rows, rows), 1)
        rank = jnp.dot(match.astype(BF), jnp.where(before, 1.0, 0.0).astype(BF), preferred_element_type=F32)
        code = jnp.where(match > 0.5, rank, -1.0)
        table[0:experts] = code
        table[experts : 2 * experts] = gain
        slot = lax.broadcasted_iota(jnp.int32, (SLOTS, rows), 0).astype(F32)
        for e in range(experts):
            onehot[e * SLOTS : (e + 1) * SLOTS] = jnp.where(code[e : e + 1, :] == slot, 1.0, 0.0).astype(BF)

    @pl.loop(0, 4)
    def _(i):
        part = pl.ds(pl.multiple_of(i * 256, 256), 256)
        out[part] = jnp.dot(onehot[part], tokens[...], preferred_element_type=F32).astype(BF)


def dispatch(routes, gains, tokens):
    rows, width = tokens.shape
    step = 512
    return pl.pallas_call(
        dispatch_kernel,
        out_shape=(jax.ShapeDtypeStruct((32 * SLOTS, width), BF), jax.ShapeDtypeStruct((64, rows), F32)),
        grid=(width // step,),
        in_specs=[
            pl.BlockSpec((6, rows), lambda j: (0, 0)),
            pl.BlockSpec((6, rows), lambda j: (0, 0)),
            pl.BlockSpec((rows, step), lambda j: (0, j)),
        ],
        out_specs=(pl.BlockSpec((32 * SLOTS, step), lambda j: (0, j)), pl.BlockSpec((64, rows), lambda j: (0, 0))),
        scratch_shapes=[pltpu.VMEM((32 * SLOTS, rows), BF)],
        compiler_params=params(62),
        cost_estimate=cost(1 << 29, 5 << 20),
    )(routes, gains, tokens)


def mixing_kernel(place, *refs):
    tables, out = refs[:8], refs[8]
    slot = lax.broadcasted_iota(jnp.int32, (SLOTS, 128), 0).astype(F32)
    for s in range(8):
        parts = []
        for k in range(4):
            expert = 4 * place[0] + lax.bitwise_xor(place[1], k)
            code, gain = tables[s][pl.ds(expert, 1), :], tables[s][pl.ds(expert + 32, 1), :]
            parts.append(jnp.where(code == slot, gain, 0.0))
        weight = jnp.concatenate(parts, axis=0).T
        high = weight.astype(BF)
        out[s, :, 0:128] = high
        out[s, :, 128:256] = (weight - high.astype(F32)).astype(BF)


def mixing(place, tables):
    return pl.pallas_call(
        mixing_kernel,
        out_shape=jax.ShapeDtypeStruct((8, 128, 256), BF),
        in_specs=[SMEM] + [VMEM] * 8,
        out_specs=VMEM,
        compiler_params=params(8),
        cost_estimate=cost(1 << 22, 1 << 20),
    )(place, *tables)


def expert_kernel(groups, place, offsets, *refs):
    arrived, gates, ups, downs = refs[0], refs[1:7], refs[7:13], refs[13:19]
    outs, (x, hidden, gate, up, down, sems) = refs[19:-6], refs[-6:]
    copies = []

    def copy(src, dst):
        c = pltpu.make_async_copy(src, dst, sems.at[len(copies)])
        c.start()
        copies.append(c)

    for parts, whole in ((gates, gate), (ups, up)):
        copy(parts[0], whole.at[pl.ds(pl.multiple_of(offsets[0], 1024), 1024)])
        for i in range(3):
            copy(parts[1 + i], whole.at[pl.ds(pl.multiple_of(offsets[1 + i], 256), 256)])
        far = pl.multiple_of(offsets[4], 256)
        copy(parts[4], whole.at[pl.ds(far, 128)])
        copy(parts[5], whole.at[pl.ds(pl.multiple_of(far + 128, 128), 128)])
    at = 0
    for group in groups:
        for k in range(4):
            for s in group:
                source = 4 * lax.rem(place[0] + 8 - s, 8) + lax.bitwise_xor(place[1], k)
                copy(arrived.at[pl.ds(pl.multiple_of(source * SLOTS, SLOTS), SLOTS)], x.at[at : at + SLOTS])
                at += SLOTS
    first = len(copies)
    copy(downs[0], down.at[:, pl.ds(pl.multiple_of(offsets[0], 1024), 1024)])
    for i in range(3):
        copy(downs[1 + i], down.at[:, pl.ds(pl.multiple_of(offsets[1 + i], 256), 256)])
    far = pl.ds(pl.multiple_of(offsets[4], 256), 256)
    copy(downs[4], down.at[0:384, far])
    copy(downs[5], down.at[384:768, far])
    for c in copies[:first]:
        c.wait()

    @pl.loop(0, gate.shape[1] // 256)
    def _(j):
        cols = pl.ds(pl.multiple_of(j * 256, 256), 256)
        g = jnp.dot(x[...], gate[:, cols], preferred_element_type=F32)
        u = jnp.dot(x[...], up[:, cols], preferred_element_type=F32)
        hidden[:, cols] = (g / (1.0 + jnp.exp(-g)) * u).astype(BF)

    for c in copies[first:]:
        c.wait()

    @pl.loop(0, down.shape[1] // 256)
    def _(j):
        cols = pl.ds(pl.multiple_of(j * 256, 256), 256)
        answer = jnp.dot(hidden[...], down[:, cols], preferred_element_type=F32).astype(BF)
        at = 0
        for i, group in enumerate(groups):
            for k in range(4):
                size = len(group) * SLOTS
                outs[4 * i + k][:, cols] = answer[at : at + size]
                at += size


def expert(groups, place, offsets, arrived, gates, ups, downs):
    width, units = arrived.shape[1], gates[0].shape[1]
    shapes = [jax.ShapeDtypeStruct((len(g) * SLOTS, width), BF) for g in groups for _ in range(4)]
    rows = sum(x.shape[0] for x in shapes)
    out = pl.pallas_call(
        functools.partial(expert_kernel, groups),
        out_shape=tuple(shapes),
        in_specs=[SMEM, SMEM] + [ANY] * 19,
        out_specs=(VMEM,) * len(shapes),
        scratch_shapes=[
            pltpu.VMEM((rows, width), BF),
            pltpu.VMEM((rows, units), BF),
            pltpu.VMEM((width, units), BF),
            pltpu.VMEM((width, units), BF),
            pltpu.VMEM((units, width), BF),
            pltpu.SemaphoreType.DMA((18 + rows // SLOTS,)),
        ],
        compiler_params=params(62),
        cost_estimate=cost(6 * rows * width * units, 16 << 20),
    )(place, offsets, arrived, *gates, *ups, *downs)
    return [out[4 * i : 4 * i + 4] for i in range(len(groups))]


def combined(weight, answers):
    rows = jnp.concatenate(list(answers) * 2, axis=0)
    return jnp.dot(weight, rows, preferred_element_type=F32)


def combine_kernel(blocks, n_in, *refs):
    weights, refs = refs[: len(blocks)], refs[len(blocks) :]
    answers, arrived, outs = refs[:4], refs[4 : 4 + n_in], refs[4 + n_in :]
    for i, s in enumerate(blocks):
        rows = slice(i * SLOTS, (i + 1) * SLOTS)
        total = combined(weights[i][...], [a[rows] for a in answers])
        if s == 4:
            outs[0][...] = total[0:64].astype(BF)
            outs[1][...] = total[64:128].astype(BF)
        elif s == 3:
            outs[i][0:64] = (total[0:64] + arrived[i][...].astype(F32)).astype(BF)
            outs[i][64:128] = total[64:128].astype(BF)
        elif s == 5:
            outs[i][0:64] = total[0:64].astype(BF)
            outs[i][64:128] = (total[64:128] + arrived[i][...].astype(F32)).astype(BF)
        else:
            outs[i][...] = (total + arrived[i][...].astype(F32)).astype(BF)


def weight_of(s):
    return pl.BlockSpec((None, 128, 256), lambda *_: (s, 0, 0))


def combine(blocks, weights, answers, arrived):
    width, step = answers[0].shape[1], 1024
    height = 64 if blocks == (4,) else 128
    used = len(blocks) * SLOTS
    return pl.pallas_call(
        functools.partial(combine_kernel, blocks, len(arrived)),
        out_shape=(jax.ShapeDtypeStruct((height, width), BF),) * 2,
        grid=(width // step,),
        in_specs=[weight_of(s) for s in blocks]
        + [pl.BlockSpec((used, step), lambda j: (0, j))] * 4
        + [pl.BlockSpec((x.shape[0], step), lambda j: (0, j)) for x in arrived],
        out_specs=(pl.BlockSpec((height, step), lambda j: (0, j)),) * 2,
        compiler_params=params(8),
        cost_estimate=cost(len(blocks) << 27, 2 << 20),
    )(*[weights] * len(blocks), *answers, *arrived)


def final_kernel(offsets, weight, a0, a1, a2, a3, tokens, left, right, norm, q0, q1, mixed, query, total, normed, held, sems):
    copies = [pltpu.make_async_copy(q, held.at[i], sems.at[i]) for i, q in enumerate((q0, q1))]
    for c in copies:
        c.start()
    width, step = tokens.shape[1], 512
    square = jnp.zeros((128, 1), F32)
    start = 2 * SLOTS
    for j in range(width // step):
        cols = slice(j * step, (j + 1) * step)
        part = combined(weight[...], [a[start : start + SLOTS, cols] for a in (a0, a1, a2, a3)])
        part = part + tokens[:, cols].astype(F32)
        part = part + left[:, cols].astype(F32) + right[:, cols].astype(F32)
        mixed[:, cols] = part.astype(BF)
        total[:, cols] = part
        square = square + jnp.sum(part * part, axis=1, keepdims=True)
    scale = lax.rsqrt(square / width + 1e-06)
    for j in range(width // step):
        cols = slice(j * step, (j + 1) * step)
        normed[:, cols] = (total[:, cols] * scale * norm[:, cols]).astype(BF)
    for c in copies:
        c.wait()
    half = width // 2
    sides = [normed[:, pl.ds(pl.multiple_of(offsets[i], half), half)] for i in range(2)]
    dims = (((1,), (1,)), ((), ()))

    @pl.loop(0, query.shape[1] // 256)
    def _(j):
        cols = pl.ds(pl.multiple_of(j * 256, 256), 256)
        out = lax.dot_general(sides[0], held[0, cols], dims, preferred_element_type=F32)
        out = out + lax.dot_general(sides[1], held[1, cols], dims, preferred_element_type=F32)
        query[:, cols] = out.astype(BF)


def final(offsets, weights, answers, tokens, left, right, norm, q0, q1):
    rows, width = tokens.shape
    features = q0.shape[0]

    def whole(x):
        return pl.BlockSpec(x.shape, lambda i: (0, 0))

    return pl.pallas_call(
        final_kernel,
        out_shape=(jax.ShapeDtypeStruct((rows, width), BF), jax.ShapeDtypeStruct((rows, features), BF)),
        grid=(1,),
        in_specs=[SMEM, weight_of(0)] + [whole(x) for x in (*answers, tokens, left, right, norm)] + [ANY] * 2,
        out_specs=(pl.BlockSpec((rows, width), lambda i: (0, 0)), pl.BlockSpec((rows, features), lambda i: (0, 0))),
        scratch_shapes=[
            pltpu.VMEM((rows, width), F32),
            pltpu.VMEM((rows, width), BF),
            pltpu.VMEM((2, features, width // 2), BF),
            pltpu.SemaphoreType.DMA((2,)),
        ],
        compiler_params=params(24),
        cost_estimate=cost(2 * rows * width * features, 8 << 20),
    )(offsets, weights, *answers, tokens, left, right, norm, q0, q1)


def across_x(x):
    other = swap(x, "xl", 1)
    up, down = shift(other, "y", 1), shift(other, "y", -1)
    half = x.shape[0] // 2
    return [other, up, down, shift(up[:half], "y", 1), shift(down[half:], "y", -1)]


def shards(tokens, routes, route_gain, gate_weight, up_weight, down_weight, norm_gain, query_weight):
    xl, y, z, c = (lax.axis_index(a) for a in ("xl", "y", "z", "c"))
    me = 2 * lax.axis_index("xh") + c
    plane = ("xh", "c")
    across = [1024 * (1 - xl) + 256 * lax.rem(y + d, 4) for d in (0, 3, 1, 2)]
    offsets = jnp.stack([1024 * xl] + across).astype(jnp.int32)
    place = jnp.stack([z, me]).astype(jnp.int32)
    hold = lax.optimization_barrier

    outbound, table = dispatch(routes.T, route_gain.T, tokens)
    arrived = lax.all_to_all(outbound, ("z", "xh", "c"), split_axis=0, concat_axis=0, tiled=True)

    gates = [lax.all_gather(gate_weight[0], "y", axis=0, tiled=True)] + across_x(gate_weight[0])
    ups = [lax.all_gather(up_weight[0], "y", axis=0, tiled=True)] + across_x(up_weight[0])
    downs = [lax.all_gather(down_weight[0], "y", axis=1, tiled=True)] + across_x(down_weight[0])
    weights = mixing(place, [table] + [shift(table, "z", s) for s in range(1, 8)])

    half = query_weight.shape[0] // 2
    share = lax.dynamic_slice(query_weight.T, (0, c * half), (query_weight.shape[1], half))
    share, gates, ups, downs, weights = hold((share, gates, ups, downs, weights))
    q_own = lax.all_gather(share, ("xl", "y"), axis=0, tiled=True)

    def exchange(pieces):
        return tuple(swap(pieces[k], plane, k) for k in (1, 2, 3))

    ans4, ans3 = expert(GROUPS[:2], place, offsets, arrived, gates, ups, downs)
    got4 = exchange(ans4)
    ans2, ans1 = expert(GROUPS[2:], place, offsets, arrived, gates, ups, downs)
    got4, ans3, ans2, ans1 = hold((got4, ans3, ans2, ans1))
    low, high = combine((4,), weights, (ans4[0],) + got4, [])
    low, high, got3 = shift(low, "z", -1), shift(high, "z", 1), exchange(ans3)
    low, high, got3, ans2, q_own = hold((low, high, got3, ans2, q_own))
    low, high = combine((3, 5), weights, (ans3[0],) + got3, [low, high])
    q_other = swap(q_own, "c", 1)
    low, high, got2 = shift(low, "z", -1), shift(high, "z", 1), exchange(ans2)
    low, high, got2, ans1, q_other = hold((low, high, got2, ans1, q_other))
    low, high = combine((2, 6), weights, (ans2[0],) + got2, [low, high])
    low, high, got1 = shift(low, "z", -1), shift(high, "z", 1), exchange(ans1)
    low, high, got1 = hold((low, high, got1))
    got1 = (ans1[0],) + got1
    low, high = combine((1, 7), weights, got1, [low, high])
    low, high = shift(low, "z", -1), shift(high, "z", 1)
    sides = (half * jnp.stack([c, 1 - c])).astype(jnp.int32)
    return final(sides, weights, got1, tokens, low, high, norm_gain[None, :], q_own, q_other)


def solution(mesh):
    fine = Mesh(mesh.devices.reshape(2, 4, 8, 2, 2), ("xl", "y", "z", "xh", "c"))
    grp, ep = ("xl", "y"), ("z", "xh", "c")
    placed = (
        P(grp + ep, None),
        P(grp + ep, None),
        P(grp + ep, None),
        P(ep, grp, None),
        P(ep, grp, None),
        P(ep, None, grp),
        P(),
        P(None, grp),
    )
    return jax.shard_map(
        shards,
        mesh=fine,
        in_specs=placed,
        out_specs=(P(grp + ep, None), P(grp + ep, None)),
        check_vma=False,
    )
```

```python
import functools

import jax
import jax.numpy as jnp
from jax import lax
from jax.experimental import pallas as pl
from jax.experimental.pallas import tpu as pltpu
from jax.sharding import Mesh, PartitionSpec as P

BF = jnp.bfloat16
F32 = jnp.float32
SLOTS = 32
ANY = pl.BlockSpec(memory_space=pltpu.HBM)
SMEM = pl.BlockSpec(memory_space=pltpu.SMEM)
VMEM = pl.BlockSpec(memory_space=pltpu.VMEM)
GROUPS = ((4,), (3, 5), (2, 6), (1, 7, 0))


def params(mib):
    return pltpu.CompilerParams(vmem_limit_bytes=mib << 20)


def cost(flops, size):
    return pl.CostEstimate(flops=flops, bytes_accessed=size, transcendentals=0)


def shift(x, axis, by):
    n = lax.axis_size(axis)
    return lax.ppermute(x, axis, [(i, (i + by) % n) for i in range(n)])


def swap(x, axes, k):
    n = lax.axis_size(axes)
    return lax.ppermute(x, axes, [(i, i ^ k) for i in range(n)])


def dispatch_kernel(routes, gains, tokens, out, table, onehot):
    experts, rows = 32, tokens.shape[0]

    @pl.when(pl.program_id(0) == 0)
    def _():
        expert = lax.broadcasted_iota(jnp.int32, (experts, rows), 0)
        match = jnp.zeros((experts, rows), F32)
        gain = jnp.zeros((experts, rows), F32)
        for j in range(6):
            hit = routes[j : j + 1, :] == expert
            match = match + jnp.where(hit, 1.0, 0.0)
            gain = gain + jnp.where(hit, gains[j : j + 1, :], 0.0)
        before = lax.broadcasted_iota(jnp.int32, (rows, rows), 0) < lax.broadcasted_iota(jnp.int32, (rows, rows), 1)
        rank = jnp.dot(match.astype(BF), jnp.where(before, 1.0, 0.0).astype(BF), preferred_element_type=F32)
        code = jnp.where(match > 0.5, rank, -1.0)
        for d in range(experts // 4):
            own = slice(4 * d, 4 * d + 4)
            table[8 * d : 8 * d + 4] = code[own]
            table[8 * d + 4 : 8 * d + 8] = gain[own]
        slot = lax.broadcasted_iota(jnp.int32, (SLOTS, rows), 0).astype(F32)
        for e in range(experts):
            onehot[e * SLOTS : (e + 1) * SLOTS] = jnp.where(code[e : e + 1, :] == slot, 1.0, 0.0).astype(BF)

    @pl.loop(0, 4)
    def _(i):
        part = pl.ds(pl.multiple_of(i * 256, 256), 256)
        out[part] = jnp.dot(onehot[part], tokens[...], preferred_element_type=F32).astype(BF)


def dispatch(routes, gains, tokens):
    rows, width = tokens.shape
    step = 512
    return pl.pallas_call(
        dispatch_kernel,
        out_shape=(jax.ShapeDtypeStruct((32 * SLOTS, width), BF), jax.ShapeDtypeStruct((64, rows), F32)),
        grid=(width // step,),
        in_specs=[
            pl.BlockSpec((6, rows), lambda j: (0, 0)),
            pl.BlockSpec((6, rows), lambda j: (0, 0)),
            pl.BlockSpec((rows, step), lambda j: (0, j)),
        ],
        out_specs=(pl.BlockSpec((32 * SLOTS, step), lambda j: (0, j)), pl.BlockSpec((64, rows), lambda j: (0, 0))),
        scratch_shapes=[pltpu.VMEM((32 * SLOTS, rows), BF)],
        compiler_params=params(62),
        cost_estimate=cost(1 << 29, 5 << 20),
    )(routes, gains, tokens)


def mixing_kernel(place, table, out):
    slot = lax.broadcasted_iota(jnp.int32, (SLOTS, 128), 0).astype(F32)
    for s in range(8):
        source = lax.rem(place[0] + 8 - s, 8)
        parts = []
        for k in range(4):
            row = 8 * source + lax.bitwise_xor(place[1], k)
            code, gain = table[pl.ds(row, 1), :], table[pl.ds(row + 4, 1), :]
            parts.append(jnp.where(code == slot, gain, 0.0))
        weight = jnp.concatenate(parts, axis=0).T
        high = weight.astype(BF)
        out[s, :, 0:128] = high
        out[s, :, 128:256] = (weight - high.astype(F32)).astype(BF)


def mixing(place, table):
    return pl.pallas_call(
        mixing_kernel,
        out_shape=jax.ShapeDtypeStruct((8, 128, 256), BF),
        in_specs=[SMEM, VMEM],
        out_specs=VMEM,
        compiler_params=params(8),
        cost_estimate=cost(1 << 22, 1 << 20),
    )(place, table)


def expert_kernel(groups, place, offsets, *refs):
    arrived, gates, ups, downs = refs[0], refs[1:7], refs[7:13], refs[13:19]
    outs, (x, hidden, gate, up, down, sems) = refs[19:-6], refs[-6:]
    copies = []

    def copy(src, dst):
        c = pltpu.make_async_copy(src, dst, sems.at[len(copies)])
        c.start()
        copies.append(c)

    for parts, whole in ((gates, gate), (ups, up)):
        copy(parts[0], whole.at[pl.ds(pl.multiple_of(offsets[0], 1024), 1024)])
        for i in range(3):
            copy(parts[1 + i], whole.at[pl.ds(pl.multiple_of(offsets[1 + i], 256), 256)])
        far = pl.multiple_of(offsets[4], 256)
        copy(parts[4], whole.at[pl.ds(far, 128)])
        copy(parts[5], whole.at[pl.ds(pl.multiple_of(far + 128, 128), 128)])
    at = 0
    for group in groups:
        for k in range(4):
            for s in group:
                source = 4 * lax.rem(place[0] + 8 - s, 8) + lax.bitwise_xor(place[1], k)
                copy(arrived.at[pl.ds(pl.multiple_of(source * SLOTS, SLOTS), SLOTS)], x.at[at : at + SLOTS])
                at += SLOTS
    first = len(copies)
    copy(downs[0], down.at[:, pl.ds(pl.multiple_of(offsets[0], 1024), 1024)])
    for i in range(3):
        copy(downs[1 + i], down.at[:, pl.ds(pl.multiple_of(offsets[1 + i], 256), 256)])
    far = pl.ds(pl.multiple_of(offsets[4], 256), 256)
    copy(downs[4], down.at[0:384, far])
    copy(downs[5], down.at[384:768, far])
    for c in copies[:first]:
        c.wait()

    @pl.loop(0, gate.shape[1] // 256)
    def _(j):
        cols = pl.ds(pl.multiple_of(j * 256, 256), 256)
        g = jnp.dot(x[...], gate[:, cols], preferred_element_type=F32)
        u = jnp.dot(x[...], up[:, cols], preferred_element_type=F32)
        hidden[:, cols] = (g / (1.0 + jnp.exp(-g)) * u).astype(BF)

    for c in copies[first:]:
        c.wait()

    @pl.loop(0, down.shape[1] // 256)
    def _(j):
        cols = pl.ds(pl.multiple_of(j * 256, 256), 256)
        answer = jnp.dot(hidden[...], down[:, cols], preferred_element_type=F32).astype(BF)
        at = 0
        for i, group in enumerate(groups):
            for k in range(4):
                size = len(group) * SLOTS
                outs[4 * i + k][:, cols] = answer[at : at + size]
                at += size


def expert(groups, place, offsets, arrived, gates, ups, downs):
    width, units = arrived.shape[1], gates[0].shape[1]
    shapes = [jax.ShapeDtypeStruct((len(g) * SLOTS, width), BF) for g in groups for _ in range(4)]
    rows = sum(x.shape[0] for x in shapes)
    out = pl.pallas_call(
        functools.partial(expert_kernel, groups),
        out_shape=tuple(shapes),
        in_specs=[SMEM, SMEM] + [ANY] * 19,
        out_specs=(VMEM,) * len(shapes),
        scratch_shapes=[
            pltpu.VMEM((rows, width), BF),
            pltpu.VMEM((rows, units), BF),
            pltpu.VMEM((width, units), BF),
            pltpu.VMEM((width, units), BF),
            pltpu.VMEM((units, width), BF),
            pltpu.SemaphoreType.DMA((18 + rows // SLOTS,)),
        ],
        compiler_params=params(62),
        cost_estimate=cost(6 * rows * width * units, 16 << 20),
    )(place, offsets, arrived, *gates, *ups, *downs)
    return [out[4 * i : 4 * i + 4] for i in range(len(groups))]


def combined(weight, answers):
    rows = jnp.concatenate(list(answers) * 2, axis=0)
    return jnp.dot(weight, rows, preferred_element_type=F32)


def combine_kernel(blocks, n_in, *refs):
    weights, refs = refs[: len(blocks)], refs[len(blocks) :]
    answers, arrived, outs = refs[:4], refs[4 : 4 + n_in], refs[4 + n_in :]
    for i, s in enumerate(blocks):
        rows = slice(i * SLOTS, (i + 1) * SLOTS)
        total = combined(weights[i][...], [a[rows] for a in answers])
        if s == 4:
            outs[0][...] = total[0:64].astype(BF)
            outs[1][...] = total[64:128].astype(BF)
        elif s == 3:
            outs[i][0:64] = (total[0:64] + arrived[i][...].astype(F32)).astype(BF)
            outs[i][64:128] = total[64:128].astype(BF)
        elif s == 5:
            outs[i][0:64] = total[0:64].astype(BF)
            outs[i][64:128] = (total[64:128] + arrived[i][...].astype(F32)).astype(BF)
        else:
            outs[i][...] = (total + arrived[i][...].astype(F32)).astype(BF)


def weight_of(s):
    return pl.BlockSpec((None, 128, 256), lambda *_: (s, 0, 0))


def combine(blocks, weights, answers, arrived):
    width, step = answers[0].shape[1], 1024
    height = 64 if blocks == (4,) else 128
    used = len(blocks) * SLOTS
    return pl.pallas_call(
        functools.partial(combine_kernel, blocks, len(arrived)),
        out_shape=(jax.ShapeDtypeStruct((height, width), BF),) * 2,
        grid=(width // step,),
        in_specs=[weight_of(s) for s in blocks]
        + [pl.BlockSpec((used, step), lambda j: (0, j))] * 4
        + [pl.BlockSpec((x.shape[0], step), lambda j: (0, j)) for x in arrived],
        out_specs=(pl.BlockSpec((height, step), lambda j: (0, j)),) * 2,
        compiler_params=params(8),
        cost_estimate=cost(len(blocks) << 27, 2 << 20),
    )(*[weights] * len(blocks), *answers, *arrived)


def final_kernel(offsets, weight, a0, a1, a2, a3, tokens, left, right, norm, q0, q1, mixed, query, total, normed, held, sems):
    copies = [pltpu.make_async_copy(q, held.at[i], sems.at[i]) for i, q in enumerate((q0, q1))]
    for c in copies:
        c.start()
    width, step = tokens.shape[1], 512
    square = jnp.zeros((128, 1), F32)
    start = 2 * SLOTS
    for j in range(width // step):
        cols = slice(j * step, (j + 1) * step)
        part = combined(weight[...], [a[start : start + SLOTS, cols] for a in (a0, a1, a2, a3)])
        part = part + tokens[:, cols].astype(F32)
        part = part + left[:, cols].astype(F32) + right[:, cols].astype(F32)
        mixed[:, cols] = part.astype(BF)
        total[:, cols] = part
        square = square + jnp.sum(part * part, axis=1, keepdims=True)
    scale = lax.rsqrt(square / width + 1e-06)
    for j in range(width // step):
        cols = slice(j * step, (j + 1) * step)
        normed[:, cols] = (total[:, cols] * scale * norm[:, cols]).astype(BF)
    for c in copies:
        c.wait()
    half = width // 2
    sides = [normed[:, pl.ds(pl.multiple_of(offsets[i], half), half)] for i in range(2)]
    dims = (((1,), (1,)), ((), ()))

    @pl.loop(0, query.shape[1] // 256)
    def _(j):
        cols = pl.ds(pl.multiple_of(j * 256, 256), 256)
        out = lax.dot_general(sides[0], held[0, cols], dims, preferred_element_type=F32)
        out = out + lax.dot_general(sides[1], held[1, cols], dims, preferred_element_type=F32)
        query[:, cols] = out.astype(BF)


def final(offsets, weights, answers, tokens, left, right, norm, q0, q1):
    rows, width = tokens.shape
    features = q0.shape[0]

    def whole(x):
        return pl.BlockSpec(x.shape, lambda i: (0, 0))

    return pl.pallas_call(
        final_kernel,
        out_shape=(jax.ShapeDtypeStruct((rows, width), BF), jax.ShapeDtypeStruct((rows, features), BF)),
        grid=(1,),
        in_specs=[SMEM, weight_of(0)] + [whole(x) for x in (*answers, tokens, left, right, norm)] + [ANY] * 2,
        out_specs=(pl.BlockSpec((rows, width), lambda i: (0, 0)), pl.BlockSpec((rows, features), lambda i: (0, 0))),
        scratch_shapes=[
            pltpu.VMEM((rows, width), F32),
            pltpu.VMEM((rows, width), BF),
            pltpu.VMEM((2, features, width // 2), BF),
            pltpu.SemaphoreType.DMA((2,)),
        ],
        compiler_params=params(62),
        cost_estimate=cost(2 * rows * width * features, 8 << 20),
    )(offsets, weights, *answers, tokens, left, right, norm, q0, q1)


def across_x(x):
    other = swap(x, "xl", 1)
    up, down = shift(other, "y", 1), shift(other, "y", -1)
    half = x.shape[0] // 2
    return [other, up, down, shift(up[:half], "y", 1), shift(down[half:], "y", -1)]


def shards(tokens, routes, route_gain, gate_weight, up_weight, down_weight, norm_gain, query_weight):
    xl, y, z, c = (lax.axis_index(a) for a in ("xl", "y", "z", "c"))
    me = 2 * lax.axis_index("xh") + c
    plane = ("xh", "c")
    across = [1024 * (1 - xl) + 256 * lax.rem(y + d, 4) for d in (0, 3, 1, 2)]
    offsets = jnp.stack([1024 * xl] + across).astype(jnp.int32)
    place = jnp.stack([z, me]).astype(jnp.int32)
    hold = lax.optimization_barrier

    outbound, table = dispatch(routes.T, route_gain.T, tokens)
    arrived = lax.all_to_all(outbound, ("z", "xh", "c"), split_axis=0, concat_axis=0, tiled=True)

    gates = [lax.all_gather(gate_weight[0], "y", axis=0, tiled=True)] + across_x(gate_weight[0])
    ups = [lax.all_gather(up_weight[0], "y", axis=0, tiled=True)] + across_x(up_weight[0])
    downs = [lax.all_gather(down_weight[0], "y", axis=1, tiled=True)] + across_x(down_weight[0])
    tables = lax.all_to_all(table, "z", split_axis=0, concat_axis=0, tiled=True)
    weights = mixing(place, tables)

    half = query_weight.shape[0] // 2
    share = lax.dynamic_slice(query_weight.T, (0, c * half), (query_weight.shape[1], half))
    q_own = lax.all_gather(share, ("xl", "y"), axis=0, tiled=True)

    def exchange(pieces):
        return tuple(swap(pieces[k], plane, k) for k in (1, 2, 3))

    ans4, ans3 = expert(GROUPS[:2], place, offsets, arrived, gates, ups, downs)
    got4 = exchange(ans4)
    ans2, ans1 = expert(GROUPS[2:], place, offsets, arrived, gates, ups, downs)
    got4, ans3, ans2, ans1 = hold((got4, ans3, ans2, ans1))
    low, high = combine((4,), weights, (ans4[0],) + got4, [])
    low, high, got3 = shift(low, "z", -1), shift(high, "z", 1), exchange(ans3)
    low, high, got3, ans2, q_own = hold((low, high, got3, ans2, q_own))
    low, high = combine((3, 5), weights, (ans3[0],) + got3, [low, high])
    q_other = swap(q_own, "c", 1)
    low, high, got2 = shift(low, "z", -1), shift(high, "z", 1), exchange(ans2)
    low, high, got2, ans1, q_other = hold((low, high, got2, ans1, q_other))
    low, high = combine((2, 6), weights, (ans2[0],) + got2, [low, high])
    low, high, got1 = shift(low, "z", -1), shift(high, "z", 1), exchange(ans1)
    low, high, got1 = hold((low, high, got1))
    got1 = (ans1[0],) + got1
    low, high = combine((1, 7), weights, got1, [low, high])
    low, high = shift(low, "z", -1), shift(high, "z", 1)
    sides = (half * jnp.stack([c, 1 - c])).astype(jnp.int32)
    return final(sides, weights, got1, tokens, low, high, norm_gain[None, :], q_own, q_other)


def solution(mesh):
    fine = Mesh(mesh.devices.reshape(2, 4, 8, 2, 2), ("xl", "y", "z", "xh", "c"))
    grp, ep = ("xl", "y"), ("z", "xh", "c")
    placed = (
        P(grp + ep, None),
        P(grp + ep, None),
        P(grp + ep, None),
        P(ep, grp, None),
        P(ep, grp, None),
        P(ep, None, grp),
        P(),
        P(None, grp),
    )
    return jax.shard_map(
        shards,
        mesh=fine,
        in_specs=placed,
        out_specs=(P(grp + ep, None), P(grp + ep, None)),
        check_vma=False,
    )
```

```python
import functools

import jax
import jax.numpy as jnp
from jax import lax
from jax.experimental import pallas as pl
from jax.experimental.pallas import tpu as pltpu
from jax.sharding import Mesh, PartitionSpec as P

BF = jnp.bfloat16
F32 = jnp.float32
SLOTS = 32
ROWS = 64
ANY = pl.BlockSpec(memory_space=pltpu.HBM)
SMEM = pl.BlockSpec(memory_space=pltpu.SMEM)
VMEM = pl.BlockSpec(memory_space=pltpu.VMEM)
GROUPS = ((4,), (3, 5), (2, 6), (1, 7, 0))


def params(mib):
    return pltpu.CompilerParams(vmem_limit_bytes=mib << 20)


def cost(flops, size):
    return pl.CostEstimate(flops=flops, bytes_accessed=size, transcendentals=0)


def shift(x, axis, by):
    n = lax.axis_size(axis)
    return lax.ppermute(x, axis, [(i, (i + by) % n) for i in range(n)])


def swap(x, axes, k):
    n = lax.axis_size(axes)
    return lax.ppermute(x, axes, [(i, i ^ k) for i in range(n)])


def dispatch_kernel(routes, tokens, out, onehot):
    experts, rows = 32, tokens.shape[0]

    @pl.when(pl.program_id(0) == 0)
    def _():
        expert = lax.broadcasted_iota(jnp.int32, (experts, rows), 0)
        match = jnp.zeros((experts, rows), F32)
        for j in range(6):
            match = match + jnp.where(routes[j : j + 1, :] == expert, 1.0, 0.0)
        before = lax.broadcasted_iota(jnp.int32, (rows, rows), 0) < lax.broadcasted_iota(jnp.int32, (rows, rows), 1)
        rank = jnp.dot(match.astype(BF), jnp.where(before, 1.0, 0.0).astype(BF), preferred_element_type=F32)
        code = jnp.where(match > 0.5, rank, -1.0)
        slot = lax.broadcasted_iota(jnp.int32, (SLOTS, rows), 0).astype(F32)
        for e in range(experts):
            onehot[e * SLOTS : (e + 1) * SLOTS] = jnp.where(code[e : e + 1, :] == slot, 1.0, 0.0).astype(BF)

    @pl.loop(0, 4)
    def _(i):
        part = pl.ds(pl.multiple_of(i * 256, 256), 256)
        out[part] = jnp.dot(onehot[part], tokens[...], preferred_element_type=F32).astype(BF)


def dispatch(routes, tokens):
    rows, width = tokens.shape
    step = 512
    return pl.pallas_call(
        dispatch_kernel,
        out_shape=jax.ShapeDtypeStruct((32 * SLOTS, width), BF),
        grid=(width // step,),
        in_specs=[
            pl.BlockSpec((6, rows), lambda j: (0, 0)),
            pl.BlockSpec((rows, step), lambda j: (0, j)),
        ],
        out_specs=pl.BlockSpec((32 * SLOTS, step), lambda j: (0, j)),
        scratch_shapes=[pltpu.VMEM((32 * SLOTS, rows), BF)],
        compiler_params=params(62),
        cost_estimate=cost(1 << 29, 5 << 20),
    )(routes, tokens)


def mixing_kernel(place, table, out, match, gain):
    z, me = place[0], place[1]
    for s in range(8):
        block = table[lax.rem(z + 8 - s, 8)].astype(F32)
        routes = block[0:6, 0:128]
        gains = block[0:6, 128:256] + block[0:6, 256:384] + block[0:6, 384:512]
        for k in range(4):
            hit = routes == (4 * z + lax.bitwise_xor(me, k)).astype(F32)
            row = slice(4 * s + k, 4 * s + k + 1)
            match[row] = jnp.sum(jnp.where(hit, 1.0, 0.0), axis=0, keepdims=True)
            gain[row] = jnp.sum(jnp.where(hit, gains, 0.0), axis=0, keepdims=True)
    chosen = match[...]
    before = lax.broadcasted_iota(jnp.int32, (128, 128), 0) < lax.broadcasted_iota(jnp.int32, (128, 128), 1)
    rank = jnp.dot(chosen.astype(BF), jnp.where(before, 1.0, 0.0).astype(BF), preferred_element_type=F32)
    match[...] = jnp.where(chosen > 0.5, rank, -1.0)
    slot = lax.broadcasted_iota(jnp.int32, (SLOTS, 128), 0).astype(F32)
    for s in range(8):
        rows = [slice(4 * s + k, 4 * s + k + 1) for k in range(4)]
        weight = jnp.concatenate([jnp.where(match[r] == slot, gain[r], 0.0) for r in rows], axis=0).T
        high = weight.astype(BF)
        out[s, :, 0:128] = high
        out[s, :, 128:256] = (weight - high.astype(F32)).astype(BF)


def mixing(place, table):
    return pl.pallas_call(
        mixing_kernel,
        out_shape=jax.ShapeDtypeStruct((8, 128, 256), BF),
        in_specs=[SMEM, VMEM],
        out_specs=VMEM,
        scratch_shapes=[pltpu.VMEM((32, 128), F32), pltpu.VMEM((32, 128), F32)],
        compiler_params=params(8),
        cost_estimate=cost(1 << 22, 1 << 20),
    )(place, table)


def expert_kernel(groups, place, offsets, *refs):
    arrived, gates, ups, downs = refs[0], refs[1:7], refs[7:13], refs[13:23]
    outs, (x, hidden, gate, up, down, sems) = refs[23:-6], refs[-6:]
    copies = []

    def copy(src, dst):
        c = pltpu.make_async_copy(src, dst, sems.at[len(copies)])
        c.start()
        copies.append(c)

    spans = [(pl.multiple_of(offsets[0], 1024), 1024)]
    spans += [(pl.multiple_of(offsets[1 + i], 256), 256) for i in range(3)]
    far = pl.multiple_of(offsets[4], 256)
    spans += [(far, 128), (pl.multiple_of(far + 128, 128), 128)]
    tile, marks = 256, []

    def load(j):
        cols = slice(j * tile, (j + 1) * tile)
        for parts, whole in ((gates, gate), (ups, up)):
            for part, (start, size) in zip(parts, spans):
                copy(part.at[:, cols], whole.at[pl.ds(start, size), cols])
        marks.append(len(copies))

    at = 0
    for group in groups:
        for k in range(4):
            for s in group:
                source = 4 * lax.rem(place[0] + 8 - s, 8) + lax.bitwise_xor(place[1], k)
                copy(arrived.at[pl.ds(pl.multiple_of(source * SLOTS, SLOTS), SLOTS)], x.at[at : at + SLOTS])
                at += SLOTS
    tiles = gate.shape[1] // tile
    for j in range(tiles):
        load(j)
    for side in range(2):
        parts = downs[5 * side : 5 * side + 5]
        cols = [pl.ds(pl.multiple_of(offsets[5 - 4 * side + i], 256), 256) for i in range(4)]
        for i in range(3):
            copy(parts[i], down.at[:, cols[i]])
        copy(parts[3], down.at[0:384, cols[3]])
        copy(parts[4], down.at[384:768, cols[3]])
    done = 0
    for j in range(tiles):
        for c in copies[done : marks[j]]:
            c.wait()
        done = marks[j]
        cols = slice(j * tile, (j + 1) * tile)
        g = jnp.dot(x[...], gate[:, cols], preferred_element_type=F32)
        u = jnp.dot(x[...], up[:, cols], preferred_element_type=F32)
        hidden[:, cols] = (g / (1.0 + jnp.exp(-g)) * u).astype(BF)
    for c in copies[done:]:
        c.wait()

    @pl.loop(0, down.shape[1] // 256)
    def _(j):
        cols = pl.ds(pl.multiple_of(j * 256, 256), 256)
        answer = jnp.dot(hidden[...], down[:, cols], preferred_element_type=F32).astype(BF)
        at = 0
        for i, group in enumerate(groups):
            for k in range(4):
                size = len(group) * SLOTS
                outs[4 * i + k][:, cols] = answer[at : at + size]
                at += size


def expert(groups, place, offsets, arrived, gates, ups, downs):
    width, units = arrived.shape[1], gates[0].shape[1]
    shapes = [jax.ShapeDtypeStruct((len(g) * SLOTS, width), BF) for g in groups for _ in range(4)]
    rows = sum(x.shape[0] for x in shapes)
    out = pl.pallas_call(
        functools.partial(expert_kernel, groups),
        out_shape=tuple(shapes),
        in_specs=[SMEM, SMEM] + [ANY] * 23,
        out_specs=(VMEM,) * len(shapes),
        scratch_shapes=[
            pltpu.VMEM((rows, width), BF),
            pltpu.VMEM((rows, units), BF),
            pltpu.VMEM((width, units), BF),
            pltpu.VMEM((width, units), BF),
            pltpu.VMEM((units, width), BF),
            pltpu.SemaphoreType.DMA((46 + rows // SLOTS,)),
        ],
        compiler_params=params(62),
        cost_estimate=cost(6 * rows * width * units, 16 << 20),
    )(place, offsets, arrived, *gates, *ups, *downs)
    return [out[4 * i : 4 * i + 4] for i in range(len(groups))]


def combined(weight, answers):
    rows = jnp.concatenate(list(answers) * 2, axis=0)
    return jnp.dot(weight, rows, preferred_element_type=F32)


def combine_kernel(blocks, n_in, *refs):
    weights, refs = refs[: len(blocks)], refs[len(blocks) :]
    answers, arrived, outs = refs[:4], refs[4 : 4 + n_in], refs[4 + n_in :]
    for i, s in enumerate(blocks):
        rows = slice(i * SLOTS, (i + 1) * SLOTS)
        total = combined(weights[i][...], [a[rows] for a in answers])
        if s == 4:
            outs[0][...] = total[0:64].astype(BF)
            outs[1][...] = total[64:128].astype(BF)
        elif s == 3:
            outs[i][0:64] = (total[0:64] + arrived[i][...].astype(F32)).astype(BF)
            outs[i][64:128] = total[64:128].astype(BF)
        elif s == 5:
            outs[i][0:64] = total[0:64].astype(BF)
            outs[i][64:128] = (total[64:128] + arrived[i][...].astype(F32)).astype(BF)
        else:
            outs[i][...] = (total + arrived[i][...].astype(F32)).astype(BF)


def weight_of(s):
    return pl.BlockSpec((None, 128, 256), lambda *_: (s, 0, 0))


def combine(blocks, weights, answers, arrived):
    width, step = answers[0].shape[1], 1024
    height = 64 if blocks == (4,) else 128
    used = len(blocks) * SLOTS
    return pl.pallas_call(
        functools.partial(combine_kernel, blocks, len(arrived)),
        out_shape=(jax.ShapeDtypeStruct((height, width), BF),) * 2,
        grid=(width // step,),
        in_specs=[weight_of(s) for s in blocks]
        + [pl.BlockSpec((used, step), lambda j: (0, j))] * 4
        + [pl.BlockSpec((x.shape[0], step), lambda j: (0, j)) for x in arrived],
        out_specs=(pl.BlockSpec((height, step), lambda j: (0, j)),) * 2,
        compiler_params=params(8),
        cost_estimate=cost(len(blocks) << 27, 2 << 20),
    )(*[weights] * len(blocks), *answers, *arrived)


def final_kernel(offsets, weight, a0, a1, a2, a3, tokens, left, right, norm, q0, q1, mixed, query, total, normed, held, sems):
    copies = [pltpu.make_async_copy(q, held.at[i], sems.at[i]) for i, q in enumerate((q0, q1))]
    for c in copies:
        c.start()
    width, step = tokens.shape[1], 512
    square = jnp.zeros((128, 1), F32)
    start = 2 * SLOTS
    for j in range(width // step):
        cols = slice(j * step, (j + 1) * step)
        part = combined(weight[...], [a[start : start + SLOTS, cols] for a in (a0, a1, a2, a3)])
        part = part + tokens[:, cols].astype(F32)
        part = part + left[:, cols].astype(F32) + right[:, cols].astype(F32)
        mixed[:, cols] = part.astype(BF)
        total[:, cols] = part
        square = square + jnp.sum(part * part, axis=1, keepdims=True)
    scale = lax.rsqrt(square / width + 1e-06)
    for j in range(width // step):
        cols = slice(j * step, (j + 1) * step)
        normed[:, cols] = (total[:, cols] * scale * norm[:, cols]).astype(BF)
    for c in copies:
        c.wait()
    half = width // 2
    sides = [normed[:, pl.ds(pl.multiple_of(offsets[i], half), half)] for i in range(2)]
    dims = (((1,), (1,)), ((), ()))

    @pl.loop(0, query.shape[1] // 256)
    def _(j):
        cols = pl.ds(pl.multiple_of(j * 256, 256), 256)
        out = lax.dot_general(sides[0], held[0, cols], dims, preferred_element_type=F32)
        out = out + lax.dot_general(sides[1], held[1, cols], dims, preferred_element_type=F32)
        query[:, cols] = out.astype(BF)


def final(offsets, weights, answers, tokens, left, right, norm, q0, q1):
    rows, width = tokens.shape
    features = q0.shape[0]

    def whole(x):
        return pl.BlockSpec(x.shape, lambda i: (0, 0))

    return pl.pallas_call(
        final_kernel,
        out_shape=(jax.ShapeDtypeStruct((rows, width), BF), jax.ShapeDtypeStruct((rows, features), BF)),
        grid=(1,),
        in_specs=[SMEM, weight_of(0)] + [whole(x) for x in (*answers, tokens, left, right, norm)] + [ANY] * 2,
        out_specs=(pl.BlockSpec((rows, width), lambda i: (0, 0)), pl.BlockSpec((rows, features), lambda i: (0, 0))),
        scratch_shapes=[
            pltpu.VMEM((rows, width), F32),
            pltpu.VMEM((rows, width), BF),
            pltpu.VMEM((2, features, width // 2), BF),
            pltpu.SemaphoreType.DMA((2,)),
        ],
        compiler_params=params(62),
        cost_estimate=cost(2 * rows * width * features, 8 << 20),
    )(offsets, weights, *answers, tokens, left, right, norm, q0, q1)


def along_y(x):
    up, down = shift(x, "y", 1), shift(x, "y", -1)
    half = x.shape[0] // 2
    return [x, up, down, shift(up[:half], "y", 1), shift(down[half:], "y", -1)]


def across_x(x):
    return along_y(swap(x, "xl", 1))


def shards(tokens, routes, route_gain, gate_weight, up_weight, down_weight, norm_gain, query_weight):
    xl, y, z, c = (lax.axis_index(a) for a in ("xl", "y", "z", "c"))
    me = 2 * lax.axis_index("xh") + c
    plane = ("xh", "c")
    across = [1024 * (1 - xl) + 256 * lax.rem(y + d, 4) for d in (0, 3, 1, 2)]
    around = [1024 * xl + 256 * lax.rem(y + d, 4) for d in (0, 3, 1, 2)]
    offsets = jnp.stack([1024 * xl] + across + around).astype(jnp.int32)
    place = jnp.stack([z, me]).astype(jnp.int32)
    hold = lax.optimization_barrier

    outbound = dispatch(routes.T, tokens)
    arrived = lax.all_to_all(outbound, ("z", "xh", "c"), split_axis=0, concat_axis=0, tiled=True)

    gates = [lax.all_gather(gate_weight[0], "y", axis=0, tiled=True)] + across_x(gate_weight[0])
    ups = [lax.all_gather(up_weight[0], "y", axis=0, tiled=True)] + across_x(up_weight[0])
    downs = along_y(down_weight[0]) + across_x(down_weight[0])
    high = lax.reduce_precision(route_gain.T, 8, 7)
    middle = lax.reduce_precision(route_gain.T - high, 8, 7)
    table = jnp.concatenate([routes.T.astype(F32), high, middle, route_gain.T - high - middle], axis=1).astype(BF)
    table = jnp.pad(table, ((0, ROWS - 6), (0, 512)))
    weights = mixing(place, lax.all_gather(table, "z"))

    half = query_weight.shape[0] // 2
    share = lax.dynamic_slice(query_weight.T, (0, c * half), (query_weight.shape[1], half))
    q_own = lax.all_gather(share, ("xl", "y"), axis=0, tiled=True)

    def exchange(pieces):
        return tuple(swap(pieces[k], plane, k) for k in (1, 2, 3))

    ans4, ans3 = expert(GROUPS[:2], place, offsets, arrived, gates, ups, downs)
    got4 = exchange(ans4)
    ans2, ans1 = expert(GROUPS[2:], place, offsets, arrived, gates, ups, downs)
    got4, ans3, ans2, ans1 = hold((got4, ans3, ans2, ans1))
    low, high = combine((4,), weights, (ans4[0],) + got4, [])
    low, high, got3 = shift(low, "z", -1), shift(high, "z", 1), exchange(ans3)
    low, high, got3, ans2 = hold((low, high, got3, ans2))
    low, high = combine((3, 5), weights, (ans3[0],) + got3, [low, high])
    low, high, got2 = shift(low, "z", -1), shift(high, "z", 1), exchange(ans2)
    low, high, got2, ans1, q_own = hold((low, high, got2, ans1, q_own))
    low, high = combine((2, 6), weights, (ans2[0],) + got2, [low, high])
    low, high, got1 = shift(low, "z", -1), shift(high, "z", 1), exchange(ans1)
    q_other = swap(q_own, "c", 1)
    low, high, got1, q_other = hold((low, high, got1, q_other))
    got1 = (ans1[0],) + got1
    low, high = combine((1, 7), weights, got1, [low, high])
    low, high = shift(low, "z", -1), shift(high, "z", 1)
    sides = (half * jnp.stack([c, 1 - c])).astype(jnp.int32)
    return final(sides, weights, got1, tokens, low, high, norm_gain[None, :], q_own, q_other)


def solution(mesh):
    fine = Mesh(mesh.devices.reshape(2, 4, 8, 2, 2), ("xl", "y", "z", "xh", "c"))
    grp, ep = ("xl", "y"), ("z", "xh", "c")
    placed = (
        P(grp + ep, None),
        P(grp + ep, None),
        P(grp + ep, None),
        P(ep, grp, None),
        P(ep, grp, None),
        P(ep, None, grp),
        P(),
        P(None, grp),
    )
    return jax.shard_map(
        shards,
        mesh=fine,
        in_specs=placed,
        out_specs=(P(grp + ep, None), P(grp + ep, None)),
        check_vma=False,
    )
```

```python
import functools

import jax
import jax.numpy as jnp
from jax import lax
from jax.experimental import pallas as pl
from jax.experimental.pallas import tpu as pltpu
from jax.sharding import Mesh, PartitionSpec as P

BF = jnp.bfloat16
F32 = jnp.float32
SLOTS = 32
ROWS = 64
ANY = pl.BlockSpec(memory_space=pltpu.HBM)
SMEM = pl.BlockSpec(memory_space=pltpu.SMEM)
VMEM = pl.BlockSpec(memory_space=pltpu.VMEM)
GROUPS = ((4,), (3, 5), (2, 6), (1, 7, 0))


def params(mib):
    return pltpu.CompilerParams(vmem_limit_bytes=mib << 20)


def cost(flops, size):
    return pl.CostEstimate(flops=flops, bytes_accessed=size, transcendentals=0)


def shift(x, axis, by):
    n = lax.axis_size(axis)
    return lax.ppermute(x, axis, [(i, (i + by) % n) for i in range(n)])


def swap(x, axes, k):
    n = lax.axis_size(axes)
    return lax.ppermute(x, axes, [(i, i ^ k) for i in range(n)])


def dispatch_kernel(routes, tokens, out, onehot):
    experts, rows = 32, tokens.shape[0]

    @pl.when(pl.program_id(0) == 0)
    def _():
        expert = lax.broadcasted_iota(jnp.int32, (experts, rows), 0)
        match = jnp.zeros((experts, rows), F32)
        for j in range(6):
            match = match + jnp.where(routes[j : j + 1, :] == expert, 1.0, 0.0)
        before = lax.broadcasted_iota(jnp.int32, (rows, rows), 0) < lax.broadcasted_iota(jnp.int32, (rows, rows), 1)
        rank = jnp.dot(match.astype(BF), jnp.where(before, 1.0, 0.0).astype(BF), preferred_element_type=F32)
        code = jnp.where(match > 0.5, rank, -1.0)
        slot = lax.broadcasted_iota(jnp.int32, (SLOTS, rows), 0).astype(F32)
        for e in range(experts):
            onehot[e * SLOTS : (e + 1) * SLOTS] = jnp.where(code[e : e + 1, :] == slot, 1.0, 0.0).astype(BF)

    @pl.loop(0, 4)
    def _(i):
        part = pl.ds(pl.multiple_of(i * 256, 256), 256)
        out[part] = jnp.dot(onehot[part], tokens[...], preferred_element_type=F32).astype(BF)


def dispatch(routes, tokens):
    rows, width = tokens.shape
    step = 512
    return pl.pallas_call(
        dispatch_kernel,
        out_shape=jax.ShapeDtypeStruct((32 * SLOTS, width), BF),
        grid=(width // step,),
        in_specs=[
            pl.BlockSpec((6, rows), lambda j: (0, 0)),
            pl.BlockSpec((rows, step), lambda j: (0, j)),
        ],
        out_specs=pl.BlockSpec((32 * SLOTS, step), lambda j: (0, j)),
        scratch_shapes=[pltpu.VMEM((32 * SLOTS, rows), BF)],
        compiler_params=params(62),
        cost_estimate=cost(1 << 29, 5 << 20),
    )(routes, tokens)


def mixing_kernel(place, table, out, match, gain):
    z, me = place[0], place[1]
    for s in range(8):
        block = table[lax.rem(z + 8 - s, 8)].astype(F32)
        routes = block[0:6, 0:128]
        gains = block[0:6, 128:256] + block[0:6, 256:384] + block[0:6, 384:512]
        for k in range(4):
            hit = routes == (4 * z + lax.bitwise_xor(me, k)).astype(F32)
            row = slice(4 * s + k, 4 * s + k + 1)
            match[row] = jnp.sum(jnp.where(hit, 1.0, 0.0), axis=0, keepdims=True)
            gain[row] = jnp.sum(jnp.where(hit, gains, 0.0), axis=0, keepdims=True)
    chosen = match[...]
    before = lax.broadcasted_iota(jnp.int32, (128, 128), 0) < lax.broadcasted_iota(jnp.int32, (128, 128), 1)
    rank = jnp.dot(chosen.astype(BF), jnp.where(before, 1.0, 0.0).astype(BF), preferred_element_type=F32)
    match[...] = jnp.where(chosen > 0.5, rank, -1.0)
    slot = lax.broadcasted_iota(jnp.int32, (SLOTS, 128), 0).astype(F32)
    for s in range(8):
        rows = [slice(4 * s + k, 4 * s + k + 1) for k in range(4)]
        weight = jnp.concatenate([jnp.where(match[r] == slot, gain[r], 0.0) for r in rows], axis=0).T
        high = weight.astype(BF)
        out[s, :, 0:128] = high
        out[s, :, 128:256] = (weight - high.astype(F32)).astype(BF)


def mixing(place, table):
    return pl.pallas_call(
        mixing_kernel,
        out_shape=jax.ShapeDtypeStruct((8, 128, 256), BF),
        in_specs=[SMEM, VMEM],
        out_specs=VMEM,
        scratch_shapes=[pltpu.VMEM((32, 128), F32), pltpu.VMEM((32, 128), F32)],
        compiler_params=params(8),
        cost_estimate=cost(1 << 22, 1 << 20),
    )(place, table)


def expert_kernel(groups, place, offsets, *refs):
    arrived, gates, ups, downs = refs[0], refs[1:7], refs[7:13], refs[13:23]
    outs, (x, hidden, gate, up, down, sems) = refs[23:-6], refs[-6:]
    copies = []

    def copy(src, dst):
        c = pltpu.make_async_copy(src, dst, sems.at[len(copies)])
        c.start()
        copies.append(c)

    spans = [(pl.multiple_of(offsets[0], 1024), 1024)]
    spans += [(pl.multiple_of(offsets[1 + i], 256), 256) for i in range(3)]
    far = pl.multiple_of(offsets[4], 256)
    spans += [(far, 128), (pl.multiple_of(far + 128, 128), 128)]
    tile, marks = 256, []

    def load(j):
        cols = slice(j * tile, (j + 1) * tile)
        for parts, whole in ((gates, gate), (ups, up)):
            for part, (start, size) in zip(parts, spans):
                copy(part.at[:, cols], whole.at[pl.ds(start, size), cols])
        marks.append(len(copies))

    at = 0
    for group in groups:
        for k in range(4):
            for s in group:
                source = 4 * lax.rem(place[0] + 8 - s, 8) + lax.bitwise_xor(place[1], k)
                copy(arrived.at[pl.ds(pl.multiple_of(source * SLOTS, SLOTS), SLOTS)], x.at[at : at + SLOTS])
                at += SLOTS
    tiles = gate.shape[1] // tile
    for j in range(tiles):
        load(j)
    for side in range(2):
        parts = downs[5 * side : 5 * side + 5]
        cols = [pl.ds(pl.multiple_of(offsets[5 - 4 * side + i], 256), 256) for i in range(4)]
        for i in range(3):
            copy(parts[i], down.at[:, cols[i]])
        copy(parts[3], down.at[0:384, cols[3]])
        copy(parts[4], down.at[384:768, cols[3]])
    done = 0
    for j in range(tiles):
        for c in copies[done : marks[j]]:
            c.wait()
        done = marks[j]
        cols = slice(j * tile, (j + 1) * tile)
        g = jnp.dot(x[...], gate[:, cols], preferred_element_type=F32)
        u = jnp.dot(x[...], up[:, cols], preferred_element_type=F32)
        hidden[:, cols] = (g / (1.0 + jnp.exp(-g)) * u).astype(BF)
    for c in copies[done:]:
        c.wait()

    @pl.loop(0, down.shape[1] // 256)
    def _(j):
        cols = pl.ds(pl.multiple_of(j * 256, 256), 256)
        answer = jnp.dot(hidden[...], down[:, cols], preferred_element_type=F32).astype(BF)
        at = 0
        for i, group in enumerate(groups):
            for k in range(4):
                size = len(group) * SLOTS
                outs[4 * i + k][:, cols] = answer[at : at + size]
                at += size


def expert(groups, place, offsets, arrived, gates, ups, downs):
    width, units = arrived.shape[1], gates[0].shape[1]
    shapes = [jax.ShapeDtypeStruct((len(g) * SLOTS, width), BF) for g in groups for _ in range(4)]
    rows = sum(x.shape[0] for x in shapes)
    out = pl.pallas_call(
        functools.partial(expert_kernel, groups),
        out_shape=tuple(shapes),
        in_specs=[SMEM, SMEM] + [ANY] * 23,
        out_specs=(VMEM,) * len(shapes),
        scratch_shapes=[
            pltpu.VMEM((rows, width), BF),
            pltpu.VMEM((rows, units), BF),
            pltpu.VMEM((width, units), BF),
            pltpu.VMEM((width, units), BF),
            pltpu.VMEM((units, width), BF),
            pltpu.SemaphoreType.DMA((46 + rows // SLOTS,)),
        ],
        compiler_params=params(62),
        cost_estimate=cost(6 * rows * width * units, 16 << 20),
    )(place, offsets, arrived, *gates, *ups, *downs)
    return [out[4 * i : 4 * i + 4] for i in range(len(groups))]


def combined(weight, answers):
    rows = jnp.concatenate(list(answers) * 2, axis=0)
    return jnp.dot(weight, rows, preferred_element_type=F32)


def combine_kernel(blocks, n_in, *refs):
    weights, refs = refs[: len(blocks)], refs[len(blocks) :]
    answers, arrived, outs = refs[:4], refs[4 : 4 + n_in], refs[4 + n_in :]
    for i, s in enumerate(blocks):
        rows = slice(i * SLOTS, (i + 1) * SLOTS)
        total = combined(weights[i][...], [a[rows] for a in answers])
        if s == 4:
            outs[0][...] = total[0:64].astype(BF)
            outs[1][...] = total[64:128].astype(BF)
        elif s == 3:
            outs[i][0:64] = (total[0:64] + arrived[i][...].astype(F32)).astype(BF)
            outs[i][64:128] = total[64:128].astype(BF)
        elif s == 5:
            outs[i][0:64] = total[0:64].astype(BF)
            outs[i][64:128] = (total[64:128] + arrived[i][...].astype(F32)).astype(BF)
        else:
            outs[i][...] = (total + arrived[i][...].astype(F32)).astype(BF)


def weight_of(s):
    return pl.BlockSpec((None, 128, 256), lambda *_: (s, 0, 0))


def combine(blocks, weights, answers, arrived):
    width, step = answers[0].shape[1], 1024
    height = 64 if blocks == (4,) else 128
    used = len(blocks) * SLOTS
    return pl.pallas_call(
        functools.partial(combine_kernel, blocks, len(arrived)),
        out_shape=(jax.ShapeDtypeStruct((height, width), BF),) * 2,
        grid=(width // step,),
        in_specs=[weight_of(s) for s in blocks]
        + [pl.BlockSpec((used, step), lambda j: (0, j))] * 4
        + [pl.BlockSpec((x.shape[0], step), lambda j: (0, j)) for x in arrived],
        out_specs=(pl.BlockSpec((height, step), lambda j: (0, j)),) * 2,
        compiler_params=params(8),
        cost_estimate=cost(len(blocks) << 27, 2 << 20),
    )(*[weights] * len(blocks), *answers, *arrived)


def final_kernel(offsets, weight, a0, a1, a2, a3, tokens, left, right, norm, q0, q1, mixed, query, total, normed, held, sems):
    copies = [pltpu.make_async_copy(q, held.at[i], sems.at[i]) for i, q in enumerate((q0, q1))]
    for c in copies:
        c.start()
    width, step = tokens.shape[1], 512
    square = jnp.zeros((128, 1), F32)
    start = 2 * SLOTS
    for j in range(width // step):
        cols = slice(j * step, (j + 1) * step)
        part = combined(weight[...], [a[start : start + SLOTS, cols] for a in (a0, a1, a2, a3)])
        part = part + tokens[:, cols].astype(F32)
        part = part + left[:, cols].astype(F32) + right[:, cols].astype(F32)
        mixed[:, cols] = part.astype(BF)
        total[:, cols] = part
        square = square + jnp.sum(part * part, axis=1, keepdims=True)
    scale = lax.rsqrt(square / width + 1e-06)
    for j in range(width // step):
        cols = slice(j * step, (j + 1) * step)
        normed[:, cols] = (total[:, cols] * scale * norm[:, cols]).astype(BF)
    for c in copies:
        c.wait()
    half = width // 2
    sides = [normed[:, pl.ds(pl.multiple_of(offsets[i], half), half)] for i in range(2)]
    dims = (((1,), (1,)), ((), ()))

    @pl.loop(0, query.shape[1] // 256)
    def _(j):
        cols = pl.ds(pl.multiple_of(j * 256, 256), 256)
        out = lax.dot_general(sides[0], held[0, cols], dims, preferred_element_type=F32)
        out = out + lax.dot_general(sides[1], held[1, cols], dims, preferred_element_type=F32)
        query[:, cols] = out.astype(BF)


def final(offsets, weights, answers, tokens, left, right, norm, q0, q1):
    rows, width = tokens.shape
    features = q0.shape[0]

    def whole(x):
        return pl.BlockSpec(x.shape, lambda i: (0, 0))

    return pl.pallas_call(
        final_kernel,
        out_shape=(jax.ShapeDtypeStruct((rows, width), BF), jax.ShapeDtypeStruct((rows, features), BF)),
        grid=(1,),
        in_specs=[SMEM, weight_of(0)] + [whole(x) for x in (*answers, tokens, left, right, norm)] + [ANY] * 2,
        out_specs=(pl.BlockSpec((rows, width), lambda i: (0, 0)), pl.BlockSpec((rows, features), lambda i: (0, 0))),
        scratch_shapes=[
            pltpu.VMEM((rows, width), F32),
            pltpu.VMEM((rows, width), BF),
            pltpu.VMEM((2, features, width // 2), BF),
            pltpu.SemaphoreType.DMA((2,)),
        ],
        compiler_params=params(62),
        cost_estimate=cost(2 * rows * width * features, 8 << 20),
    )(offsets, weights, *answers, tokens, left, right, norm, q0, q1)


def along_y(x):
    up, down = shift(x, "y", 1), shift(x, "y", -1)
    half = x.shape[0] // 2
    return [x, up, down, shift(up[:half], "y", 1), shift(down[half:], "y", -1)]


def across_x(x):
    return along_y(swap(x, "xl", 1))


def shards(tokens, routes, route_gain, gate_weight, up_weight, down_weight, norm_gain, query_weight):
    xl, y, z, c = (lax.axis_index(a) for a in ("xl", "y", "z", "c"))
    me = 2 * lax.axis_index("xh") + c
    plane = ("xh", "c")
    across = [1024 * (1 - xl) + 256 * lax.rem(y + d, 4) for d in (0, 3, 1, 2)]
    around = [1024 * xl + 256 * lax.rem(y + d, 4) for d in (0, 3, 1, 2)]
    offsets = jnp.stack([1024 * xl] + across + around).astype(jnp.int32)
    place = jnp.stack([z, me]).astype(jnp.int32)
    hold = lax.optimization_barrier

    outbound = dispatch(routes.T, tokens)
    arrived = lax.all_to_all(outbound, ("z", "xh", "c"), split_axis=0, concat_axis=0, tiled=True)

    gates = [lax.all_gather(gate_weight[0], "y", axis=0, tiled=True)] + across_x(gate_weight[0])
    ups = [lax.all_gather(up_weight[0], "y", axis=0, tiled=True)] + across_x(up_weight[0])
    downs = along_y(down_weight[0]) + across_x(down_weight[0])
    high = lax.reduce_precision(route_gain.T, 8, 7)
    middle = lax.reduce_precision(route_gain.T - high, 8, 7)
    table = jnp.concatenate([routes.T.astype(F32), high, middle, route_gain.T - high - middle], axis=1).astype(BF)
    table = jnp.pad(table, ((0, ROWS - 6), (0, 512)))
    table, arrived, gates, ups, downs = hold((table, arrived, gates, ups, downs))
    tables = lax.all_gather(table, "z")

    half = query_weight.shape[0] // 2
    share = lax.dynamic_slice(query_weight.T, (0, c * half), (query_weight.shape[1], half))
    q_own = lax.all_gather(share, ("xl", "y"), axis=0, tiled=True)

    def exchange(pieces):
        return tuple(swap(pieces[k], plane, k) for k in (1, 2, 3))

    ans4, ans3 = expert(GROUPS[:2], place, offsets, arrived, gates, ups, downs)
    got4 = exchange(ans4)
    late, _ = hold((place, ans4[0]))
    weights = mixing(late, tables)
    ans2, ans1 = expert(GROUPS[2:], place, offsets, arrived, gates, ups, downs)
    got4, ans3, ans2, ans1, q_own = hold((got4, ans3, ans2, ans1, q_own))
    low, high = combine((4,), weights, (ans4[0],) + got4, [])
    low, high, got3 = shift(low, "z", -1), shift(high, "z", 1), exchange(ans3)
    low, high, got3, ans2 = hold((low, high, got3, ans2))
    low, high = combine((3, 5), weights, (ans3[0],) + got3, [low, high])
    low, high, got2 = shift(low, "z", -1), shift(high, "z", 1), exchange(ans2)
    low, high, got2, ans1 = hold((low, high, got2, ans1))
    low, high = combine((2, 6), weights, (ans2[0],) + got2, [low, high])
    low, high, got1 = shift(low, "z", -1), shift(high, "z", 1), exchange(ans1)
    q_other = swap(q_own, "c", 1)
    low, high, got1, q_other = hold((low, high, got1, q_other))
    got1 = (ans1[0],) + got1
    low, high = combine((1, 7), weights, got1, [low, high])
    low, high = shift(low, "z", -1), shift(high, "z", 1)
    sides = (half * jnp.stack([c, 1 - c])).astype(jnp.int32)
    return final(sides, weights, got1, tokens, low, high, norm_gain[None, :], q_own, q_other)


def solution(mesh):
    fine = Mesh(mesh.devices.reshape(2, 4, 8, 2, 2), ("xl", "y", "z", "xh", "c"))
    grp, ep = ("xl", "y"), ("z", "xh", "c")
    placed = (
        P(grp + ep, None),
        P(grp + ep, None),
        P(grp + ep, None),
        P(ep, grp, None),
        P(ep, grp, None),
        P(ep, None, grp),
        P(),
        P(None, grp),
    )
    return jax.shard_map(
        shards,
        mesh=fine,
        in_specs=placed,
        out_specs=(P(grp + ep, None), P(grp + ep, None)),
        check_vma=False,
    )
```

```python
import functools

import jax
import jax.numpy as jnp
from jax import lax
from jax.experimental import pallas as pl
from jax.experimental.pallas import tpu as pltpu
from jax.sharding import Mesh, PartitionSpec as P

BF = jnp.bfloat16
F32 = jnp.float32
SLOTS = 32
ANY = pl.BlockSpec(memory_space=pltpu.HBM)
SMEM = pl.BlockSpec(memory_space=pltpu.SMEM)
VMEM = pl.BlockSpec(memory_space=pltpu.VMEM)
GROUPS = ((4,), (3, 5), (2, 6), (1, 7), (0,))


def params(mib):
    return pltpu.CompilerParams(vmem_limit_bytes=mib << 20)


def cost(flops, size):
    return pl.CostEstimate(flops=flops, bytes_accessed=size, transcendentals=0)


def shift(x, axis, by):
    n = lax.axis_size(axis)
    return lax.ppermute(x, axis, [(i, (i + by) % n) for i in range(n)])


def swap(x, axes, k):
    n = lax.axis_size(axes)
    return lax.ppermute(x, axes, [(i, i ^ k) for i in range(n)])


def dispatch_kernel(routes, gains, tokens, out, table, onehot):
    experts, rows = 32, tokens.shape[0]

    @pl.when(pl.program_id(0) == 0)
    def _():
        expert = lax.broadcasted_iota(jnp.int32, (experts, rows), 0)
        match = jnp.zeros((experts, rows), F32)
        gain = jnp.zeros((experts, rows), F32)
        for j in range(6):
            hit = routes[j : j + 1, :] == expert
            match = match + jnp.where(hit, 1.0, 0.0)
            gain = gain + jnp.where(hit, gains[j : j + 1, :], 0.0)
        before = lax.broadcasted_iota(jnp.int32, (rows, rows), 0) < lax.broadcasted_iota(jnp.int32, (rows, rows), 1)
        rank = jnp.dot(match.astype(BF), jnp.where(before, 1.0, 0.0).astype(BF), preferred_element_type=F32)
        code = jnp.where(match > 0.5, rank, -1.0)
        for d in range(experts // 4):
            own = slice(4 * d, 4 * d + 4)
            table[8 * d : 8 * d + 4] = code[own]
            table[8 * d + 4 : 8 * d + 8] = gain[own]
        slot = lax.broadcasted_iota(jnp.int32, (SLOTS, rows), 0).astype(F32)
        for e in range(experts):
            onehot[e * SLOTS : (e + 1) * SLOTS] = jnp.where(code[e : e + 1, :] == slot, 1.0, 0.0).astype(BF)

    @pl.loop(0, 4)
    def _(i):
        part = pl.ds(pl.multiple_of(i * 256, 256), 256)
        out[part] = jnp.dot(onehot[part], tokens[...], preferred_element_type=F32).astype(BF)


def dispatch(routes, gains, tokens):
    rows, width = tokens.shape
    step = 512
    return pl.pallas_call(
        dispatch_kernel,
        out_shape=(jax.ShapeDtypeStruct((32 * SLOTS, width), BF), jax.ShapeDtypeStruct((64, rows), F32)),
        grid=(width // step,),
        in_specs=[
            pl.BlockSpec((6, rows), lambda j: (0, 0)),
            pl.BlockSpec((6, rows), lambda j: (0, 0)),
            pl.BlockSpec((rows, step), lambda j: (0, j)),
        ],
        out_specs=(pl.BlockSpec((32 * SLOTS, step), lambda j: (0, j)), pl.BlockSpec((64, rows), lambda j: (0, 0))),
        scratch_shapes=[pltpu.VMEM((32 * SLOTS, rows), BF)],
        compiler_params=params(62),
        cost_estimate=cost(1 << 29, 5 << 20),
    )(routes, gains, tokens)


def mixing_kernel(place, table, out):
    slot = lax.broadcasted_iota(jnp.int32, (SLOTS, 128), 0).astype(F32)
    for s in range(8):
        source = lax.rem(place[0] + 8 - s, 8)
        parts = []
        for k in range(4):
            row = 8 * source + lax.bitwise_xor(place[1], k)
            code, gain = table[pl.ds(row, 1), :], table[pl.ds(row + 4, 1), :]
            parts.append(jnp.where(code == slot, gain, 0.0))
        weight = jnp.concatenate(parts, axis=0).T
        high = weight.astype(BF)
        out[s, :, 0:128] = high
        out[s, :, 128:256] = (weight - high.astype(F32)).astype(BF)


def mixing(place, table):
    return pl.pallas_call(
        mixing_kernel,
        out_shape=jax.ShapeDtypeStruct((8, 128, 256), BF),
        in_specs=[SMEM, VMEM],
        out_specs=VMEM,
        compiler_params=params(8),
        cost_estimate=cost(1 << 22, 1 << 20),
    )(place, table)


def expert_kernel(groups, place, offsets, *refs):
    arrived, gates, ups, downs = refs[0], refs[1:7], refs[7:13], refs[13:19]
    outs, (x, hidden, gate, up, down, sems) = refs[19:-6], refs[-6:]
    copies = []

    def copy(src, dst):
        c = pltpu.make_async_copy(src, dst, sems.at[len(copies)])
        c.start()
        copies.append(c)

    for parts, whole in ((gates, gate), (ups, up)):
        copy(parts[0], whole.at[pl.ds(pl.multiple_of(offsets[0], 1024), 1024)])
        for i in range(3):
            copy(parts[1 + i], whole.at[pl.ds(pl.multiple_of(offsets[1 + i], 256), 256)])
        far = pl.multiple_of(offsets[4], 256)
        copy(parts[4], whole.at[pl.ds(far, 128)])
        copy(parts[5], whole.at[pl.ds(pl.multiple_of(far + 128, 128), 128)])
    at = 0
    for group in groups:
        for k in range(4):
            for s in group:
                source = 4 * lax.rem(place[0] + 8 - s, 8) + lax.bitwise_xor(place[1], k)
                copy(arrived.at[pl.ds(pl.multiple_of(source * SLOTS, SLOTS), SLOTS)], x.at[at : at + SLOTS])
                at += SLOTS
    first = len(copies)
    copy(downs[0], down.at[:, pl.ds(pl.multiple_of(offsets[0], 1024), 1024)])
    for i in range(3):
        copy(downs[1 + i], down.at[:, pl.ds(pl.multiple_of(offsets[1 + i], 256), 256)])
    far = pl.ds(pl.multiple_of(offsets[4], 256), 256)
    copy(downs[4], down.at[0:384, far])
    copy(downs[5], down.at[384:768, far])
    for c in copies[:first]:
        c.wait()

    @pl.loop(0, gate.shape[1] // 256)
    def _(j):
        cols = pl.ds(pl.multiple_of(j * 256, 256), 256)
        g = jnp.dot(x[...], gate[:, cols], preferred_element_type=F32)
        u = jnp.dot(x[...], up[:, cols], preferred_element_type=F32)
        hidden[:, cols] = (g / (1.0 + jnp.exp(-g)) * u).astype(BF)

    for c in copies[first:]:
        c.wait()

    @pl.loop(0, down.shape[1] // 256)
    def _(j):
        cols = pl.ds(pl.multiple_of(j * 256, 256), 256)
        answer = jnp.dot(hidden[...], down[:, cols], preferred_element_type=F32).astype(BF)
        at = 0
        for i, group in enumerate(groups):
            for k in range(4):
                size = len(group) * SLOTS
                outs[4 * i + k][:, cols] = answer[at : at + size]
                at += size


def expert(groups, place, offsets, arrived, gates, ups, downs):
    width, units = arrived.shape[1], gates[0].shape[1]
    shapes = [jax.ShapeDtypeStruct((len(g) * SLOTS, width), BF) for g in groups for _ in range(4)]
    rows = sum(x.shape[0] for x in shapes)
    out = pl.pallas_call(
        functools.partial(expert_kernel, groups),
        out_shape=tuple(shapes),
        in_specs=[SMEM, SMEM] + [ANY] * 19,
        out_specs=(VMEM,) * len(shapes),
        scratch_shapes=[
            pltpu.VMEM((rows, width), BF),
            pltpu.VMEM((rows, units), BF),
            pltpu.VMEM((width, units), BF),
            pltpu.VMEM((width, units), BF),
            pltpu.VMEM((units, width), BF),
            pltpu.SemaphoreType.DMA((18 + rows // SLOTS,)),
        ],
        compiler_params=params(62),
        cost_estimate=cost(6 * rows * width * units, 16 << 20),
    )(place, offsets, arrived, *gates, *ups, *downs)
    return [out[4 * i : 4 * i + 4] for i in range(len(groups))]


def combined(weight, answers):
    rows = jnp.concatenate(list(answers) * 2, axis=0)
    return jnp.dot(weight, rows, preferred_element_type=F32)


def combine_kernel(blocks, n_in, *refs):
    weights, refs = refs[: len(blocks)], refs[len(blocks) :]
    answers, arrived, outs = refs[:4], refs[4 : 4 + n_in], refs[4 + n_in :]
    for i, s in enumerate(blocks):
        rows = slice(i * SLOTS, (i + 1) * SLOTS)
        total = combined(weights[i][...], [a[rows] for a in answers])
        if s == 4:
            outs[0][...] = total[0:64].astype(BF)
            outs[1][...] = total[64:128].astype(BF)
        elif s == 3:
            outs[i][0:64] = (total[0:64] + arrived[i][...].astype(F32)).astype(BF)
            outs[i][64:128] = total[64:128].astype(BF)
        elif s == 5:
            outs[i][0:64] = total[0:64].astype(BF)
            outs[i][64:128] = (total[64:128] + arrived[i][...].astype(F32)).astype(BF)
        else:
            outs[i][...] = (total + arrived[i][...].astype(F32)).astype(BF)


def weight_of(s):
    return pl.BlockSpec((None, 128, 256), lambda *_: (s, 0, 0))


def combine(blocks, weights, answers, arrived):
    width, step = answers[0].shape[1], 1024
    height = 64 if blocks == (4,) else 128
    used = len(blocks) * SLOTS
    return pl.pallas_call(
        functools.partial(combine_kernel, blocks, len(arrived)),
        out_shape=(jax.ShapeDtypeStruct((height, width), BF),) * 2,
        grid=(width // step,),
        in_specs=[weight_of(s) for s in blocks]
        + [pl.BlockSpec((used, step), lambda j: (0, j))] * 4
        + [pl.BlockSpec((x.shape[0], step), lambda j: (0, j)) for x in arrived],
        out_specs=(pl.BlockSpec((height, step), lambda j: (0, j)),) * 2,
        compiler_params=params(8),
        cost_estimate=cost(len(blocks) << 27, 2 << 20),
    )(*[weights] * len(blocks), *answers, *arrived)


def final_kernel(offsets, weight, a0, a1, a2, a3, tokens, left, right, norm, q0, q1, mixed, query, total, normed, held, sems):
    copies = [pltpu.make_async_copy(q, held.at[i], sems.at[i]) for i, q in enumerate((q0, q1))]
    for c in copies:
        c.start()
    width, step = tokens.shape[1], 512
    square = jnp.zeros((128, 1), F32)
    for j in range(width // step):
        cols = slice(j * step, (j + 1) * step)
        part = combined(weight[...], [a[:, cols] for a in (a0, a1, a2, a3)])
        part = part + tokens[:, cols].astype(F32)
        part = part + left[:, cols].astype(F32) + right[:, cols].astype(F32)
        mixed[:, cols] = part.astype(BF)
        total[:, cols] = part
        square = square + jnp.sum(part * part, axis=1, keepdims=True)
    scale = lax.rsqrt(square / width + 1e-06)
    for j in range(width // step):
        cols = slice(j * step, (j + 1) * step)
        normed[:, cols] = (total[:, cols] * scale * norm[:, cols]).astype(BF)
    for c in copies:
        c.wait()
    half = width // 2
    sides = [normed[:, pl.ds(pl.multiple_of(offsets[i], half), half)] for i in range(2)]
    dims = (((1,), (1,)), ((), ()))

    @pl.loop(0, query.shape[1] // 256)
    def _(j):
        cols = pl.ds(pl.multiple_of(j * 256, 256), 256)
        out = lax.dot_general(sides[0], held[0, cols], dims, preferred_element_type=F32)
        out = out + lax.dot_general(sides[1], held[1, cols], dims, preferred_element_type=F32)
        query[:, cols] = out.astype(BF)


def final(offsets, weights, answers, tokens, left, right, norm, q0, q1):
    rows, width = tokens.shape
    features = q0.shape[0]

    def whole(x):
        return pl.BlockSpec(x.shape, lambda i: (0, 0))

    return pl.pallas_call(
        final_kernel,
        out_shape=(jax.ShapeDtypeStruct((rows, width), BF), jax.ShapeDtypeStruct((rows, features), BF)),
        grid=(1,),
        in_specs=[SMEM, weight_of(0)] + [whole(x) for x in (*answers, tokens, left, right, norm)] + [ANY] * 2,
        out_specs=(pl.BlockSpec((rows, width), lambda i: (0, 0)), pl.BlockSpec((rows, features), lambda i: (0, 0))),
        scratch_shapes=[
            pltpu.VMEM((rows, width), F32),
            pltpu.VMEM((rows, width), BF),
            pltpu.VMEM((2, features, width // 2), BF),
            pltpu.SemaphoreType.DMA((2,)),
        ],
        compiler_params=params(62),
        cost_estimate=cost(2 * rows * width * features, 8 << 20),
    )(offsets, weights, *answers, tokens, left, right, norm, q0, q1)


def across_x(x):
    other = swap(x, "xl", 1)
    up, down = shift(other, "y", 1), shift(other, "y", -1)
    half = x.shape[0] // 2
    return [other, up, down, shift(up[:half], "y", 1), shift(down[half:], "y", -1)]


def shards(tokens, routes, route_gain, gate_weight, up_weight, down_weight, norm_gain, query_weight):
    xl, y, z, c = (lax.axis_index(a) for a in ("xl", "y", "z", "c"))
    me = 2 * lax.axis_index("xh") + c
    plane = ("xh", "c")
    across = [1024 * (1 - xl) + 256 * lax.rem(y + d, 4) for d in (0, 3, 1, 2)]
    offsets = jnp.stack([1024 * xl] + across).astype(jnp.int32)
    place = jnp.stack([z, me]).astype(jnp.int32)
    hold = lax.optimization_barrier

    outbound, table = dispatch(routes.T, route_gain.T, tokens)
    arrived = lax.all_to_all(outbound, ("z", "xh", "c"), split_axis=0, concat_axis=0, tiled=True)

    gates = [lax.all_gather(gate_weight[0], "y", axis=0, tiled=True)] + across_x(gate_weight[0])
    ups = [lax.all_gather(up_weight[0], "y", axis=0, tiled=True)] + across_x(up_weight[0])
    downs = [lax.all_gather(down_weight[0], "y", axis=1, tiled=True)] + across_x(down_weight[0])
    tables = lax.all_to_all(table, "z", split_axis=0, concat_axis=0, tiled=True)
    weights = mixing(place, tables)

    half = query_weight.shape[0] // 2
    share = lax.dynamic_slice(query_weight.T, (0, c * half), (query_weight.shape[1], half))
    q_own = lax.all_gather(share, ("xl", "y"), axis=0, tiled=True)

    def exchange(pieces):
        return tuple(swap(pieces[k], plane, k) for k in (1, 2, 3))

    ans4, ans3 = expert(GROUPS[:2], place, offsets, arrived, gates, ups, downs)
    got4, got3 = exchange(ans4), exchange(ans3)
    ans2, ans1, ans0 = expert(GROUPS[2:], place, offsets, arrived, gates, ups, downs)
    got4, ans2, ans1, ans0 = hold((got4, ans2, ans1, ans0))
    low, high = combine((4,), weights, (ans4[0],) + got4, [])
    low, high, got0 = shift(low, "z", -1), shift(high, "z", 1), exchange(ans0)
    low, high, got3, got0, ans2 = hold((low, high, got3, got0, ans2))
    low, high = combine((3, 5), weights, (ans3[0],) + got3, [low, high])
    low, high, got2 = shift(low, "z", -1), shift(high, "z", 1), exchange(ans2)
    low, high, got2, ans1, q_own = hold((low, high, got2, ans1, q_own))
    low, high = combine((2, 6), weights, (ans2[0],) + got2, [low, high])
    q_other = swap(q_own, "c", 1)
    low, high, got1 = shift(low, "z", -1), shift(high, "z", 1), exchange(ans1)
    low, high, got1, q_other = hold((low, high, got1, q_other))
    low, high = combine((1, 7), weights, (ans1[0],) + got1, [low, high])
    low, high = shift(low, "z", -1), shift(high, "z", 1)
    got0 = (ans0[0],) + got0
    sides = (half * jnp.stack([c, 1 - c])).astype(jnp.int32)
    return final(sides, weights, got0, tokens, low, high, norm_gain[None, :], q_own, q_other)


def solution(mesh):
    fine = Mesh(mesh.devices.reshape(2, 4, 8, 2, 2), ("xl", "y", "z", "xh", "c"))
    grp, ep = ("xl", "y"), ("z", "xh", "c")
    placed = (
        P(grp + ep, None),
        P(grp + ep, None),
        P(grp + ep, None),
        P(ep, grp, None),
        P(ep, grp, None),
        P(ep, None, grp),
        P(),
        P(None, grp),
    )
    return jax.shard_map(
        shards,
        mesh=fine,
        in_specs=placed,
        out_specs=(P(grp + ep, None), P(grp + ep, None)),
        check_vma=False,
    )
```

```python
import functools

import jax
import jax.numpy as jnp
from jax import lax
from jax.experimental import pallas as pl
from jax.experimental.pallas import tpu as pltpu
from jax.sharding import Mesh, PartitionSpec as P

BF = jnp.bfloat16
F32 = jnp.float32
SLOTS = 32
ANY = pl.BlockSpec(memory_space=pltpu.HBM)
SMEM = pl.BlockSpec(memory_space=pltpu.SMEM)
VMEM = pl.BlockSpec(memory_space=pltpu.VMEM)
GROUPS = ((4,), (3, 5), (2, 6), (1, 7), (0,))


def params(mib):
    return pltpu.CompilerParams(vmem_limit_bytes=mib << 20)


def cost(flops, size):
    return pl.CostEstimate(flops=flops, bytes_accessed=size, transcendentals=0)


def shift(x, axis, by):
    n = lax.axis_size(axis)
    return lax.ppermute(x, axis, [(i, (i + by) % n) for i in range(n)])


def swap(x, axes, k):
    n = lax.axis_size(axes)
    return lax.ppermute(x, axes, [(i, i ^ k) for i in range(n)])


def dispatch_kernel(routes, gains, tokens, out, table, onehot):
    experts, rows = 32, tokens.shape[0]

    @pl.when(pl.program_id(0) == 0)
    def _():
        expert = lax.broadcasted_iota(jnp.int32, (experts, rows), 0)
        match = jnp.zeros((experts, rows), F32)
        gain = jnp.zeros((experts, rows), F32)
        for j in range(6):
            hit = routes[j : j + 1, :] == expert
            match = match + jnp.where(hit, 1.0, 0.0)
            gain = gain + jnp.where(hit, gains[j : j + 1, :], 0.0)
        before = lax.broadcasted_iota(jnp.int32, (rows, rows), 0) < lax.broadcasted_iota(jnp.int32, (rows, rows), 1)
        rank = jnp.dot(match.astype(BF), jnp.where(before, 1.0, 0.0).astype(BF), preferred_element_type=F32)
        code = jnp.where(match > 0.5, rank, -1.0)
        for d in range(experts // 4):
            own = slice(4 * d, 4 * d + 4)
            table[8 * d : 8 * d + 4] = code[own]
            table[8 * d + 4 : 8 * d + 8] = gain[own]
        slot = lax.broadcasted_iota(jnp.int32, (SLOTS, rows), 0).astype(F32)
        for e in range(experts):
            onehot[e * SLOTS : (e + 1) * SLOTS] = jnp.where(code[e : e + 1, :] == slot, 1.0, 0.0).astype(BF)

    @pl.loop(0, 4)
    def _(i):
        part = pl.ds(pl.multiple_of(i * 256, 256), 256)
        out[part] = jnp.dot(onehot[part], tokens[...], preferred_element_type=F32).astype(BF)


def dispatch(routes, gains, tokens):
    rows, width = tokens.shape
    step = 512
    return pl.pallas_call(
        dispatch_kernel,
        out_shape=(jax.ShapeDtypeStruct((32 * SLOTS, width), BF), jax.ShapeDtypeStruct((64, rows), F32)),
        grid=(width // step,),
        in_specs=[
            pl.BlockSpec((6, rows), lambda j: (0, 0)),
            pl.BlockSpec((6, rows), lambda j: (0, 0)),
            pl.BlockSpec((rows, step), lambda j: (0, j)),
        ],
        out_specs=(pl.BlockSpec((32 * SLOTS, step), lambda j: (0, j)), pl.BlockSpec((64, rows), lambda j: (0, 0))),
        scratch_shapes=[pltpu.VMEM((32 * SLOTS, rows), BF)],
        compiler_params=params(62),
        cost_estimate=cost(1 << 29, 5 << 20),
    )(routes, gains, tokens)


def mixing_kernel(place, table, out):
    slot = lax.broadcasted_iota(jnp.int32, (SLOTS, 128), 0).astype(F32)
    for s in range(8):
        source = lax.rem(place[0] + 8 - s, 8)
        parts = []
        for k in range(4):
            row = 8 * source + lax.bitwise_xor(place[1], k)
            code, gain = table[pl.ds(row, 1), :], table[pl.ds(row + 4, 1), :]
            parts.append(jnp.where(code == slot, gain, 0.0))
        weight = jnp.concatenate(parts, axis=0).T
        high = weight.astype(BF)
        out[s, :, 0:128] = high
        out[s, :, 128:256] = (weight - high.astype(F32)).astype(BF)


def mixing(place, table):
    return pl.pallas_call(
        mixing_kernel,
        out_shape=jax.ShapeDtypeStruct((8, 128, 256), BF),
        in_specs=[SMEM, VMEM],
        out_specs=VMEM,
        compiler_params=params(8),
        cost_estimate=cost(1 << 22, 1 << 20),
    )(place, table)


def expert_kernel(groups, place, offsets, *refs):
    arrived, gates, ups, downs = refs[0], refs[1:7], refs[7:13], refs[13:19]
    outs, (x, hidden, gate, up, down, sems) = refs[19:-6], refs[-6:]
    copies = []

    def copy(src, dst):
        c = pltpu.make_async_copy(src, dst, sems.at[len(copies)])
        c.start()
        copies.append(c)

    for parts, whole in ((gates, gate), (ups, up)):
        copy(parts[0], whole.at[pl.ds(pl.multiple_of(offsets[0], 1024), 1024)])
        for i in range(3):
            copy(parts[1 + i], whole.at[pl.ds(pl.multiple_of(offsets[1 + i], 256), 256)])
        far = pl.multiple_of(offsets[4], 256)
        copy(parts[4], whole.at[pl.ds(far, 128)])
        copy(parts[5], whole.at[pl.ds(pl.multiple_of(far + 128, 128), 128)])
    at = 0
    for group in groups:
        for k in range(4):
            for s in group:
                source = 4 * lax.rem(place[0] + 8 - s, 8) + lax.bitwise_xor(place[1], k)
                copy(arrived.at[pl.ds(pl.multiple_of(source * SLOTS, SLOTS), SLOTS)], x.at[at : at + SLOTS])
                at += SLOTS
    first = len(copies)
    copy(downs[0], down.at[:, pl.ds(pl.multiple_of(offsets[0], 1024), 1024)])
    for i in range(3):
        copy(downs[1 + i], down.at[:, pl.ds(pl.multiple_of(offsets[1 + i], 256), 256)])
    far = pl.ds(pl.multiple_of(offsets[4], 256), 256)
    copy(downs[4], down.at[0:384, far])
    copy(downs[5], down.at[384:768, far])
    for c in copies[:first]:
        c.wait()

    @pl.loop(0, gate.shape[1] // 256)
    def _(j):
        cols = pl.ds(pl.multiple_of(j * 256, 256), 256)
        g = jnp.dot(x[...], gate[:, cols], preferred_element_type=F32)
        u = jnp.dot(x[...], up[:, cols], preferred_element_type=F32)
        hidden[:, cols] = (g / (1.0 + jnp.exp(-g)) * u).astype(BF)

    for c in copies[first:]:
        c.wait()

    @pl.loop(0, down.shape[1] // 256)
    def _(j):
        cols = pl.ds(pl.multiple_of(j * 256, 256), 256)
        answer = jnp.dot(hidden[...], down[:, cols], preferred_element_type=F32).astype(BF)
        at = 0
        for i, group in enumerate(groups):
            for k in range(4):
                size = len(group) * SLOTS
                outs[4 * i + k][:, cols] = answer[at : at + size]
                at += size


def expert(groups, place, offsets, arrived, gates, ups, downs):
    width, units = arrived.shape[1], gates[0].shape[1]
    shapes = [jax.ShapeDtypeStruct((len(g) * SLOTS, width), BF) for g in groups for _ in range(4)]
    rows = sum(x.shape[0] for x in shapes)
    out = pl.pallas_call(
        functools.partial(expert_kernel, groups),
        out_shape=tuple(shapes),
        in_specs=[SMEM, SMEM] + [ANY] * 19,
        out_specs=(VMEM,) * len(shapes),
        scratch_shapes=[
            pltpu.VMEM((rows, width), BF),
            pltpu.VMEM((rows, units), BF),
            pltpu.VMEM((width, units), BF),
            pltpu.VMEM((width, units), BF),
            pltpu.VMEM((units, width), BF),
            pltpu.SemaphoreType.DMA((18 + rows // SLOTS,)),
        ],
        compiler_params=params(62),
        cost_estimate=cost(6 * rows * width * units, 16 << 20),
    )(place, offsets, arrived, *gates, *ups, *downs)
    return [out[4 * i : 4 * i + 4] for i in range(len(groups))]


def combined(weight, answers):
    rows = jnp.concatenate(list(answers) * 2, axis=0)
    return jnp.dot(weight, rows, preferred_element_type=F32)


def combine_kernel(blocks, n_in, *refs):
    weights, refs = refs[: len(blocks)], refs[len(blocks) :]
    answers, arrived, outs = refs[:4], refs[4 : 4 + n_in], refs[4 + n_in :]
    for i, s in enumerate(blocks):
        rows = slice(i * SLOTS, (i + 1) * SLOTS)
        total = combined(weights[i][...], [a[rows] for a in answers])
        if s == 4:
            outs[0][...] = total[0:64].astype(BF)
            outs[1][...] = total[64:128].astype(BF)
        elif s == 3:
            outs[i][0:64] = (total[0:64] + arrived[i][...].astype(F32)).astype(BF)
            outs[i][64:128] = total[64:128].astype(BF)
        elif s == 5:
            outs[i][0:64] = total[0:64].astype(BF)
            outs[i][64:128] = (total[64:128] + arrived[i][...].astype(F32)).astype(BF)
        else:
            outs[i][...] = (total + arrived[i][...].astype(F32)).astype(BF)


def weight_of(s):
    return pl.BlockSpec((None, 128, 256), lambda *_: (s, 0, 0))


def combine(blocks, weights, answers, arrived):
    width, step = answers[0].shape[1], 1024
    height = 64 if blocks == (4,) else 128
    used = len(blocks) * SLOTS
    return pl.pallas_call(
        functools.partial(combine_kernel, blocks, len(arrived)),
        out_shape=(jax.ShapeDtypeStruct((height, width), BF),) * 2,
        grid=(width // step,),
        in_specs=[weight_of(s) for s in blocks]
        + [pl.BlockSpec((used, step), lambda j: (0, j))] * 4
        + [pl.BlockSpec((x.shape[0], step), lambda j: (0, j)) for x in arrived],
        out_specs=(pl.BlockSpec((height, step), lambda j: (0, j)),) * 2,
        compiler_params=params(8),
        cost_estimate=cost(len(blocks) << 27, 2 << 20),
    )(*[weights] * len(blocks), *answers, *arrived)


def final_kernel(offsets, weight, a0, a1, a2, a3, tokens, left, right, norm, q0, q1, mixed, query, total, normed, held, sems):
    copies = [pltpu.make_async_copy(q, held.at[i], sems.at[i]) for i, q in enumerate((q0, q1))]
    for c in copies:
        c.start()
    width, step = tokens.shape[1], 512
    square = jnp.zeros((128, 1), F32)
    for j in range(width // step):
        cols = slice(j * step, (j + 1) * step)
        part = combined(weight[...], [a[:, cols] for a in (a0, a1, a2, a3)])
        part = part + tokens[:, cols].astype(F32)
        part = part + left[:, cols].astype(F32) + right[:, cols].astype(F32)
        mixed[:, cols] = part.astype(BF)
        total[:, cols] = part
        square = square + jnp.sum(part * part, axis=1, keepdims=True)
    scale = lax.rsqrt(square / width + 1e-06)
    for j in range(width // step):
        cols = slice(j * step, (j + 1) * step)
        normed[:, cols] = (total[:, cols] * scale * norm[:, cols]).astype(BF)
    for c in copies:
        c.wait()
    half = width // 2
    sides = [normed[:, pl.ds(pl.multiple_of(offsets[i], half), half)] for i in range(2)]
    dims = (((1,), (1,)), ((), ()))

    @pl.loop(0, query.shape[1] // 256)
    def _(j):
        cols = pl.ds(pl.multiple_of(j * 256, 256), 256)
        out = lax.dot_general(sides[0], held[0, cols], dims, preferred_element_type=F32)
        out = out + lax.dot_general(sides[1], held[1, cols], dims, preferred_element_type=F32)
        query[:, cols] = out.astype(BF)


def final(offsets, weights, answers, tokens, left, right, norm, q0, q1):
    rows, width = tokens.shape
    features = q0.shape[0]

    def whole(x):
        return pl.BlockSpec(x.shape, lambda i: (0, 0))

    return pl.pallas_call(
        final_kernel,
        out_shape=(jax.ShapeDtypeStruct((rows, width), BF), jax.ShapeDtypeStruct((rows, features), BF)),
        grid=(1,),
        in_specs=[SMEM, weight_of(0)] + [whole(x) for x in (*answers, tokens, left, right, norm)] + [ANY] * 2,
        out_specs=(pl.BlockSpec((rows, width), lambda i: (0, 0)), pl.BlockSpec((rows, features), lambda i: (0, 0))),
        scratch_shapes=[
            pltpu.VMEM((rows, width), F32),
            pltpu.VMEM((rows, width), BF),
            pltpu.VMEM((2, features, width // 2), BF),
            pltpu.SemaphoreType.DMA((2,)),
        ],
        compiler_params=params(62),
        cost_estimate=cost(2 * rows * width * features, 8 << 20),
    )(offsets, weights, *answers, tokens, left, right, norm, q0, q1)


def across_x(x):
    other = swap(x, "xl", 1)
    up, down = shift(other, "y", 1), shift(other, "y", -1)
    half = x.shape[0] // 2
    return [other, up, down, shift(up[:half], "y", 1), shift(down[half:], "y", -1)]


def shards(tokens, routes, route_gain, gate_weight, up_weight, down_weight, norm_gain, query_weight):
    xl, y, z, c = (lax.axis_index(a) for a in ("xl", "y", "z", "c"))
    me = 2 * lax.axis_index("xh") + c
    plane = ("xh", "c")
    across = [1024 * (1 - xl) + 256 * lax.rem(y + d, 4) for d in (0, 3, 1, 2)]
    offsets = jnp.stack([1024 * xl] + across).astype(jnp.int32)
    place = jnp.stack([z, me]).astype(jnp.int32)
    hold = lax.optimization_barrier

    outbound, table = dispatch(routes.T, route_gain.T, tokens)
    tables = lax.all_to_all(table, "z", split_axis=0, concat_axis=0, tiled=True)
    outbound, tables = hold((outbound, tables))
    arrived = lax.all_to_all(outbound, ("z", "xh", "c"), split_axis=0, concat_axis=0, tiled=True)

    gates = [lax.all_gather(gate_weight[0], "y", axis=0, tiled=True)] + across_x(gate_weight[0])
    ups = [lax.all_gather(up_weight[0], "y", axis=0, tiled=True)] + across_x(up_weight[0])
    downs = [lax.all_gather(down_weight[0], "y", axis=1, tiled=True)] + across_x(down_weight[0])
    weights = mixing(place, tables)

    half = query_weight.shape[0] // 2
    share = lax.dynamic_slice(query_weight.T, (0, c * half), (query_weight.shape[1], half))
    q_own = lax.all_gather(share, ("xl", "y"), axis=0, tiled=True)

    def exchange(pieces):
        return tuple(swap(pieces[k], plane, k) for k in (1, 2, 3))

    ans4, ans3 = expert(GROUPS[:2], place, offsets, arrived, gates, ups, downs)
    got4, got3 = exchange(ans4), exchange(ans3)
    ans2, ans1, ans0 = expert(GROUPS[2:], place, offsets, arrived, gates, ups, downs)
    got4, got3, ans2, ans1, ans0 = hold((got4, got3, ans2, ans1, ans0))
    low, high = combine((4,), weights, (ans4[0],) + got4, [])
    low, high, got0 = shift(low, "z", -1), shift(high, "z", 1), exchange(ans0)
    low, high, got0, ans2 = hold((low, high, got0, ans2))
    low, high = combine((3, 5), weights, (ans3[0],) + got3, [low, high])
    low, high, got2 = shift(low, "z", -1), shift(high, "z", 1), exchange(ans2)
    low, high, got2, ans1, q_own = hold((low, high, got2, ans1, q_own))
    low, high = combine((2, 6), weights, (ans2[0],) + got2, [low, high])
    q_other = swap(q_own, "c", 1)
    low, high, got1 = shift(low, "z", -1), shift(high, "z", 1), exchange(ans1)
    low, high, got1, q_other = hold((low, high, got1, q_other))
    low, high = combine((1, 7), weights, (ans1[0],) + got1, [low, high])
    low, high = shift(low, "z", -1), shift(high, "z", 1)
    got0 = (ans0[0],) + got0
    sides = (half * jnp.stack([c, 1 - c])).astype(jnp.int32)
    return final(sides, weights, got0, tokens, low, high, norm_gain[None, :], q_own, q_other)


def solution(mesh):
    fine = Mesh(mesh.devices.reshape(2, 4, 8, 2, 2), ("xl", "y", "z", "xh", "c"))
    grp, ep = ("xl", "y"), ("z", "xh", "c")
    placed = (
        P(grp + ep, None),
        P(grp + ep, None),
        P(grp + ep, None),
        P(ep, grp, None),
        P(ep, grp, None),
        P(ep, None, grp),
        P(),
        P(None, grp),
    )
    return jax.shard_map(
        shards,
        mesh=fine,
        in_specs=placed,
        out_specs=(P(grp + ep, None), P(grp + ep, None)),
        check_vma=False,
    )
```

```python
import functools

import jax
import jax.numpy as jnp
from jax import lax
from jax.experimental import pallas as pl
from jax.experimental.pallas import tpu as pltpu
from jax.sharding import Mesh, PartitionSpec as P

BF = jnp.bfloat16
F32 = jnp.float32
SLOTS = 32
ANY = pl.BlockSpec(memory_space=pltpu.HBM)
SMEM = pl.BlockSpec(memory_space=pltpu.SMEM)
VMEM = pl.BlockSpec(memory_space=pltpu.VMEM)
GROUPS = ((4,), (3, 5), (2, 6), (1, 7), (0,))


def params(mib):
    return pltpu.CompilerParams(vmem_limit_bytes=mib << 20)


def cost(flops, size):
    return pl.CostEstimate(flops=flops, bytes_accessed=size, transcendentals=0)


def shift(x, axis, by):
    n = lax.axis_size(axis)
    return lax.ppermute(x, axis, [(i, (i + by) % n) for i in range(n)])


def swap(x, axes, k):
    n = lax.axis_size(axes)
    return lax.ppermute(x, axes, [(i, i ^ k) for i in range(n)])


def dispatch_kernel(routes, gains, tokens, out, table, onehot):
    experts, rows = 32, tokens.shape[0]

    @pl.when(pl.program_id(0) == 0)
    def _():
        expert = lax.broadcasted_iota(jnp.int32, (experts, rows), 0)
        match = jnp.zeros((experts, rows), F32)
        gain = jnp.zeros((experts, rows), F32)
        for j in range(6):
            hit = routes[j : j + 1, :] == expert
            match = match + jnp.where(hit, 1.0, 0.0)
            gain = gain + jnp.where(hit, gains[j : j + 1, :], 0.0)
        before = lax.broadcasted_iota(jnp.int32, (rows, rows), 0) < lax.broadcasted_iota(jnp.int32, (rows, rows), 1)
        rank = jnp.dot(match.astype(BF), jnp.where(before, 1.0, 0.0).astype(BF), preferred_element_type=F32)
        code = jnp.where(match > 0.5, rank, -1.0)
        for d in range(experts // 4):
            own = slice(4 * d, 4 * d + 4)
            table[8 * d : 8 * d + 4] = code[own]
            table[8 * d + 4 : 8 * d + 8] = gain[own]
        slot = lax.broadcasted_iota(jnp.int32, (SLOTS, rows), 0).astype(F32)
        for e in range(experts):
            onehot[e * SLOTS : (e + 1) * SLOTS] = jnp.where(code[e : e + 1, :] == slot, 1.0, 0.0).astype(BF)

    @pl.loop(0, 4)
    def _(i):
        part = pl.ds(pl.multiple_of(i * 256, 256), 256)
        out[part] = jnp.dot(onehot[part], tokens[...], preferred_element_type=F32).astype(BF)


def dispatch(routes, gains, tokens):
    rows, width = tokens.shape
    step = 512
    return pl.pallas_call(
        dispatch_kernel,
        out_shape=(jax.ShapeDtypeStruct((32 * SLOTS, width), BF), jax.ShapeDtypeStruct((64, rows), F32)),
        grid=(width // step,),
        in_specs=[
            pl.BlockSpec((6, rows), lambda j: (0, 0)),
            pl.BlockSpec((6, rows), lambda j: (0, 0)),
            pl.BlockSpec((rows, step), lambda j: (0, j)),
        ],
        out_specs=(pl.BlockSpec((32 * SLOTS, step), lambda j: (0, j)), pl.BlockSpec((64, rows), lambda j: (0, 0))),
        scratch_shapes=[pltpu.VMEM((32 * SLOTS, rows), BF)],
        compiler_params=params(62),
        cost_estimate=cost(1 << 29, 5 << 20),
    )(routes, gains, tokens)


def mixing_kernel(place, table, out):
    slot = lax.broadcasted_iota(jnp.int32, (SLOTS, 128), 0).astype(F32)
    for s in range(8):
        source = lax.rem(place[0] + 8 - s, 8)
        parts = []
        for k in range(4):
            row = 8 * source + lax.bitwise_xor(place[1], k)
            code, gain = table[pl.ds(row, 1), :], table[pl.ds(row + 4, 1), :]
            parts.append(jnp.where(code == slot, gain, 0.0))
        weight = jnp.concatenate(parts, axis=0).T
        high = weight.astype(BF)
        out[s, :, 0:128] = high
        out[s, :, 128:256] = (weight - high.astype(F32)).astype(BF)


def mixing(place, table):
    return pl.pallas_call(
        mixing_kernel,
        out_shape=jax.ShapeDtypeStruct((8, 128, 256), BF),
        in_specs=[SMEM, VMEM],
        out_specs=VMEM,
        compiler_params=params(8),
        cost_estimate=cost(1 << 22, 1 << 20),
    )(place, table)


def expert_kernel(groups, place, offsets, *refs):
    arrived, gates, ups, downs = refs[0], refs[1:7], refs[7:13], refs[13:19]
    outs, (x, hidden, gate, up, down, sems) = refs[19:-6], refs[-6:]
    copies = []

    def copy(src, dst):
        c = pltpu.make_async_copy(src, dst, sems.at[len(copies)])
        c.start()
        copies.append(c)

    for parts, whole in ((gates, gate), (ups, up)):
        copy(parts[0], whole.at[pl.ds(pl.multiple_of(offsets[0], 1024), 1024)])
        for i in range(3):
            copy(parts[1 + i], whole.at[pl.ds(pl.multiple_of(offsets[1 + i], 256), 256)])
        far = pl.multiple_of(offsets[4], 256)
        copy(parts[4], whole.at[pl.ds(far, 128)])
        copy(parts[5], whole.at[pl.ds(pl.multiple_of(far + 128, 128), 128)])
    at = 0
    for group in groups:
        for k in range(4):
            for s in group:
                source = 4 * lax.rem(place[0] + 8 - s, 8) + lax.bitwise_xor(place[1], k)
                copy(arrived.at[pl.ds(pl.multiple_of(source * SLOTS, SLOTS), SLOTS)], x.at[at : at + SLOTS])
                at += SLOTS
    first = len(copies)
    copy(downs[0], down.at[:, pl.ds(pl.multiple_of(offsets[0], 1024), 1024)])
    for i in range(3):
        copy(downs[1 + i], down.at[:, pl.ds(pl.multiple_of(offsets[1 + i], 256), 256)])
    far = pl.ds(pl.multiple_of(offsets[4], 256), 256)
    copy(downs[4], down.at[0:384, far])
    copy(downs[5], down.at[384:768, far])
    for c in copies[:first]:
        c.wait()

    @pl.loop(0, gate.shape[1] // 256)
    def _(j):
        cols = pl.ds(pl.multiple_of(j * 256, 256), 256)
        g = jnp.dot(x[...], gate[:, cols], preferred_element_type=F32)
        u = jnp.dot(x[...], up[:, cols], preferred_element_type=F32)
        hidden[:, cols] = (g / (1.0 + jnp.exp(-g)) * u).astype(BF)

    for c in copies[first:]:
        c.wait()

    @pl.loop(0, down.shape[1] // 256)
    def _(j):
        cols = pl.ds(pl.multiple_of(j * 256, 256), 256)
        answer = jnp.dot(hidden[...], down[:, cols], preferred_element_type=F32).astype(BF)
        at = 0
        for i, group in enumerate(groups):
            for k in range(4):
                size = len(group) * SLOTS
                outs[4 * i + k][:, cols] = answer[at : at + size]
                at += size


def expert(groups, place, offsets, arrived, gates, ups, downs):
    width, units = arrived.shape[1], gates[0].shape[1]
    shapes = [jax.ShapeDtypeStruct((len(g) * SLOTS, width), BF) for g in groups for _ in range(4)]
    rows = sum(x.shape[0] for x in shapes)
    out = pl.pallas_call(
        functools.partial(expert_kernel, groups),
        out_shape=tuple(shapes),
        in_specs=[SMEM, SMEM] + [ANY] * 19,
        out_specs=(VMEM,) * len(shapes),
        scratch_shapes=[
            pltpu.VMEM((rows, width), BF),
            pltpu.VMEM((rows, units), BF),
            pltpu.VMEM((width, units), BF),
            pltpu.VMEM((width, units), BF),
            pltpu.VMEM((units, width), BF),
            pltpu.SemaphoreType.DMA((18 + rows // SLOTS,)),
        ],
        compiler_params=params(62),
        cost_estimate=cost(6 * rows * width * units, 16 << 20),
    )(place, offsets, arrived, *gates, *ups, *downs)
    return [out[4 * i : 4 * i + 4] for i in range(len(groups))]


def combined(weight, answers):
    rows = jnp.concatenate(list(answers) * 2, axis=0)
    return jnp.dot(weight, rows, preferred_element_type=F32)


def combine_kernel(blocks, n_in, *refs):
    weights, refs = refs[: len(blocks)], refs[len(blocks) :]
    answers, arrived, outs = refs[:4], refs[4 : 4 + n_in], refs[4 + n_in :]
    for i, s in enumerate(blocks):
        rows = slice(i * SLOTS, (i + 1) * SLOTS)
        total = combined(weights[i][...], [a[rows] for a in answers])
        if s == 4:
            outs[0][...] = total[0:64].astype(BF)
            outs[1][...] = total[64:128].astype(BF)
        elif s == 3:
            outs[i][0:64] = (total[0:64] + arrived[i][...].astype(F32)).astype(BF)
            outs[i][64:128] = total[64:128].astype(BF)
        elif s == 5:
            outs[i][0:64] = total[0:64].astype(BF)
            outs[i][64:128] = (total[64:128] + arrived[i][...].astype(F32)).astype(BF)
        else:
            outs[i][...] = (total + arrived[i][...].astype(F32)).astype(BF)


def weight_of(s):
    return pl.BlockSpec((None, 128, 256), lambda *_: (s, 0, 0))


def combine(blocks, weights, answers, arrived):
    width, step = answers[0].shape[1], 1024
    height = 64 if blocks == (4,) else 128
    used = len(blocks) * SLOTS
    return pl.pallas_call(
        functools.partial(combine_kernel, blocks, len(arrived)),
        out_shape=(jax.ShapeDtypeStruct((height, width), BF),) * 2,
        grid=(width // step,),
        in_specs=[weight_of(s) for s in blocks]
        + [pl.BlockSpec((used, step), lambda j: (0, j))] * 4
        + [pl.BlockSpec((x.shape[0], step), lambda j: (0, j)) for x in arrived],
        out_specs=(pl.BlockSpec((height, step), lambda j: (0, j)),) * 2,
        compiler_params=params(8),
        cost_estimate=cost(len(blocks) << 27, 2 << 20),
    )(*[weights] * len(blocks), *answers, *arrived)


def final_kernel(offsets, weight, a0, a1, a2, a3, tokens, left, right, norm, q0, q1, q2, q3, mixed, query, total, normed, held, sems):
    copies = []
    for i, q in enumerate((q0, q1, q2, q3)):
        rows = pl.ds(pl.multiple_of(offsets[2 + i % 2], 768), 768)
        copies.append(pltpu.make_async_copy(q, held.at[i // 2, rows], sems.at[i]))
    for c in copies:
        c.start()
    width, step = tokens.shape[1], 512
    square = jnp.zeros((128, 1), F32)
    for j in range(width // step):
        cols = slice(j * step, (j + 1) * step)
        part = combined(weight[...], [a[:, cols] for a in (a0, a1, a2, a3)])
        part = part + tokens[:, cols].astype(F32)
        part = part + left[:, cols].astype(F32) + right[:, cols].astype(F32)
        mixed[:, cols] = part.astype(BF)
        total[:, cols] = part
        square = square + jnp.sum(part * part, axis=1, keepdims=True)
    scale = lax.rsqrt(square / width + 1e-06)
    for j in range(width // step):
        cols = slice(j * step, (j + 1) * step)
        normed[:, cols] = (total[:, cols] * scale * norm[:, cols]).astype(BF)
    for c in copies:
        c.wait()
    half = width // 2
    sides = [normed[:, pl.ds(pl.multiple_of(offsets[i], half), half)] for i in range(2)]
    dims = (((1,), (1,)), ((), ()))

    @pl.loop(0, query.shape[1] // 256)
    def _(j):
        cols = pl.ds(pl.multiple_of(j * 256, 256), 256)
        out = lax.dot_general(sides[0], held[0, cols], dims, preferred_element_type=F32)
        out = out + lax.dot_general(sides[1], held[1, cols], dims, preferred_element_type=F32)
        query[:, cols] = out.astype(BF)


def final(offsets, weights, answers, tokens, left, right, norm, parts):
    rows, width = tokens.shape
    features = 2 * parts[0].shape[0]

    def whole(x):
        return pl.BlockSpec(x.shape, lambda i: (0, 0))

    return pl.pallas_call(
        final_kernel,
        out_shape=(jax.ShapeDtypeStruct((rows, width), BF), jax.ShapeDtypeStruct((rows, features), BF)),
        grid=(1,),
        in_specs=[SMEM, weight_of(0)] + [whole(x) for x in (*answers, tokens, left, right, norm)] + [ANY] * 4,
        out_specs=(pl.BlockSpec((rows, width), lambda i: (0, 0)), pl.BlockSpec((rows, features), lambda i: (0, 0))),
        scratch_shapes=[
            pltpu.VMEM((rows, width), F32),
            pltpu.VMEM((rows, width), BF),
            pltpu.VMEM((2, features, width // 2), BF),
            pltpu.SemaphoreType.DMA((4,)),
        ],
        compiler_params=params(62),
        cost_estimate=cost(2 * rows * width * features, 8 << 20),
    )(offsets, weights, *answers, tokens, left, right, norm, *parts)


def across_x(x):
    other = swap(x, "xl", 1)
    up, down = shift(other, "y", 1), shift(other, "y", -1)
    half = x.shape[0] // 2
    return [other, up, down, shift(up[:half], "y", 1), shift(down[half:], "y", -1)]


def shards(tokens, routes, route_gain, gate_weight, up_weight, down_weight, norm_gain, query_weight):
    xl, y, z, c = (lax.axis_index(a) for a in ("xl", "y", "z", "c"))
    me = 2 * lax.axis_index("xh") + c
    plane = ("xh", "c")
    across = [1024 * (1 - xl) + 256 * lax.rem(y + d, 4) for d in (0, 3, 1, 2)]
    offsets = jnp.stack([1024 * xl] + across).astype(jnp.int32)
    place = jnp.stack([z, me]).astype(jnp.int32)
    hold = lax.optimization_barrier

    outbound, table = dispatch(routes.T, route_gain.T, tokens)
    tables = lax.all_to_all(table, "z", split_axis=0, concat_axis=0, tiled=True)
    outbound, tables = hold((outbound, tables))
    arrived = lax.all_to_all(outbound, ("z", "xh", "c"), split_axis=0, concat_axis=0, tiled=True)

    gates = [lax.all_gather(gate_weight[0], "y", axis=0, tiled=True)] + across_x(gate_weight[0])
    ups = [lax.all_gather(up_weight[0], "y", axis=0, tiled=True)] + across_x(up_weight[0])
    downs = [lax.all_gather(down_weight[0], "y", axis=1, tiled=True)] + across_x(down_weight[0])
    weights = mixing(place, tables)

    half = query_weight.shape[0] // 2
    share = lax.dynamic_slice(query_weight.T, (0, c * half), (query_weight.shape[1], half))
    q_own = tuple(lax.all_gather(x, "y", axis=0, tiled=True) for x in (share, swap(share, "xl", 1)))

    def exchange(pieces):
        return tuple(swap(pieces[k], plane, k) for k in (1, 2, 3))

    ans4, ans3 = expert(GROUPS[:2], place, offsets, arrived, gates, ups, downs)
    got4, got3 = exchange(ans4), exchange(ans3)
    ans2, ans1, ans0 = expert(GROUPS[2:], place, offsets, arrived, gates, ups, downs)
    got4, got3, ans2, ans1, ans0 = hold((got4, got3, ans2, ans1, ans0))
    low, high = combine((4,), weights, (ans4[0],) + got4, [])
    low, high, got0 = shift(low, "z", -1), shift(high, "z", 1), exchange(ans0)
    low, high, got0, ans2 = hold((low, high, got0, ans2))
    low, high = combine((3, 5), weights, (ans3[0],) + got3, [low, high])
    low, high, got2 = shift(low, "z", -1), shift(high, "z", 1), exchange(ans2)
    low, high, got2, ans1, q_own = hold((low, high, got2, ans1, q_own))
    low, high = combine((2, 6), weights, (ans2[0],) + got2, [low, high])
    q_other = tuple(swap(x, "c", 1) for x in q_own)
    low, high, got1 = shift(low, "z", -1), shift(high, "z", 1), exchange(ans1)
    low, high, got1, q_other = hold((low, high, got1, q_other))
    low, high = combine((1, 7), weights, (ans1[0],) + got1, [low, high])
    low, high = shift(low, "z", -1), shift(high, "z", 1)
    got0 = (ans0[0],) + got0
    sides = jnp.stack([half * c, half * (1 - c), 768 * xl, 768 * (1 - xl)]).astype(jnp.int32)
    return final(sides, weights, got0, tokens, low, high, norm_gain[None, :], q_own + q_other)


def solution(mesh):
    fine = Mesh(mesh.devices.reshape(2, 4, 8, 2, 2), ("xl", "y", "z", "xh", "c"))
    grp, ep = ("xl", "y"), ("z", "xh", "c")
    placed = (
        P(grp + ep, None),
        P(grp + ep, None),
        P(grp + ep, None),
        P(ep, grp, None),
        P(ep, grp, None),
        P(ep, None, grp),
        P(),
        P(None, grp),
    )
    return jax.shard_map(
        shards,
        mesh=fine,
        in_specs=placed,
        out_specs=(P(grp + ep, None), P(grp + ep, None)),
        check_vma=False,
    )
```

```python
import functools

import jax
import jax.numpy as jnp
from jax import lax
from jax.experimental import pallas as pl
from jax.experimental.pallas import tpu as pltpu
from jax.sharding import Mesh, PartitionSpec as P

BF = jnp.bfloat16
F32 = jnp.float32
SLOTS = 32
ANY = pl.BlockSpec(memory_space=pltpu.HBM)
SMEM = pl.BlockSpec(memory_space=pltpu.SMEM)
VMEM = pl.BlockSpec(memory_space=pltpu.VMEM)
GROUPS = ((4,), (3, 5), (2, 6), (1, 7), (0,))


def params(mib):
    return pltpu.CompilerParams(vmem_limit_bytes=mib << 20)


def cost(flops, size):
    return pl.CostEstimate(flops=flops, bytes_accessed=size, transcendentals=0)


def shift(x, axis, by):
    n = lax.axis_size(axis)
    return lax.ppermute(x, axis, [(i, (i + by) % n) for i in range(n)])


def swap(x, axes, k):
    n = lax.axis_size(axes)
    return lax.ppermute(x, axes, [(i, i ^ k) for i in range(n)])


def dispatch_kernel(routes, gains, tokens, out, table, onehot):
    experts, rows = 32, tokens.shape[0]

    @pl.when(pl.program_id(0) == 0)
    def _():
        expert = lax.broadcasted_iota(jnp.int32, (experts, rows), 0)
        match = jnp.zeros((experts, rows), F32)
        gain = jnp.zeros((experts, rows), F32)
        for j in range(6):
            hit = routes[j : j + 1, :] == expert
            match = match + jnp.where(hit, 1.0, 0.0)
            gain = gain + jnp.where(hit, gains[j : j + 1, :], 0.0)
        before = lax.broadcasted_iota(jnp.int32, (rows, rows), 0) < lax.broadcasted_iota(jnp.int32, (rows, rows), 1)
        rank = jnp.dot(match.astype(BF), jnp.where(before, 1.0, 0.0).astype(BF), preferred_element_type=F32)
        code = jnp.where(match > 0.5, rank, -1.0)
        for d in range(experts // 4):
            own = slice(4 * d, 4 * d + 4)
            table[8 * d : 8 * d + 4] = code[own]
            table[8 * d + 4 : 8 * d + 8] = gain[own]
        slot = lax.broadcasted_iota(jnp.int32, (SLOTS, rows), 0).astype(F32)
        for e in range(experts):
            onehot[e * SLOTS : (e + 1) * SLOTS] = jnp.where(code[e : e + 1, :] == slot, 1.0, 0.0).astype(BF)

    @pl.loop(0, 4)
    def _(i):
        part = pl.ds(pl.multiple_of(i * 256, 256), 256)
        out[part] = jnp.dot(onehot[part], tokens[...], preferred_element_type=F32).astype(BF)


def dispatch(routes, gains, tokens):
    rows, width = tokens.shape
    step = 512
    return pl.pallas_call(
        dispatch_kernel,
        out_shape=(jax.ShapeDtypeStruct((32 * SLOTS, width), BF), jax.ShapeDtypeStruct((64, rows), F32)),
        grid=(width // step,),
        in_specs=[
            pl.BlockSpec((6, rows), lambda j: (0, 0)),
            pl.BlockSpec((6, rows), lambda j: (0, 0)),
            pl.BlockSpec((rows, step), lambda j: (0, j)),
        ],
        out_specs=(pl.BlockSpec((32 * SLOTS, step), lambda j: (0, j)), pl.BlockSpec((64, rows), lambda j: (0, 0))),
        scratch_shapes=[pltpu.VMEM((32 * SLOTS, rows), BF)],
        compiler_params=params(62),
        cost_estimate=cost(1 << 29, 5 << 20),
    )(routes, gains, tokens)


def mixing_kernel(place, table, out):
    slot = lax.broadcasted_iota(jnp.int32, (SLOTS, 128), 0).astype(F32)
    for s in range(8):
        source = lax.rem(place[0] + 8 - s, 8)
        parts = []
        for k in range(4):
            row = 8 * source + lax.bitwise_xor(place[1], k)
            code, gain = table[pl.ds(row, 1), :], table[pl.ds(row + 4, 1), :]
            parts.append(jnp.where(code == slot, gain, 0.0))
        weight = jnp.concatenate(parts, axis=0).T
        high = weight.astype(BF)
        out[s, :, 0:128] = high
        out[s, :, 128:256] = (weight - high.astype(F32)).astype(BF)


def mixing(place, table):
    return pl.pallas_call(
        mixing_kernel,
        out_shape=jax.ShapeDtypeStruct((8, 128, 256), BF),
        in_specs=[SMEM, VMEM],
        out_specs=VMEM,
        compiler_params=params(8),
        cost_estimate=cost(1 << 22, 1 << 20),
    )(place, table)


def expert_kernel(groups, place, offsets, *refs):
    arrived, gates, ups, downs = refs[0], refs[1:7], refs[7:13], refs[13:19]
    outs, (x, hidden, gate, up, down, sems) = refs[19:-6], refs[-6:]
    copies = []

    def copy(src, dst):
        c = pltpu.make_async_copy(src, dst, sems.at[len(copies)])
        c.start()
        copies.append(c)

    for parts, whole in ((gates, gate), (ups, up)):
        copy(parts[0], whole.at[pl.ds(pl.multiple_of(offsets[0], 1024), 1024)])
        for i in range(3):
            copy(parts[1 + i], whole.at[pl.ds(pl.multiple_of(offsets[1 + i], 256), 256)])
        far = pl.multiple_of(offsets[4], 256)
        copy(parts[4], whole.at[pl.ds(far, 128)])
        copy(parts[5], whole.at[pl.ds(pl.multiple_of(far + 128, 128), 128)])
    at = 0
    for group in groups:
        for k in range(4):
            for s in group:
                source = 4 * lax.rem(place[0] + 8 - s, 8) + lax.bitwise_xor(place[1], k)
                copy(arrived.at[pl.ds(pl.multiple_of(source * SLOTS, SLOTS), SLOTS)], x.at[at : at + SLOTS])
                at += SLOTS
    first = len(copies)
    copy(downs[0], down.at[:, pl.ds(pl.multiple_of(offsets[0], 1024), 1024)])
    for i in range(3):
        copy(downs[1 + i], down.at[:, pl.ds(pl.multiple_of(offsets[1 + i], 256), 256)])
    far = pl.ds(pl.multiple_of(offsets[4], 256), 256)
    copy(downs[4], down.at[0:384, far])
    copy(downs[5], down.at[384:768, far])
    for c in copies[:first]:
        c.wait()

    @pl.loop(0, gate.shape[1] // 256)
    def _(j):
        cols = pl.ds(pl.multiple_of(j * 256, 256), 256)
        g = jnp.dot(x[...], gate[:, cols], preferred_element_type=F32)
        u = jnp.dot(x[...], up[:, cols], preferred_element_type=F32)
        hidden[:, cols] = (g / (1.0 + jnp.exp(-g)) * u).astype(BF)

    for c in copies[first:]:
        c.wait()

    @pl.loop(0, down.shape[1] // 256)
    def _(j):
        cols = pl.ds(pl.multiple_of(j * 256, 256), 256)
        answer = jnp.dot(hidden[...], down[:, cols], preferred_element_type=F32).astype(BF)
        at = 0
        for i, group in enumerate(groups):
            for k in range(4):
                size = len(group) * SLOTS
                outs[4 * i + k][:, cols] = answer[at : at + size]
                at += size


def expert(groups, place, offsets, arrived, gates, ups, downs):
    width, units = arrived.shape[1], gates[0].shape[1]
    shapes = [jax.ShapeDtypeStruct((len(g) * SLOTS, width), BF) for g in groups for _ in range(4)]
    rows = sum(x.shape[0] for x in shapes)
    out = pl.pallas_call(
        functools.partial(expert_kernel, groups),
        out_shape=tuple(shapes),
        in_specs=[SMEM, SMEM] + [ANY] * 19,
        out_specs=(VMEM,) * len(shapes),
        scratch_shapes=[
            pltpu.VMEM((rows, width), BF),
            pltpu.VMEM((rows, units), BF),
            pltpu.VMEM((width, units), BF),
            pltpu.VMEM((width, units), BF),
            pltpu.VMEM((units, width), BF),
            pltpu.SemaphoreType.DMA((18 + rows // SLOTS,)),
        ],
        compiler_params=params(62),
        cost_estimate=cost(6 * rows * width * units, 16 << 20),
    )(place, offsets, arrived, *gates, *ups, *downs)
    return [out[4 * i : 4 * i + 4] for i in range(len(groups))]


def combined(weight, answers):
    rows = jnp.concatenate(list(answers) * 2, axis=0)
    return jnp.dot(weight, rows, preferred_element_type=F32)


def combine_kernel(blocks, n_in, *refs):
    weights, refs = refs[: len(blocks)], refs[len(blocks) :]
    answers, arrived, outs = refs[:4], refs[4 : 4 + n_in], refs[4 + n_in :]
    for i, s in enumerate(blocks):
        rows = slice(i * SLOTS, (i + 1) * SLOTS)
        total = combined(weights[i][...], [a[rows] for a in answers])
        if s == 4:
            outs[0][...] = total[0:64].astype(BF)
            outs[1][...] = total[64:128].astype(BF)
        elif s == 3:
            outs[i][0:64] = (total[0:64] + arrived[i][...].astype(F32)).astype(BF)
            outs[i][64:128] = total[64:128].astype(BF)
        elif s == 5:
            outs[i][0:64] = total[0:64].astype(BF)
            outs[i][64:128] = (total[64:128] + arrived[i][...].astype(F32)).astype(BF)
        else:
            outs[i][...] = (total + arrived[i][...].astype(F32)).astype(BF)


def weight_of(s):
    return pl.BlockSpec((None, 128, 256), lambda *_: (s, 0, 0))


def combine(blocks, weights, answers, arrived):
    width, step = answers[0].shape[1], 1024
    height = 64 if blocks == (4,) else 128
    used = len(blocks) * SLOTS
    return pl.pallas_call(
        functools.partial(combine_kernel, blocks, len(arrived)),
        out_shape=(jax.ShapeDtypeStruct((height, width), BF),) * 2,
        grid=(width // step,),
        in_specs=[weight_of(s) for s in blocks]
        + [pl.BlockSpec((used, step), lambda j: (0, j))] * 4
        + [pl.BlockSpec((x.shape[0], step), lambda j: (0, j)) for x in arrived],
        out_specs=(pl.BlockSpec((height, step), lambda j: (0, j)),) * 2,
        compiler_params=params(8),
        cost_estimate=cost(len(blocks) << 27, 2 << 20),
    )(*[weights] * len(blocks), *answers, *arrived)


def final_kernel(offsets, weight, a0, a1, a2, a3, tokens, left, right, norm, q0, q1, q2, q3, mixed, query, total, normed, held, sems):
    copies = []
    for i, q in enumerate((q0, q1, q2, q3)):
        rows = pl.ds(pl.multiple_of(offsets[2 + i % 2], 768), 768)
        copies.append(pltpu.make_async_copy(q, held.at[i // 2, rows], sems.at[i]))
    for c in copies:
        c.start()
    width, step = tokens.shape[1], 512
    square = jnp.zeros((128, 1), F32)
    for j in range(width // step):
        cols = slice(j * step, (j + 1) * step)
        part = combined(weight[...], [a[:, cols] for a in (a0, a1, a2, a3)])
        part = part + tokens[:, cols].astype(F32)
        part = part + left[:, cols].astype(F32) + right[:, cols].astype(F32)
        mixed[:, cols] = part.astype(BF)
        total[:, cols] = part
        square = square + jnp.sum(part * part, axis=1, keepdims=True)
    scale = lax.rsqrt(square / width + 1e-06)
    for j in range(width // step):
        cols = slice(j * step, (j + 1) * step)
        normed[:, cols] = (total[:, cols] * scale * norm[:, cols]).astype(BF)
    for c in copies:
        c.wait()
    half = width // 2
    sides = [normed[:, pl.ds(pl.multiple_of(offsets[i], half), half)] for i in range(2)]
    dims = (((1,), (1,)), ((), ()))

    @pl.loop(0, query.shape[1] // 256)
    def _(j):
        cols = pl.ds(pl.multiple_of(j * 256, 256), 256)
        out = lax.dot_general(sides[0], held[0, cols], dims, preferred_element_type=F32)
        out = out + lax.dot_general(sides[1], held[1, cols], dims, preferred_element_type=F32)
        query[:, cols] = out.astype(BF)


def final(offsets, weights, answers, tokens, left, right, norm, parts):
    rows, width = tokens.shape
    features = 2 * parts[0].shape[0]

    def whole(x):
        return pl.BlockSpec(x.shape, lambda i: (0, 0))

    return pl.pallas_call(
        final_kernel,
        out_shape=(jax.ShapeDtypeStruct((rows, width), BF), jax.ShapeDtypeStruct((rows, features), BF)),
        grid=(1,),
        in_specs=[SMEM, weight_of(0)] + [whole(x) for x in (*answers, tokens, left, right, norm)] + [ANY] * 4,
        out_specs=(pl.BlockSpec((rows, width), lambda i: (0, 0)), pl.BlockSpec((rows, features), lambda i: (0, 0))),
        scratch_shapes=[
            pltpu.VMEM((rows, width), F32),
            pltpu.VMEM((rows, width), BF),
            pltpu.VMEM((2, features, width // 2), BF),
            pltpu.SemaphoreType.DMA((4,)),
        ],
        compiler_params=params(62),
        cost_estimate=cost(2 * rows * width * features, 8 << 20),
    )(offsets, weights, *answers, tokens, left, right, norm, *parts)


def across_x(x):
    other = swap(x, "xl", 1)
    up, down = shift(other, "y", 1), shift(other, "y", -1)
    half = x.shape[0] // 2
    return [other, up, down, shift(up[:half], "y", 1), shift(down[half:], "y", -1)]


def shards(tokens, routes, route_gain, gate_weight, up_weight, down_weight, norm_gain, query_weight):
    xl, y, z, c = (lax.axis_index(a) for a in ("xl", "y", "z", "c"))
    me = 2 * lax.axis_index("xh") + c
    plane = ("xh", "c")
    across = [1024 * (1 - xl) + 256 * lax.rem(y + d, 4) for d in (0, 3, 1, 2)]
    offsets = jnp.stack([1024 * xl] + across).astype(jnp.int32)
    place = jnp.stack([z, me]).astype(jnp.int32)
    hold = lax.optimization_barrier

    outbound, table = dispatch(routes.T, route_gain.T, tokens)
    tables = lax.all_to_all(table, "z", split_axis=0, concat_axis=0, tiled=True)
    outbound, tables = hold((outbound, tables))
    arrived = lax.all_to_all(outbound, ("z", "xh", "c"), split_axis=0, concat_axis=0, tiled=True)

    gates = [lax.all_gather(gate_weight[0], "y", axis=0, tiled=True)] + across_x(gate_weight[0])
    ups = [lax.all_gather(up_weight[0], "y", axis=0, tiled=True)] + across_x(up_weight[0])
    downs = [lax.all_gather(down_weight[0], "y", axis=1, tiled=True)] + across_x(down_weight[0])
    weights = mixing(place, tables)

    half = query_weight.shape[0] // 2
    share = lax.dynamic_slice(query_weight.T, (0, c * half), (query_weight.shape[1], half))
    def exchange(pieces):
        return tuple(swap(pieces[k], plane, k) for k in (1, 2, 3))

    ans4, ans3 = expert(GROUPS[:2], place, offsets, arrived, gates, ups, downs)
    across, _ = hold((swap(share, "xl", 1), ans4[0]))
    q_own = tuple(lax.all_gather(x, "y", axis=0, tiled=True) for x in (share, across))
    got4, got3 = exchange(ans4), exchange(ans3)
    ans2, ans1, ans0 = expert(GROUPS[2:], place, offsets, arrived, gates, ups, downs)
    got4, got3, ans2, ans1, ans0 = hold((got4, got3, ans2, ans1, ans0))
    low, high = combine((4,), weights, (ans4[0],) + got4, [])
    low, high, got0 = shift(low, "z", -1), shift(high, "z", 1), exchange(ans0)
    low, high, got0, ans2 = hold((low, high, got0, ans2))
    low, high = combine((3, 5), weights, (ans3[0],) + got3, [low, high])
    low, high, got2 = shift(low, "z", -1), shift(high, "z", 1), exchange(ans2)
    low, high, got2, ans1, q_own = hold((low, high, got2, ans1, q_own))
    low, high = combine((2, 6), weights, (ans2[0],) + got2, [low, high])
    q_other = tuple(swap(x, "c", 1) for x in q_own)
    low, high, got1 = shift(low, "z", -1), shift(high, "z", 1), exchange(ans1)
    low, high, got1, q_other = hold((low, high, got1, q_other))
    low, high = combine((1, 7), weights, (ans1[0],) + got1, [low, high])
    low, high = shift(low, "z", -1), shift(high, "z", 1)
    got0 = (ans0[0],) + got0
    sides = jnp.stack([half * c, half * (1 - c), 768 * xl, 768 * (1 - xl)]).astype(jnp.int32)
    return final(sides, weights, got0, tokens, low, high, norm_gain[None, :], q_own + q_other)


def solution(mesh):
    fine = Mesh(mesh.devices.reshape(2, 4, 8, 2, 2), ("xl", "y", "z", "xh", "c"))
    grp, ep = ("xl", "y"), ("z", "xh", "c")
    placed = (
        P(grp + ep, None),
        P(grp + ep, None),
        P(grp + ep, None),
        P(ep, grp, None),
        P(ep, grp, None),
        P(ep, None, grp),
        P(),
        P(None, grp),
    )
    return jax.shard_map(
        shards,
        mesh=fine,
        in_specs=placed,
        out_specs=(P(grp + ep, None), P(grp + ep, None)),
        check_vma=False,
    )
```

```python
import functools

import jax
import jax.numpy as jnp
from jax import lax
from jax.experimental import pallas as pl
from jax.experimental.pallas import tpu as pltpu
from jax.sharding import Mesh, PartitionSpec as P

BF = jnp.bfloat16
F32 = jnp.float32
SLOTS = 32
ANY = pl.BlockSpec(memory_space=pltpu.HBM)
SMEM = pl.BlockSpec(memory_space=pltpu.SMEM)
VMEM = pl.BlockSpec(memory_space=pltpu.VMEM)
GROUPS = ((4,), (3, 5), (2, 6), (1, 7), (0,))


def params(mib):
    return pltpu.CompilerParams(vmem_limit_bytes=mib << 20)


def cost(flops, size):
    return pl.CostEstimate(flops=flops, bytes_accessed=size, transcendentals=0)


def shift(x, axis, by):
    n = lax.axis_size(axis)
    return lax.ppermute(x, axis, [(i, (i + by) % n) for i in range(n)])


def swap(x, axes, k):
    n = lax.axis_size(axes)
    return lax.ppermute(x, axes, [(i, i ^ k) for i in range(n)])


def dispatch_kernel(routes, gains, tokens, out, table, onehot):
    experts, rows = 32, tokens.shape[0]

    @pl.when(pl.program_id(0) == 0)
    def _():
        expert = lax.broadcasted_iota(jnp.int32, (experts, rows), 0)
        match = jnp.zeros((experts, rows), F32)
        gain = jnp.zeros((experts, rows), F32)
        for j in range(6):
            hit = routes[j : j + 1, :] == expert
            match = match + jnp.where(hit, 1.0, 0.0)
            gain = gain + jnp.where(hit, gains[j : j + 1, :], 0.0)
        before = lax.broadcasted_iota(jnp.int32, (rows, rows), 0) < lax.broadcasted_iota(jnp.int32, (rows, rows), 1)
        rank = jnp.dot(match.astype(BF), jnp.where(before, 1.0, 0.0).astype(BF), preferred_element_type=F32)
        code = jnp.where(match > 0.5, rank, -1.0)
        for d in range(experts // 4):
            own = slice(4 * d, 4 * d + 4)
            table[8 * d : 8 * d + 4] = code[own]
            table[8 * d + 4 : 8 * d + 8] = gain[own]
        slot = lax.broadcasted_iota(jnp.int32, (SLOTS, rows), 0).astype(F32)
        for e in range(experts):
            onehot[e * SLOTS : (e + 1) * SLOTS] = jnp.where(code[e : e + 1, :] == slot, 1.0, 0.0).astype(BF)

    @pl.loop(0, 4)
    def _(i):
        part = pl.ds(pl.multiple_of(i * 256, 256), 256)
        out[part] = jnp.dot(onehot[part], tokens[...], preferred_element_type=F32).astype(BF)


def dispatch(routes, gains, tokens):
    rows, width = tokens.shape
    step = 512
    return pl.pallas_call(
        dispatch_kernel,
        out_shape=(jax.ShapeDtypeStruct((32 * SLOTS, width), BF), jax.ShapeDtypeStruct((64, rows), F32)),
        grid=(width // step,),
        in_specs=[
            pl.BlockSpec((6, rows), lambda j: (0, 0)),
            pl.BlockSpec((6, rows), lambda j: (0, 0)),
            pl.BlockSpec((rows, step), lambda j: (0, j)),
        ],
        out_specs=(pl.BlockSpec((32 * SLOTS, step), lambda j: (0, j)), pl.BlockSpec((64, rows), lambda j: (0, 0))),
        scratch_shapes=[pltpu.VMEM((32 * SLOTS, rows), BF)],
        compiler_params=params(62),
        cost_estimate=cost(1 << 29, 5 << 20),
    )(routes, gains, tokens)


def mixing_kernel(place, table, out):
    slot = lax.broadcasted_iota(jnp.int32, (SLOTS, 128), 0).astype(F32)
    for s in range(8):
        source = lax.rem(place[0] + 8 - s, 8)
        parts = []
        for k in range(4):
            row = 8 * source + lax.bitwise_xor(place[1], k)
            code, gain = table[pl.ds(row, 1), :], table[pl.ds(row + 4, 1), :]
            parts.append(jnp.where(code == slot, gain, 0.0))
        weight = jnp.concatenate(parts, axis=0).T
        high = weight.astype(BF)
        out[s, :, 0:128] = high
        out[s, :, 128:256] = (weight - high.astype(F32)).astype(BF)


def mixing(place, table):
    return pl.pallas_call(
        mixing_kernel,
        out_shape=jax.ShapeDtypeStruct((8, 128, 256), BF),
        in_specs=[SMEM, VMEM],
        out_specs=VMEM,
        compiler_params=params(8),
        cost_estimate=cost(1 << 22, 1 << 20),
    )(place, table)


def expert_kernel(groups, place, offsets, *refs):
    arrived, gates, ups, downs = refs[0], refs[1:7], refs[7:13], refs[13:19]
    outs, (x, hidden, gate, up, down, sems) = refs[19:-6], refs[-6:]
    copies = []

    def copy(src, dst):
        c = pltpu.make_async_copy(src, dst, sems.at[len(copies)])
        c.start()
        copies.append(c)

    for parts, whole in ((gates, gate), (ups, up)):
        copy(parts[0], whole.at[pl.ds(pl.multiple_of(offsets[0], 1024), 1024)])
        for i in range(3):
            copy(parts[1 + i], whole.at[pl.ds(pl.multiple_of(offsets[1 + i], 256), 256)])
        far = pl.multiple_of(offsets[4], 256)
        copy(parts[4], whole.at[pl.ds(far, 128)])
        copy(parts[5], whole.at[pl.ds(pl.multiple_of(far + 128, 128), 128)])
    at = 0
    for group in groups:
        for k in range(4):
            for s in group:
                source = 4 * lax.rem(place[0] + 8 - s, 8) + lax.bitwise_xor(place[1], k)
                copy(arrived.at[pl.ds(pl.multiple_of(source * SLOTS, SLOTS), SLOTS)], x.at[at : at + SLOTS])
                at += SLOTS
    first = len(copies)
    copy(downs[0], down.at[:, pl.ds(pl.multiple_of(offsets[0], 1024), 1024)])
    for i in range(3):
        copy(downs[1 + i], down.at[:, pl.ds(pl.multiple_of(offsets[1 + i], 256), 256)])
    far = pl.ds(pl.multiple_of(offsets[4], 256), 256)
    copy(downs[4], down.at[0:384, far])
    copy(downs[5], down.at[384:768, far])
    for c in copies[:first]:
        c.wait()

    @pl.loop(0, gate.shape[1] // 256)
    def _(j):
        cols = pl.ds(pl.multiple_of(j * 256, 256), 256)
        g = jnp.dot(x[...], gate[:, cols], preferred_element_type=F32)
        u = jnp.dot(x[...], up[:, cols], preferred_element_type=F32)
        hidden[:, cols] = (g / (1.0 + jnp.exp(-g)) * u).astype(BF)

    for c in copies[first:]:
        c.wait()

    @pl.loop(0, down.shape[1] // 256)
    def _(j):
        cols = pl.ds(pl.multiple_of(j * 256, 256), 256)
        answer = jnp.dot(hidden[...], down[:, cols], preferred_element_type=F32).astype(BF)
        at = 0
        for i, group in enumerate(groups):
            for k in range(4):
                size = len(group) * SLOTS
                outs[4 * i + k][:, cols] = answer[at : at + size]
                at += size


def expert(groups, place, offsets, arrived, gates, ups, downs):
    width, units = arrived.shape[1], gates[0].shape[1]
    shapes = [jax.ShapeDtypeStruct((len(g) * SLOTS, width), BF) for g in groups for _ in range(4)]
    rows = sum(x.shape[0] for x in shapes)
    out = pl.pallas_call(
        functools.partial(expert_kernel, groups),
        out_shape=tuple(shapes),
        in_specs=[SMEM, SMEM] + [ANY] * 19,
        out_specs=(VMEM,) * len(shapes),
        scratch_shapes=[
            pltpu.VMEM((rows, width), BF),
            pltpu.VMEM((rows, units), BF),
            pltpu.VMEM((width, units), BF),
            pltpu.VMEM((width, units), BF),
            pltpu.VMEM((units, width), BF),
            pltpu.SemaphoreType.DMA((18 + rows // SLOTS,)),
        ],
        compiler_params=params(62),
        cost_estimate=cost(6 * rows * width * units, 16 << 20),
    )(place, offsets, arrived, *gates, *ups, *downs)
    return [out[4 * i : 4 * i + 4] for i in range(len(groups))]


def combined(weight, answers):
    rows = jnp.concatenate(list(answers) * 2, axis=0)
    return jnp.dot(weight, rows, preferred_element_type=F32)


def combine_kernel(blocks, n_in, *refs):
    weights, refs = refs[: len(blocks)], refs[len(blocks) :]
    answers, arrived, outs = refs[:4], refs[4 : 4 + n_in], refs[4 + n_in :]
    for i, s in enumerate(blocks):
        rows = slice(i * SLOTS, (i + 1) * SLOTS)
        total = combined(weights[i][...], [a[rows] for a in answers])
        if s == 4:
            outs[0][...] = total[0:64].astype(BF)
            outs[1][...] = total[64:128].astype(BF)
        elif s == 3:
            outs[i][0:64] = (total[0:64] + arrived[i][...].astype(F32)).astype(BF)
            outs[i][64:128] = total[64:128].astype(BF)
        elif s == 5:
            outs[i][0:64] = total[0:64].astype(BF)
            outs[i][64:128] = (total[64:128] + arrived[i][...].astype(F32)).astype(BF)
        else:
            outs[i][...] = (total + arrived[i][...].astype(F32)).astype(BF)


def weight_of(s):
    return pl.BlockSpec((None, 128, 256), lambda *_: (s, 0, 0))


def combine(blocks, weights, answers, arrived):
    width, step = answers[0].shape[1], 1024
    height = 64 if blocks == (4,) else 128
    used = len(blocks) * SLOTS
    return pl.pallas_call(
        functools.partial(combine_kernel, blocks, len(arrived)),
        out_shape=(jax.ShapeDtypeStruct((height, width), BF),) * 2,
        grid=(width // step,),
        in_specs=[weight_of(s) for s in blocks]
        + [pl.BlockSpec((used, step), lambda j: (0, j))] * 4
        + [pl.BlockSpec((x.shape[0], step), lambda j: (0, j)) for x in arrived],
        out_specs=(pl.BlockSpec((height, step), lambda j: (0, j)),) * 2,
        compiler_params=params(8),
        cost_estimate=cost(len(blocks) << 27, 2 << 20),
    )(*[weights] * len(blocks), *answers, *arrived)


def final_kernel(offsets, weight, a0, a1, a2, a3, tokens, left, right, norm, q0, q1, q2, q3, mixed, query, total, normed, held, sems):
    copies = []
    for i, q in enumerate((q0, q1, q2, q3)):
        rows = pl.ds(pl.multiple_of(offsets[2 + i % 2], 768), 768)
        copies.append(pltpu.make_async_copy(q, held.at[i // 2, rows], sems.at[i]))
    for c in copies:
        c.start()
    width, step = tokens.shape[1], 512
    square = jnp.zeros((128, 1), F32)
    for j in range(width // step):
        cols = slice(j * step, (j + 1) * step)
        part = combined(weight[...], [a[:, cols] for a in (a0, a1, a2, a3)])
        part = part + tokens[:, cols].astype(F32)
        part = part + left[:, cols].astype(F32) + right[:, cols].astype(F32)
        mixed[:, cols] = part.astype(BF)
        total[:, cols] = part
        square = square + jnp.sum(part * part, axis=1, keepdims=True)
    scale = lax.rsqrt(square / width + 1e-06)
    for j in range(width // step):
        cols = slice(j * step, (j + 1) * step)
        normed[:, cols] = (total[:, cols] * scale * norm[:, cols]).astype(BF)
    for c in copies:
        c.wait()
    half = width // 2
    sides = [normed[:, pl.ds(pl.multiple_of(offsets[i], half), half)] for i in range(2)]
    dims = (((1,), (1,)), ((), ()))

    @pl.loop(0, query.shape[1] // 256)
    def _(j):
        cols = pl.ds(pl.multiple_of(j * 256, 256), 256)
        out = lax.dot_general(sides[0], held[0, cols], dims, preferred_element_type=F32)
        out = out + lax.dot_general(sides[1], held[1, cols], dims, preferred_element_type=F32)
        query[:, cols] = out.astype(BF)


def final(offsets, weights, answers, tokens, left, right, norm, parts):
    rows, width = tokens.shape
    features = 2 * parts[0].shape[0]

    def whole(x):
        return pl.BlockSpec(x.shape, lambda i: (0, 0))

    return pl.pallas_call(
        final_kernel,
        out_shape=(jax.ShapeDtypeStruct((rows, width), BF), jax.ShapeDtypeStruct((rows, features), BF)),
        grid=(1,),
        in_specs=[SMEM, weight_of(0)] + [whole(x) for x in (*answers, tokens, left, right, norm)] + [ANY] * 4,
        out_specs=(pl.BlockSpec((rows, width), lambda i: (0, 0)), pl.BlockSpec((rows, features), lambda i: (0, 0))),
        scratch_shapes=[
            pltpu.VMEM((rows, width), F32),
            pltpu.VMEM((rows, width), BF),
            pltpu.VMEM((2, features, width // 2), BF),
            pltpu.SemaphoreType.DMA((4,)),
        ],
        compiler_params=params(62),
        cost_estimate=cost(2 * rows * width * features, 8 << 20),
    )(offsets, weights, *answers, tokens, left, right, norm, *parts)


def across_x(x):
    other = swap(x, "xl", 1)
    up, down = shift(other, "y", 1), shift(other, "y", -1)
    half = x.shape[0] // 2
    return [other, up, down, shift(up[:half], "y", 1), shift(down[half:], "y", -1)]


def shards(tokens, routes, route_gain, gate_weight, up_weight, down_weight, norm_gain, query_weight):
    xl, y, z, c = (lax.axis_index(a) for a in ("xl", "y", "z", "c"))
    me = 2 * lax.axis_index("xh") + c
    plane = ("xh", "c")
    across = [1024 * (1 - xl) + 256 * lax.rem(y + d, 4) for d in (0, 3, 1, 2)]
    offsets = jnp.stack([1024 * xl] + across).astype(jnp.int32)
    place = jnp.stack([z, me]).astype(jnp.int32)
    hold = lax.optimization_barrier

    outbound, table = dispatch(routes.T, route_gain.T, tokens)
    tables = lax.all_to_all(table, "z", split_axis=0, concat_axis=0, tiled=True)
    outbound, tables = hold((outbound, tables))
    arrived = lax.all_to_all(outbound, ("z", "xh", "c"), split_axis=0, concat_axis=0, tiled=True)

    gates = [lax.all_gather(gate_weight[0], "y", axis=0, tiled=True)] + across_x(gate_weight[0])
    ups = [lax.all_gather(up_weight[0], "y", axis=0, tiled=True)] + across_x(up_weight[0])
    downs = [lax.all_gather(down_weight[0], "y", axis=1, tiled=True)] + across_x(down_weight[0])
    weights = mixing(place, tables)

    half = query_weight.shape[0] // 2
    share = lax.dynamic_slice(query_weight.T, (0, c * half), (query_weight.shape[1], half))
    def exchange(pieces):
        return tuple(swap(pieces[k], plane, k) for k in (1, 2, 3))

    ans4, ans3 = expert(GROUPS[:2], place, offsets, arrived, gates, ups, downs)
    across, _ = hold((swap(share, "xl", 1), ans4[0]))
    q_own = tuple(lax.all_gather(x, "y", axis=0, tiled=True) for x in (share, across))
    got4, got3 = exchange(ans4), exchange(ans3)
    ans2, ans1, ans0 = expert(GROUPS[2:], place, offsets, arrived, gates, ups, downs)
    got4, got3, ans2, ans1, ans0 = hold((got4, got3, ans2, ans1, ans0))
    low, high = combine((4,), weights, (ans4[0],) + got4, [])
    low, high, got2 = shift(low, "z", -1), shift(high, "z", 1), exchange(ans2)
    low, high, got2, ans1 = hold((low, high, got2, ans1))
    low, high = combine((3, 5), weights, (ans3[0],) + got3, [low, high])
    low, high, got1 = shift(low, "z", -1), shift(high, "z", 1), exchange(ans1)
    low, high, got1, ans0, q_own = hold((low, high, got1, ans0, q_own))
    low, high = combine((2, 6), weights, (ans2[0],) + got2, [low, high])
    q_other = tuple(swap(x, "c", 1) for x in q_own)
    low, high, got0 = shift(low, "z", -1), shift(high, "z", 1), exchange(ans0)
    low, high, got0, q_other = hold((low, high, got0, q_other))
    low, high = combine((1, 7), weights, (ans1[0],) + got1, [low, high])
    low, high = shift(low, "z", -1), shift(high, "z", 1)
    got0 = (ans0[0],) + got0
    sides = jnp.stack([half * c, half * (1 - c), 768 * xl, 768 * (1 - xl)]).astype(jnp.int32)
    return final(sides, weights, got0, tokens, low, high, norm_gain[None, :], q_own + q_other)


def solution(mesh):
    fine = Mesh(mesh.devices.reshape(2, 4, 8, 2, 2), ("xl", "y", "z", "xh", "c"))
    grp, ep = ("xl", "y"), ("z", "xh", "c")
    placed = (
        P(grp + ep, None),
        P(grp + ep, None),
        P(grp + ep, None),
        P(ep, grp, None),
        P(ep, grp, None),
        P(ep, None, grp),
        P(),
        P(None, grp),
    )
    return jax.shard_map(
        shards,
        mesh=fine,
        in_specs=placed,
        out_specs=(P(grp + ep, None), P(grp + ep, None)),
        check_vma=False,
    )
```
